32 devices in a mesh: shard: 4 (over z), ctx: 2 (over y), tp: 4 (over x, core).
Axes of the slice: x: 2, y: 2, z: 4, core: 2. Of those that a mesh axis runs over, the one named last changes fastest.
Arguments:
- inputs: bfloat16 [16, 1024, 512], P('shard', 'ctx'), may hold values from -6 to 6
- first_memory: float32 [16, 64, 512], P('shard'), may hold values from -6 to 6
- piece_start: int32 [16, 2], P('shard', 'ctx'), may hold values from 0 to 448, as said below
- piece_len: int32 [16, 2], P('shard', 'ctx'), may hold values from 64 to 256, as said below
- w_query: bfloat16 [512, 512], P(('shard', 'tp')), may hold values from -0.25 to 0.25
- w_key: bfloat16 [512, 512], P(('shard', 'tp')), may hold values from -0.25 to 0.25
- w_value: bfloat16 [512, 512], P(('shard', 'tp')), may hold values from -0.25 to 0.25
- w_out: bfloat16 [512, 512], P(('shard', 'tp')), may hold values from -1 to 1
- w_up: bfloat16 [512, 2048], P(('shard', 'tp')), may hold values from -0.25 to 0.25
- w_down: bfloat16 [2048, 512], P(('shard', 'tp')), may hold values from -0.125 to 0.125
- u_query: bfloat16 [512, 512], P(('shard', 'tp')), may hold values from -0.25 to 0.25
- u_key: bfloat16 [512, 512], P(('shard', 'tp')), may hold values from -0.25 to 0.25
- u_value: bfloat16 [512, 512], P(('shard', 'tp')), may hold values from -0.25 to 0.25
- u_out: bfloat16 [512, 512], P(('shard', 'tp')), may hold values from -1 to 1
- u_gate: bfloat16 [512, 512], P(('shard', 'tp')), may hold values from -0.25 to 0.25
- gain_attn: float32 [512], replicated, may hold values from 0.5 to 1.5
- gain_ffn: float32 [512], replicated, may hold values from 0.5 to 1.5
- gain_write: float32 [512], replicated, may hold values from 0.5 to 1.5
- gate_bias: float32 [512], replicated, may hold values from 1 to 3
- out_grad: bfloat16 [16, 1024, 512], P('shard', ('ctx', 'tp')), may hold values from -6 to 6
- memory_grad: float32 [16, 128, 512], P('shard', 'ctx'), may hold values from -6 to 6
Outputs:
- outputs: bfloat16 [16, 1024, 512], P('shard', ('ctx', 'tp'))
- memories_after: float32 [16, 128, 512], P('shard', 'ctx')
- input_grad: bfloat16 [16, 1024, 512], P('shard', ('ctx', 'tp'))
- memory_in_grad: float32 [16, 128, 512], P('shard', 'ctx')
- grad_w_query: float32 [512, 512], P(('shard', 'ctx'), 'tp')
- grad_w_key: float32 [512, 512], P(('shard', 'ctx'), 'tp')
- grad_w_value: float32 [512, 512], P(('shard', 'ctx'), 'tp')
- grad_w_out: float32 [512, 512], P(('shard', 'ctx', 'tp'))
- grad_w_up: float32 [512, 2048], P(('shard', 'ctx', 'tp'))
- grad_w_down: float32 [2048, 512], P(('shard', 'ctx', 'tp'))
- grad_u_query: float32 [512, 512], P(('shard', 'ctx'), 'tp')
- grad_u_key: float32 [512, 512], P(('shard', 'ctx'), 'tp')
- grad_u_value: float32 [512, 512], P(('shard', 'ctx'), 'tp')
- grad_u_out: float32 [512, 512], P('tp', ('shard', 'ctx'))
- grad_u_gate: float32 [512, 512], P('tp', ('shard', 'ctx'))
- grad_gain_attn: float32 [512], P(('shard', 'ctx', 'tp'))
- grad_gain_ffn: float32 [512], P(('shard', 'ctx', 'tp'))
- grad_gain_write: float32 [512], P(('shard', 'ctx', 'tp'))
- grad_gate_bias: float32 [512], P(('shard', 'ctx', 'tp'))
The draws below stay inside these ranges and needn't reach their ends.
Inputs may be any that keep to these rules, and one draw needn't show every extreme that they name: `piece_len`: each segment has one picture piece of 64 to 256 tokens; some piece has exactly 256. A piece lies inside its segment: piece_start + piece_len <= 512.
All inputs are finite; a program needn't handle non-finite values.
Results may differ from the reference program's by a relative error of at most 0.03.
Values may be sent and summed in bfloat16 or wider, within the bound.
A program may use at most 128 MiB of HBM per device.

```python
import math
import jax
import jax.numpy as jnp
from jax import lax

D = 512
HEADS = 8
HEAD_DIM = 64
FF = 2048
SLOTS = 64
SEG = 512
PIECE = 256
SEQS = 16
SEGS = 2
LENGTH = 1024


def piece_table(key):
    length_key = jax.random.fold_in(key, 101)
    place_key = jax.random.fold_in(key, 202)
    lengths = jax.random.randint(length_key, (SEQS, SEGS), PIECE // 4, PIECE + 1)
    lengths = lengths.at[0, 0].set(PIECE)
    place_raw = jax.random.randint(place_key, (SEQS, SEGS), 0, 1 << 20)
    starts = place_raw % (SEG - lengths + 1)
    return (starts.astype(jnp.int32), lengths.astype(jnp.int32))


def draw_piece_start(key, part):
    return piece_table(key)[0]


def draw_piece_len(key, part):
    return piece_table(key)[1]


def level_of(key, dims, shards, least, top_value):
    gain, own = 1.0, jax.random.fold_in(key, 6)
    for dim, blocks in shards:
        heights = jnp.exp(jax.random.uniform(jax.random.fold_in(own, dim), (blocks,), jnp.float32, least / len(shards), top_value / len(shards)))
        gain = gain * jnp.repeat(heights, dims[dim] // blocks).reshape([-1 if axis == dim else 1 for axis in range(len(dims))])
    return gain


def scatter_about(rng, extent, deviation, bound, split=(), kind=jnp.bfloat16):
    array = jax.random.normal(rng, extent, jnp.float32) * deviation
    if len(split) > 0:
        array = level_of(rng, extent, split, -0.22, 0.18) * array
    return jnp.clip(array, min=-bound, max=bound).astype(kind)


def setup_inputs(seed: int = 0) -> dict:
    streams_of = jax.random.split(jax.random.key(seed), 22)
    inputs = scatter_about(streams_of[0], (SEQS, LENGTH, D), 1.0, 6.0, ((0, 4), (1, 2)))
    first_memory = scatter_about(streams_of[1], (SEQS, SLOTS, D), 1.0, 6.0, ((0, 4),), jnp.float32)
    piece_start = draw_piece_start(jax.random.fold_in(streams_of[21], 71), 0)
    piece_len = draw_piece_len(jax.random.fold_in(streams_of[21], 71), 0)
    w_query = scatter_about(streams_of[4], (D, D), D ** -0.5, 0.25, ((0, 16),))
    w_key = scatter_about(streams_of[5], (D, D), D ** -0.5, 0.25, ((0, 16),))
    w_value = scatter_about(streams_of[6], (D, D), D ** -0.5, 0.25, ((0, 16),))
    w_out = scatter_about(streams_of[7], (D, D), (D // 16) ** -0.5, 1.0, ((0, 16),))
    w_up = scatter_about(streams_of[8], (D, FF), D ** -0.5, 0.25, ((0, 16),))
    w_down = scatter_about(streams_of[9], (FF, D), FF ** -0.5, 0.125, ((0, 16),))
    u_query = scatter_about(streams_of[10], (D, D), D ** -0.5, 0.25, ((0, 16),))
    u_key = scatter_about(streams_of[11], (D, D), D ** -0.5, 0.25, ((0, 16),))
    u_value = scatter_about(streams_of[12], (D, D), D ** -0.5, 0.25, ((0, 16),))
    u_out = scatter_about(streams_of[13], (D, D), (D // 16) ** -0.5, 1.0, ((0, 16),))
    u_gate = scatter_about(streams_of[14], (D, D), D ** -0.5, 0.25, ((0, 16),))
    gain_attn = jnp.clip(1.0 + 0.1 * jax.random.normal(streams_of[15], (D,), jnp.float32), 0.5, 1.5)
    gain_ffn = jnp.clip(1.0 + 0.1 * jax.random.normal(streams_of[16], (D,), jnp.float32), 0.5, 1.5)
    gain_write = jnp.clip(1.0 + 0.1 * jax.random.normal(streams_of[17], (D,), jnp.float32), 0.5, 1.5)
    gate_bias = jnp.clip(jax.random.uniform(streams_of[18], (D,), jnp.float32, 1.0, 3.0), 1.0, 3.0)
    out_grad = scatter_about(streams_of[19], (SEQS, LENGTH, D), 1.0, 6.0, ((0, 4), (1, 8)))
    memory_grad = scatter_about(streams_of[20], (SEQS, SEGS * SLOTS, D), 1.0, 6.0, ((0, 4), (1, 2)), jnp.float32)
    return {"inputs": inputs, "first_memory": first_memory, "piece_start": piece_start, "piece_len": piece_len, "w_query": w_query, "w_key": w_key, "w_value": w_value, "w_out": w_out, "w_up": w_up, "w_down": w_down, "u_query": u_query, "u_key": u_key, "u_value": u_value, "u_out": u_out, "u_gate": u_gate, "gain_attn": gain_attn, "gain_ffn": gain_ffn, "gain_write": gain_write, "gate_bias": gate_bias, "out_grad": out_grad, "memory_grad": memory_grad}


EPS = 1e-05
HIGH = lax.Precision.HIGHEST

@jax.custom_vjp
def low(v):
    return lax.optimization_barrier(v.astype(jnp.bfloat16)).astype(jnp.float32)

@jax.custom_vjp
def low_back(v):
    return v

def low_keep(v):
    return (low(v), None)

def low_pass(kept, grad):
    return (grad,)

def back_keep(v):
    return (v, None)

def back_low(kept, grad):
    return (low(grad),)
low.defvjp(low_keep, low_pass)
low_back.defvjp(back_keep, back_low)

def both_low(values):
    return low(low_back(values))

def norm_rows(values):
    centered = values - lax.optimization_barrier(jnp.mean(values, axis=-1, keepdims=True))
    return centered * lax.rsqrt(lax.optimization_barrier(jnp.mean(centered * centered, axis=-1, keepdims=True)) + EPS)

def project(left, right):
    return jnp.dot(left, right, precision=HIGH)

def attend(queries, key_rows, value_rows, allowed):
    row_count = queries.shape[0]
    key_count = key_rows.shape[0]
    score_scale = 1.0 / math.sqrt(HEAD_DIM)
    query_heads = queries.reshape(row_count, HEADS, HEAD_DIM)
    key_heads = key_rows.reshape(key_count, HEADS, HEAD_DIM)
    value_heads = value_rows.reshape(key_count, HEADS, HEAD_DIM)
    scores = jnp.einsum('qhe,khe->hqk', query_heads, key_heads, precision=HIGH) * score_scale
    scores = low_back(jnp.where(allowed[None], scores, -1e+30))
    soft_probs = jax.nn.softmax(scores, axis=-1)
    mixed_heads = jnp.einsum('hqk,khe->qhe', low(soft_probs), value_heads, precision=HIGH)
    return both_low(mixed_heads.reshape(row_count, HEADS * HEAD_DIM))

def mask_for(piece_first, length):
    row_ids = jnp.arange(SEG)[:, None]
    col_ids = jnp.arange(SEG)[None, :]
    inside = (row_ids >= piece_first) & (row_ids < piece_first + length) & (col_ids >= piece_first) & (col_ids < piece_first + length)
    tokens = (col_ids <= row_ids) | inside
    return jnp.concatenate([jnp.ones((SEG, SLOTS), jnp.bool_), tokens], axis=1)

def segment(weights, memory, x_seg, piece_first, length):
    w_query, w_key, w_value, w_out, w_up, w_down, u_query, u_key, u_value, u_out, u_gate, gain_attn, gain_ffn, gain_write, gate_bias = weights
    enc_in = low(norm_rows(jnp.concatenate([memory, x_seg], axis=0)) * gain_attn)
    queries = both_low(project(enc_in[SLOTS:], w_query))
    key_rows = both_low(project(enc_in, w_key))
    value_rows = both_low(project(enc_in, w_value))
    mixed = attend(queries, key_rows, value_rows, mask_for(piece_first, length))
    after_attn = x_seg + low_back(project(mixed, w_out))
    ffn_in = low(norm_rows(after_attn) * gain_ffn)
    pre_act = low_back(project(ffn_in, w_up))
    activ = low(jax.nn.gelu(pre_act, approximate=True))
    outputs = after_attn + low_back(project(activ, w_down))
    write_in = low(norm_rows(jnp.concatenate([memory, outputs], axis=0)) * gain_write)
    slot_queries = both_low(project(write_in[:SLOTS], u_query))
    slot_keys = both_low(project(write_in, u_key))
    slot_values = both_low(project(write_in, u_value))
    written = attend(slot_queries, slot_keys, slot_values, jnp.ones((SLOTS, SLOTS + SEG), jnp.bool_))
    update = low_back(project(written, u_out))
    gate_open = jax.nn.sigmoid(low_back(project(write_in[:SLOTS], u_gate)) + gate_bias)
    new_memory = gate_open * memory + (1.0 - gate_open) * jnp.tanh(update)
    return (new_memory, outputs)

def forward(weights, inputs, first_memory, nudges, piece_start, piece_len):

    def one_sequence(pieces):
        x_seq, memory_start, nudge_seq, start_seq, length_seq = pieces

        def one_segment(memory, parts):
            x_seg, nudge, piece_first, length = parts
            new_memory, outputs = jax.checkpoint(segment)(weights, memory + nudge, x_seg, piece_first, length)
            return (new_memory, (outputs, new_memory))
        last_memory, (outputs, memories) = lax.scan(one_segment, memory_start, (x_seq.reshape(SEGS, SEG, D), nudge_seq, start_seq, length_seq))
        return (outputs.reshape(LENGTH, D), memories.reshape(SEGS * SLOTS, D))
    return lax.map(one_sequence, (inputs, first_memory, nudges, piece_start, piece_len))

def reference(inputs, first_memory, piece_start, piece_len, w_query, w_key, w_value, w_out, w_up, w_down, u_query, u_key, u_value, u_out, u_gate, gain_attn, gain_ffn, gain_write, gate_bias, out_grad, memory_grad):
    weights = tuple((item.astype(jnp.float32) for item in (w_query, w_key, w_value, w_out, w_up, w_down, u_query, u_key, u_value, u_out, u_gate, gain_attn, gain_ffn, gain_write, gate_bias)))
    nudges = jnp.zeros((SEQS, SEGS, SLOTS, D), jnp.float32)

    def wrapped(weight_set, token_rows, nudge_set):
        return forward(weight_set, token_rows, first_memory, nudge_set, piece_start, piece_len)
    (outputs, memories), pullback = jax.vjp(wrapped, weights, inputs.astype(jnp.float32), nudges)
    weight_grads, input_grad, nudge_grad = pullback((out_grad.astype(jnp.float32), memory_grad))
    g_query, g_key, g_value, g_out, g_up, g_down, g_uquery, g_ukey, g_uvalue, g_uout, g_ugate, g_gain_attn, g_gain_ffn, g_gain_write, g_bias = weight_grads
    return (outputs.astype(jnp.bfloat16), memories, input_grad.astype(jnp.bfloat16), nudge_grad.reshape(SEQS, SEGS * SLOTS, D), g_query, g_key, g_value, g_out, g_up, g_down, g_uquery, g_ukey, g_uvalue, g_uout, g_ugate, g_gain_attn, g_gain_ffn, g_gain_write, g_bias)
```

```python
from functools import partial

import jax
import jax.numpy as jnp
from jax import lax
from jax.experimental import pallas as pl
from jax.experimental.pallas import tpu as pltpu
from jax.sharding import PartitionSpec as P

F32 = jnp.float32
BF = jnp.bfloat16
MESH = pl.DeviceIdType.MESH
HEAD = 64
EPS = 1e-05
NEG = -1e30
VMEM_LIMIT = 67000000

WQ, WK, WV, WO, WUP, WDOWN, UQ, UK, UV, UO, UGATE = 0, 1, 2, 3, 4, 8, 12, 13, 14, 15, 16
TILES = 17


def dot(a, b):
    return lax.dot_general(a, b, (((1,), (0,)), ((), ())), preferred_element_type=F32)


def dot_nt(a, b):
    return lax.dot_general(a, b, (((1,), (1,)), ((), ())), preferred_element_type=F32)


def dot_tn(a, b):
    return lax.dot_general(a, b, (((0,), (0,)), ((), ())), preferred_element_type=F32)


def rows_at(i, size):
    return pl.ds(pl.multiple_of(i * size, size), size)


def loop(count, unroll=1):
    def run(body):
        def step(i, carry):
            body(i)
            return carry

        lax.fori_loop(0, count, step, 0, unroll=unroll)

    return run


def normed(v):
    mean = jnp.mean(v, axis=-1, keepdims=True)
    centered = v - mean
    inv = lax.rsqrt(jnp.mean(centered * centered, axis=-1, keepdims=True) + EPS)
    return centered * inv, inv


def norm_pull(e, gain, hat, inv):
    h = e * gain
    m0 = jnp.mean(h, axis=-1, keepdims=True)
    m1 = jnp.mean(h * hat, axis=-1, keepdims=True)
    return inv * (h - m0 - hat * m1)


def lane_block(width, block):
    return lax.broadcasted_iota(jnp.int32, (1, width), 1) // block


class Weights:
    def __init__(self, ref):
        self.ref = ref
        self.blocks, _, self.rows, self.width = ref.shape

    def cols(self, tile, start, size):
        got = self.ref[:, tile, :, pl.ds(start, size)]
        return got.reshape(self.blocks * self.rows, size)

    def row_part(self, tile, part, parts):
        count = self.blocks // parts
        got = self.ref[pl.ds(part * count, count), tile]
        return got.reshape(count * self.rows, self.width)

    def down_cols(self, chunk, chunks, start, size):
        count = self.blocks // chunks
        got = self.ref[pl.ds(chunk * count, count), WDOWN : WDOWN + 4, :, pl.ds(start, size)]
        return got.reshape(count * 4 * self.rows, size)

    def down_rows(self, part, parts):
        count = self.blocks // parts
        got = self.ref[pl.ds(part * count, count), WDOWN : WDOWN + 4]
        return got.reshape(count * 4 * self.rows, self.width)


def unit_scratch(tokens, slots, width, ff):
    r = tokens + slots
    heads = width // HEAD
    quads = width // 256
    v = pltpu.VMEM
    return dict(
        mem=v((slots, width), F32),
        bias=v((tokens, tokens), F32),
        xh=v((r, width), F32),
        xr=v((r, 1), F32),
        enc=v((r, width), BF),
        q=v((tokens, width), BF),
        k=v((r, width), BF),
        v=v((r, width), BF),
        kt=v((width, r), BF),
        vt=v((width, r), BF),
        pt=v((heads, r, tokens), BF),
        mixt=v((width, tokens), BF),
        af=v((tokens, width), F32),
        ah=v((tokens, width), F32),
        ar=v((tokens, 1), F32),
        fin=v((tokens, width), BF),
        act=v((ff // 512, tokens, 512), BF),
        dg=v((ff // 512, tokens, 512), BF),
        y=v((tokens, width), F32),
        yh=v((tokens, width), F32),
        yr=v((tokens, 1), F32),
        wri=v((r, width), BF),
        sq=v((slots, width), BF),
        sk=v((r, width), BF),
        sv=v((r, width), BF),
        spt=v((quads, r, 256), BF),
        wrt=v((slots, width), BF),
        gate=v((slots, width), F32),
        f1=v((slots, width), F32),
        f2=v((slots, width), F32),
        gm=v((slots, width), F32),
        gup=v((slots, width), BF),
        ggl=v((slots, width), BF),
        dsq=v((slots, width), BF),
        dsk=v((r, width), BF),
        dsv=v((r, width), BF),
        e=v((r, width), F32),
        gy=v((tokens, width), F32),
        gyb=v((tokens, width), BF),
        bwm=v((slots, width), F32),
        gpre=v((ff // 512, tokens, 512), BF),
        gab=v((tokens, width), BF),
        gmx=v((tokens, width), BF),
        dst=v((2, r, tokens), BF),
        dqt=v((width, tokens), BF),
        dq=v((tokens, width), BF),
        dk=v((r, width), BF),
        dv=v((r, width), BF),
    )


class Unit:
    def __init__(self, refs, w, x, gains, small):
        self.__dict__.update(refs)
        self.w = w
        self.x = x
        self.gains = gains
        self.small = small
        self.tokens, self.width = x.shape
        self.slots = self.mem.shape[0]
        self.r = self.tokens + self.slots
        self.ff = self.act.shape[0] * 512

    def gain(self, i):
        return self.gains[i : i + 1, :]

    def make_bias(self, first, length):
        t = self.tokens

        @loop(t // 64)
        def _(i):
            key = lax.broadcasted_iota(jnp.int32, (64, t), 0) + i * 64
            query = lax.broadcasted_iota(jnp.int32, (64, t), 1)
            last = first + length
            inside = (key >= first) & (key < last) & (query >= first) & (query < last)
            seen = (key <= query) | inside
            self.bias[rows_at(i, 64), :] = jnp.where(seen, 0.0, NEG).astype(F32)

    def norm_in(self, rows, values):
        hat, inv = normed(values)
        self.xh[rows, :] = hat
        self.xr[rows, :] = inv
        self.enc[rows, :] = (hat * self.gain(0)).astype(BF)

    def tokens_in(self):
        @loop(self.tokens // 32, unroll=2)
        def _(i):
            rows = rows_at(i, 32)
            self.norm_in(rows, self.x[rows, :].astype(F32))

    def project_tokens(self):
        t = self.tokens

        @loop(self.width // 256)
        def _(n):
            cols = rows_at(n, 256)
            enc = self.enc[0:t, :]
            got = dot(enc, self.w.cols(WQ, n * 256, 256)).astype(BF)
            self.q[:, cols] = got * BF(HEAD**-0.5)
            self.k[0:t, cols] = dot(enc, self.w.cols(WK, n * 256, 256)).astype(BF)
            self.v[0:t, cols] = dot(enc, self.w.cols(WV, n * 256, 256)).astype(BF)

    def memory_in(self):
        t, r = self.tokens, self.r
        self.norm_in(slice(t, r), self.mem[...])
        enc = self.enc[t:r, :]
        self.k[t:r, :] = dot(enc, self.w.cols(WK, 0, self.width)).astype(BF)
        self.v[t:r, :] = dot(enc, self.w.cols(WV, 0, self.width)).astype(BF)
        self.vt[...] = self.v[...].T

    def attend(self):
        t, r = self.tokens, self.r

        @loop(self.width // 128)
        def _(p):
            cols = rows_at(p, 128)
            keys = self.k[:, cols]
            half = lane_block(128, HEAD)
            for hh in range(2):
                feats = pl.ds(pl.multiple_of(p * 128 + hh * HEAD, HEAD), HEAD)
                values = self.vt[feats, :]
                for n in range(t // 256):
                    qc = slice(n * 256, n * 256 + 256)
                    q = self.q[qc, cols]
                    q = jnp.where(half == hh, q, jnp.zeros_like(q))
                    s = dot_nt(keys, q)
                    s_tok = s[0:t] + self.bias[:, qc]
                    s_mem = s[t:r]
                    peak = jnp.maximum(
                        jnp.max(s_tok, axis=0, keepdims=True), jnp.max(s_mem, axis=0, keepdims=True)
                    )
                    e_tok = jnp.exp(s_tok - peak)
                    e_mem = jnp.exp(s_mem - peak)
                    inv = 1.0 / (
                        jnp.sum(e_tok, axis=0, keepdims=True)
                        + jnp.sum(e_mem, axis=0, keepdims=True)
                    )
                    probs = jnp.concatenate([e_tok * inv, e_mem * inv], axis=0).astype(BF)
                    self.pt[2 * p + hh, :, qc] = probs
                    self.mixt[feats, qc] = dot(values, probs).astype(BF)

    def after_attention(self):
        t = self.tokens
        self.gmx[...] = self.mixt[...].T

        @loop(self.width // 256)
        def _(n):
            cols = rows_at(n, 256)
            got = dot(self.gmx[...], self.w.cols(WO, n * 256, 256))
            self.af[:, cols] = self.x[:, cols].astype(F32) + got

        @loop(t // 32, unroll=2)
        def _(i):
            rows = rows_at(i, 32)
            hat, inv = normed(self.af[rows, :])
            self.ah[rows, :] = hat
            self.ar[rows, :] = inv
            self.fin[rows, :] = (hat * self.gain(1)).astype(BF)

    def feed_forward(self):
        t = self.tokens
        for j in range(self.ff // 512):

            @loop(2)
            def _(n, j=j):
                cols = rows_at(n, 256)
                weights = self.w.cols(WUP + j, n * 256, 256)
                for m in range(t // 128):
                    rows = slice(m * 128, m * 128 + 128)
                    pre = dot(self.fin[rows, :], weights)
                    c = 0.7978845608028654
                    sq = pre * pre
                    th = jnp.tanh(pre * (c + (c * 0.044715) * sq))
                    half = 0.5 + 0.5 * th
                    self.act[j, rows, cols] = (pre * half).astype(BF)
                    slope = half + (0.5 * pre) * (1.0 - th * th) * (c + (3 * c * 0.044715) * sq)
                    self.dg[j, rows, cols] = slope.astype(BF)

        @loop(self.width // 256)
        def _(n):
            cols = rows_at(n, 256)
            total = self.af[:, cols]
            for j in range(self.ff // 512):
                total = total + dot(
                    self.act[j], self.w.down_cols(j, self.ff // 512, n * 256, 256)
                )
            self.y[:, cols] = total

        @loop(t // 32, unroll=2)
        def _(i):
            rows = rows_at(i, 32)
            hat, inv = normed(self.y[rows, :])
            self.yh[rows, :] = hat
            self.yr[rows, :] = inv
            self.wri[rows, :] = (hat * self.gain(2)).astype(BF)

        self.wri[t : self.r, :] = (self.xh[t : self.r, :] * self.gain(2)).astype(BF)

    def spread_heads(self, rows, g):
        part = rows[:, g * 256 : g * 256 + 256]
        block = lane_block(256, HEAD)
        return jnp.concatenate(
            [jnp.where(block == h, part, jnp.zeros_like(part)) for h in range(4)], axis=0
        )

    def gather_heads(self, stacked):
        block = lane_block(256, HEAD)
        s = self.slots
        total = jnp.where(block == 0, stacked[0:s], 0.0)
        for h in range(1, 4):
            total = total + jnp.where(block == h, stacked[h * s : h * s + s], 0.0)
        return total

    def write_memory(self):
        t, r = self.tokens, self.r

        @loop(self.width // 256)
        def _(n):
            cols = rows_at(n, 256)
            wri = self.wri[...]
            self.sk[:, cols] = dot(wri, self.w.cols(UK, n * 256, 256)).astype(BF)
            self.sv[:, cols] = dot(wri, self.w.cols(UV, n * 256, 256)).astype(BF)

        wm = self.wri[t:r, :]
        sq = dot(wm, self.w.cols(UQ, 0, self.width)).astype(BF)
        self.sq[...] = sq * BF(HEAD**-0.5)
        for g in range(self.width // 256):
            cols = slice(g * 256, g * 256 + 256)
            s = dot_nt(self.sk[:, cols], self.spread_heads(self.sq[...], g))
            e = jnp.exp(s - jnp.max(s, axis=0, keepdims=True))
            probs = (e * (1.0 / jnp.sum(e, axis=0, keepdims=True))).astype(BF)
            self.spt[g] = probs
            self.wrt[:, cols] = self.gather_heads(dot_tn(probs, self.sv[:, cols])).astype(BF)
        th = jnp.tanh(dot(self.wrt[...], self.w.cols(UO, 0, self.width)))
        pre = dot(wm, self.w.cols(UGATE, 0, self.width))
        gate = jax.nn.sigmoid(pre + self.gain(3))
        mem = self.mem[...]
        self.gate[...] = gate
        self.f1[...] = (mem - th) * gate * (1.0 - gate)
        self.f2[...] = (1.0 - gate) * (1.0 - th * th)
        return gate * mem + (1.0 - gate) * th

    def backward_early(self):
        self.kt[...] = self.k[...].T

    def write_back(self, out_grad):
        t, r, s = self.tokens, self.r, self.slots
        gm = self.gm[...]
        ggp = gm * self.f1[...]
        gup = (gm * self.f2[...]).astype(BF)
        ggl = ggp.astype(BF)
        self.gup[...] = gup
        self.ggl[...] = ggl
        self.small[3:4, :] = jnp.sum(ggp, axis=0, keepdims=True)
        gwr = dot_nt(gup, self.w.row_part(UO, 0, 1)).astype(BF)
        for g in range(self.width // 256):
            cols = slice(g * 256, g * 256 + 256)
            grads = self.spread_heads(gwr, g)
            dp = dot_nt(self.sv[:, cols], grads)
            probs = self.spt[g]
            pf = probs.astype(F32)
            ds = (pf * (dp - jnp.sum(pf * dp, axis=0, keepdims=True))).astype(BF)
            self.dsv[:, cols] = dot(probs, grads).astype(BF)
            self.dsk[:, cols] = dot(ds, self.spread_heads(self.sq[...], g)).astype(BF)
            dq = self.gather_heads(dot_tn(ds, self.sk[:, cols])) * HEAD**-0.5
            self.dsq[:, cols] = dq.astype(BF)

        @loop(2)
        def _(n):
            cols = rows_at(n, self.width // 2)
            self.e[:, cols] = dot_nt(self.dsk[...], self.w.row_part(UK, n, 2)) + dot_nt(
                self.dsv[...], self.w.row_part(UV, n, 2)
            )

        em = self.e[t:r, :] + dot_nt(self.dsq[...], self.w.row_part(UQ, 0, 1))
        em = em + dot_nt(ggl, self.w.row_part(UGATE, 0, 1))
        hat = self.xh[t:r, :]
        self.bwm[...] = norm_pull(em, self.gain(2), hat, self.xr[t:r, :])
        self.small[2:3, :] = jnp.sum(em * hat, axis=0, keepdims=True)

        @loop(t // 32, unroll=2)
        def _(i):
            rows = rows_at(i, 32)
            e = self.e[rows, :]
            hat = self.yh[rows, :]
            self.small[2:3, :] += jnp.sum(e * hat, axis=0, keepdims=True)
            grad = out_grad[rows, :].astype(F32) + norm_pull(e, self.gain(2), hat, self.yr[rows, :])
            self.gy[rows, :] = grad
            self.gyb[rows, :] = grad.astype(BF)

    def feed_forward_back(self):
        t = self.tokens
        chunks = self.ff // 512

        for j in range(chunks):

            @loop(2)
            def _(n, j=j):
                cols = rows_at(n, 256)
                weights = self.w.down_rows(2 * j + n, 2 * chunks)
                for m in range(t // 128):
                    rows = slice(m * 128, m * 128 + 128)
                    got = dot_nt(self.gyb[rows, :], weights)
                    self.gpre[j, rows, cols] = (got * self.dg[j, rows, cols].astype(F32)).astype(BF)

        @loop(2)
        def _(n):
            cols = rows_at(n, self.width // 2)
            total = dot_nt(self.gpre[0], self.w.row_part(WUP, n, 2))
            for j in range(1, chunks):
                total = total + dot_nt(self.gpre[j], self.w.row_part(WUP + j, n, 2))
            self.e[0:t, cols] = total

        self.small[1:2, :] = jnp.zeros((1, self.width), F32)

        @loop(t // 32, unroll=2)
        def _(i):
            rows = rows_at(i, 32)
            e = self.e[rows, :]
            hat = self.ah[rows, :]
            self.small[1:2, :] += jnp.sum(e * hat, axis=0, keepdims=True)
            grad = self.gy[rows, :] + norm_pull(e, self.gain(1), hat, self.ar[rows, :])
            self.gy[rows, :] = grad
            self.gab[rows, :] = grad.astype(BF)

    def attend_back(self):
        t, r = self.tokens, self.r

        @loop(2)
        def _(n):
            cols = rows_at(n, self.width // 2)
            self.gmx[:, cols] = dot_nt(self.gab[...], self.w.row_part(WO, n, 2)).astype(BF)

        @loop(self.width // 128)
        def _(p):
            cols = rows_at(p, 128)
            values = self.v[:, cols]
            half = lane_block(128, HEAD)
            for hh in range(2):
                feats = pl.ds(pl.multiple_of(p * 128 + hh * HEAD, HEAD), HEAD)
                keys = self.kt[feats, :]
                for n in range(t // 256):
                    qc = slice(n * 256, n * 256 + 256)
                    g = self.gmx[qc, cols]
                    g = jnp.where(half == hh, g, jnp.zeros_like(g))
                    dp = dot_nt(values, g)
                    pf = self.pt[2 * p + hh, :, qc].astype(F32)
                    ds = (pf * (dp - jnp.sum(pf * dp, axis=0, keepdims=True))).astype(BF)
                    self.dst[hh, :, qc] = ds
                    self.dqt[feats, qc] = (dot(keys, ds) * HEAD**-0.5).astype(BF)
            g = self.gmx[:, cols]
            q = self.q[:, cols]
            dv = jnp.where(half == 0, dot(self.pt[2 * p], g), dot(self.pt[2 * p + 1], g))
            self.dv[:, cols] = dv.astype(BF)
            dk = jnp.where(half == 0, dot(self.dst[0], q), dot(self.dst[1], q))
            self.dk[:, cols] = dk.astype(BF)

        self.dq[...] = self.dqt[...].T

    def enter_back(self, input_grad):
        t, r = self.tokens, self.r

        @loop(2)
        def _(n):
            cols = rows_at(n, self.width // 2)
            self.e[:, cols] = dot_nt(self.dk[...], self.w.row_part(WK, n, 2)) + dot_nt(
                self.dv[...], self.w.row_part(WV, n, 2)
            )
            self.e[0:t, cols] += dot_nt(self.dq[...], self.w.row_part(WQ, n, 2))

        e = self.e[t:r, :]
        hat = self.xh[t:r, :]
        self.small[0:1, :] = jnp.sum(e * hat, axis=0, keepdims=True)
        mem_grad = self.gm[...] * self.gate[...] + self.bwm[...]
        mem_grad = mem_grad + norm_pull(e, self.gain(0), hat, self.xr[t:r, :])

        @loop(t // 32, unroll=2)
        def _(i):
            rows = rows_at(i, 32)
            e = self.e[rows, :]
            hat = self.xh[rows, :]
            self.small[0:1, :] += jnp.sum(e * hat, axis=0, keepdims=True)
            grad = self.gy[rows, :] + norm_pull(e, self.gain(0), hat, self.xr[rows, :])
            input_grad[rows, :] = grad.astype(BF)

        return mem_grad


class Packing:
    HEADS = dict(wq=0, wk=1, wv=2, uq=3, uk=4, uv=5, uo=6, ugate=7)

    def __init__(self, shards, ctxs, width, ff):
        self.shards, self.ctxs, self.width, self.ff = shards, ctxs, width, ff
        self.head_rows = width // (shards * ctxs)
        self.row_rows = width // (shards * ctxs * 4)
        self.down_rows = ff // (shards * ctxs * 4)
        self.at_down = 0
        self.at_up = self.at_down + self.down_rows * (width // 128)
        self.at_wo = self.at_up + self.row_rows * (ff // 128)
        self.at_heads = self.at_wo + self.row_rows * (width // 128)
        self.rows = self.at_heads + 8 * self.head_rows

    @property
    def shape(self):
        return (self.shards, self.ctxs, 2, 2, self.rows, 128)


def weight_grads(u, g, pk, names):
    width = u.width
    tile = 256

    def store_head(at, m, got):
        h = pk.head_rows
        per = tile // h
        for i in range(per):
            s = m * (per // pk.ctxs) + i // pk.ctxs
            for t in range(4):
                g[s, i % pk.ctxs, t // 2, t % 2, at : at + h, :] = got[
                    i * h : i * h + h, t * 128 : t * 128 + 128
                ]

    def store_rows(at, h, m, got, chunk0):
        per = tile // h
        for i in range(per):
            if per % (pk.ctxs * 4) == 0:
                s, c = m * (per // (pk.ctxs * 4)) + i // (pk.ctxs * 4), (i // 4) % pk.ctxs
            else:
                owner = m * (per // 4) + i // 4
                s, c = lax.div(owner, pk.ctxs), lax.rem(owner, pk.ctxs)
            for j in range(got.shape[1] // 128):
                lo = at + (chunk0 + j) * h
                g[s, c, (i // 2) % 2, i % 2, lo : lo + h, :] = got[
                    i * h : i * h + h, j * 128 : j * 128 + 128
                ]

    def head(name, left, right):
        at = pk.at_heads + pk.HEADS[name] * pk.head_rows

        @loop(width // tile)
        def _(m):
            lt = left[:, rows_at(m, tile)].T
            store_head(at, m, dot(lt, right[...]).astype(BF))

    t, r = u.tokens, u.r
    if "ff" in names:
        for j in range(u.ff // 512):

            @loop(512 // tile)
            def _(m, j=j):
                lt = u.act[j, :, rows_at(m, tile)].T
                got = dot(lt, u.gyb[...]).astype(BF)
                store_rows(pk.at_down, pk.down_rows, m + j * (512 // tile), got, 0)

        @loop(width // tile)
        def _(m):
            lt = u.fin[:, rows_at(m, tile)].T
            for j in range(u.ff // 512):
                store_rows(pk.at_up, pk.row_rows, m, dot(lt, u.gpre[j]).astype(BF), 4 * j)

    if "wo" in names:

        @loop(width // tile)
        def _(m):
            got = dot(u.mixt[rows_at(m, tile), :], u.gab[...]).astype(BF)
            store_rows(pk.at_wo, pk.row_rows, m, got, 0)

    if "write" in names:
        head("uq", u.wri.at[t:r], u.dsq)
        head("uk", u.wri, u.dsk)
        head("uv", u.wri, u.dsv)
        head("uo", u.gup, u.wrt)
        head("ugate", u.ggl, u.wri.at[t:r])
    if "enter" in names:
        head("wq", u.enc.at[0:t], u.dq)
        head("wk", u.enc, u.dk)
        head("wv", u.enc, u.dv)


def unit_kernel(
    ctxs, pk, names, first, length, w, x, first_memory, gains, out_grad, memory_grad, *rest
):
    outs, scratch = rest[:6], rest[6:]
    outputs, memory_out, input_grad, memory_in, grads, small = outs
    refs = dict(zip(names, scratch[: len(names)]))
    u = Unit(refs, Weights(w), x, gains, small)
    if ctxs > 1:
        m_send, m_recv, g_send, g_recv, sems = scratch[len(names) :]
        c = lax.axis_index("ctx")
        greet([(c > 0, {"ctx": c - 1}), (c < ctxs - 1, {"ctx": c + 1})])

        def memory_copy(to):
            return pltpu.make_async_remote_copy(
                src_ref=m_send, dst_ref=m_recv, send_sem=sems.at[0], recv_sem=sems.at[1],
                device_id={"ctx": to}, device_id_type=MESH,
            )

        def grad_copy(to):
            return pltpu.make_async_remote_copy(
                src_ref=g_send, dst_ref=g_recv, send_sem=sems.at[2], recv_sem=sems.at[3],
                device_id={"ctx": to}, device_id_type=MESH,
            )

    u.make_bias(first[0], length[0])
    u.tokens_in()
    u.project_tokens()
    if ctxs > 1:

        @pl.when(c == 0)
        def _():
            u.mem[...] = first_memory[...]

        @pl.when(c > 0)
        def _():
            memory_copy(c - 1).wait_recv()
            u.mem[...] = m_recv[...].astype(F32)
    else:
        u.mem[...] = first_memory[...]
    u.memory_in()
    u.attend()
    u.after_attention()
    u.feed_forward()
    after = u.write_memory()
    memory_out[...] = after
    if ctxs > 1:
        m_send[...] = after.astype(BF)

        @pl.when(c < ctxs - 1)
        def _():
            memory_copy(c + 1).start()

    outputs[...] = u.y[...].astype(BF)
    u.backward_early()
    u.gm[...] = memory_grad[...]
    if ctxs > 1:

        @pl.when(c < ctxs - 1)
        def _():
            grad_copy(c + 1).wait_recv()
            u.gm[...] += g_recv[...].astype(F32)

    u.write_back(out_grad)
    u.feed_forward_back()
    u.attend_back()
    back = u.enter_back(input_grad)
    memory_in[...] = back
    if ctxs > 1:
        g_send[...] = back.astype(BF)

        @pl.when(c > 0)
        def _():
            grad_copy(c - 1).start()

    weight_grads(u, grads, pk, ("ff", "wo", "write", "enter"))
    if ctxs > 1:

        @pl.when(c < ctxs - 1)
        def _():
            memory_copy(c + 1).wait_send()

        @pl.when(c > 0)
        def _():
            grad_copy(c - 1).wait_send()


def run_unit(ctxs, pk, first, length, w, x, first_memory, gains, out_grad, memory_grad):
    tokens, width = x.shape
    slots = first_memory.shape[0]
    scratch = unit_scratch(tokens, slots, width, pk.ff)
    vm = pl.BlockSpec(memory_space=pltpu.VMEM)
    sm = pl.BlockSpec(memory_space=pltpu.SMEM)
    extra = []
    params = dict(vmem_limit_bytes=VMEM_LIMIT)
    if ctxs > 1:
        extra = [pltpu.VMEM((slots, width), BF)] * 4 + [pltpu.SemaphoreType.DMA((4,))]
        params.update(collective_id=1, has_side_effects=True)
    shape = jax.ShapeDtypeStruct
    return pl.pallas_call(
        partial(unit_kernel, ctxs, pk, tuple(scratch)),
        out_shape=(
            shape((tokens, width), BF),
            shape((slots, width), F32),
            shape((tokens, width), BF),
            shape((slots, width), F32),
            shape(pk.shape, BF),
            shape((8, width), F32),
        ),
        in_specs=[sm, sm] + [vm] * 6,
        out_specs=(vm,) * 6,
        scratch_shapes=list(scratch.values()) + extra,
        compiler_params=pltpu.CompilerParams(**params),
        name="unit",
    )(first, length, w, x, first_memory, gains, out_grad, memory_grad)


GROUPS = ((0, 3), (3, 8), (8, 12), (12, 17))


def greet(peers):
    barrier = pltpu.get_barrier_semaphore()
    count = 0
    for cond, device in peers:

        @pl.when(cond)
        def _(device=device):
            pl.semaphore_signal(barrier, inc=1, device_id=device, device_id_type=MESH)

        count = count + jnp.where(cond, 1, 0)
    pl.semaphore_wait(barrier, count)


class Gather:
    def __init__(self, shards, w, send, recv):
        self.n, self.w, self.send, self.recv = shards, w, send, recv
        self.s = lax.axis_index("shard")
        self.t = lax.axis_index("tp")
        self.partner = self.t + 1 - 2 * lax.rem(self.t, 2)
        self.across = lax.rem(self.t + 2, 4)

    def copy(self, kind, source, tp, g, device):
        lo, hi = GROUPS[g]
        block = self.w.at[source * 4 + tp, lo:hi]
        return pltpu.make_async_remote_copy(
            src_ref=block, dst_ref=block, send_sem=self.send.at[kind, source, g],
            recv_sem=self.recv.at[kind, source, g], device_id=device, device_id_type=MESH,
        )

    def up(self, source, g):
        return self.copy(0, source, self.t, g, {"shard": self.s + 1})

    def down(self, source, g):
        return self.copy(1, source, self.t, g, {"shard": self.s - 1})

    def to_partner(self, source, g):
        return self.copy(2, source, self.t, g, {"tp": self.partner})

    def from_partner(self, source, g):
        return self.copy(2, source, self.partner, g, {"tp": self.partner})

    def to_across(self, source, g):
        return self.copy(3, source, self.t, g, {"tp": self.across})

    def from_across(self, source, g):
        return self.copy(3, source, self.across, g, {"tp": self.across})

    def relay(self, source, g):
        return self.copy(4, source, self.across, g, {"tp": self.partner})

    def from_relay(self, source, g):
        other = lax.rem(self.partner + 2, 4)
        return self.copy(4, source, other, g, {"tp": self.partner})

    def start_own(self, g):
        s, n = self.s, self.n
        if n > 1:

            @pl.when(s < n - 1)
            def _():
                self.up(s, g).start()

            @pl.when(s > 0)
            def _():
                self.down(s, g).start()

        self.to_across(s, g).start()
        self.to_partner(s, g).start()

    def line_step(self, d, g):
        s, n = self.s, self.n

        @pl.when(s - d >= 0)
        def _():
            self.up(s - d, g).wait_recv()

            @pl.when(s < n - 1)
            def _():
                self.up(s - d, g).start()

            self.to_across(s - d, g).start()
            self.to_partner(s - d, g).start()

        @pl.when(s + d <= n - 1)
        def _():
            self.down(s + d, g).wait_recv()

            @pl.when(s > 0)
            def _():
                self.down(s + d, g).start()

            self.to_across(s + d, g).start()
            self.to_partner(s + d, g).start()

    def across_step(self, d, g):
        s, n = self.s, self.n
        for source, cond in ((s - d, s - d >= 0), (s + d, s + d <= n - 1))[: 1 if d == 0 else 2]:

            @pl.when(cond)
            def _(source=source):
                self.from_across(source, g).wait_recv()
                self.relay(source, g).start()

    def finish(self, g):
        s, n = self.s, self.n
        for source in range(n):
            self.from_partner(source, g).wait_recv()
            self.from_relay(source, g).wait_recv()

    def drain(self, g):
        s, n = self.s, self.n
        for source in range(n):
            self.to_across(source, g).wait_send()
            self.to_partner(source, g).wait_send()
            self.relay(source, g).wait_send()

            @pl.when(jnp.logical_and(s >= source, s < n - 1))
            def _(source=source):
                self.up(source, g).wait_send()

            @pl.when(jnp.logical_and(s <= source, s > 0))
            def _(source=source):
                self.down(source, g).wait_send()


def line_peers(n):
    s = lax.axis_index("shard")
    return [(s > 0, {"shard": s - 1}), (s < n - 1, {"shard": s + 1})] if n > 1 else []


def tp_peers():
    t = lax.axis_index("tp")
    return [(t >= 0, {"tp": lax.rem(t + d, 4)}) for d in (1, 2, 3)]


def own_tiles(weights, w, own, sems):
    names = [WQ, WK, WV, WO, WUP, WDOWN, UQ, UK, UV, UO, UGATE]
    rows = w.shape[2]
    out = []
    for name, ref in zip(names, weights):
        parts = {WUP: 4, WDOWN: 4}.get(name, 1)
        for j in range(parts):
            src = ref
            if name == WUP:
                src = ref.at[:, j * 512 : j * 512 + 512]
            if name == WDOWN:
                src = ref.at[j * rows : j * rows + rows]
            out.append(pltpu.make_async_copy(src, w.at[own, name + j], sems.at[name + j]))
    return out


def gather_kernel(shards, *refs):
    weights, out_grad, w, og = refs[:11], refs[11], refs[12], refs[13]
    local, send, recv, og_send, og_recv = refs[14:]
    s, t = lax.axis_index("shard"), lax.axis_index("tp")
    copies = own_tiles(weights, w, s * 4 + t, local)
    for c in copies:
        c.start()
    mine = pltpu.make_async_copy(out_grad.at[t], og.at[t], og_send.at[0])
    mine.start()
    greet(line_peers(shards) + tp_peers())
    gather = Gather(shards, w, send, recv)

    def og_copy(d):
        to = lax.rem(t + d, 4)
        return pltpu.make_async_remote_copy(
            src_ref=out_grad.at[to], dst_ref=og.at[t], send_sem=og_send.at[d],
            recv_sem=og_recv.at[d], device_id={"tp": to}, device_id_type=MESH,
        )

    groups = range(len(GROUPS))
    for g in groups:
        for c in copies[GROUPS[g][0] : GROUPS[g][1]]:
            c.wait()
        gather.start_own(g)
    for d in range(1, shards):
        for g in groups:
            gather.line_step(d, g)
        for g in groups:
            gather.across_step(d - 1, g)
    for d in (1, 2, 3):
        og_copy(d).start()
    for g in groups:
        gather.across_step(shards - 1, g)
    for g in groups:
        gather.finish(g)
    for d in (1, 2, 3):
        og_copy(d).wait_recv()
        og_copy(d).wait_send()
    mine.wait()
    for g in groups:
        gather.drain(g)


def run_gather(shards, weights, out_grad):
    rows, width = weights[0].shape
    share = out_grad.shape[1]
    vm = pl.BlockSpec(memory_space=pltpu.VMEM)
    hbm = pl.BlockSpec(memory_space=pl.ANY)
    dma = pltpu.SemaphoreType.DMA
    shape = jax.ShapeDtypeStruct
    return pl.pallas_call(
        partial(gather_kernel, shards),
        out_shape=(shape((shards * 4, TILES, rows, width), BF), shape((4, share, width), BF)),
        in_specs=[hbm] * 12,
        out_specs=(vm, vm),
        scratch_shapes=[
            dma((TILES,)), dma((5, shards, len(GROUPS))), dma((5, shards, len(GROUPS))), dma((4,)), dma((4,)),
        ],
        compiler_params=pltpu.CompilerParams(
            vmem_limit_bytes=VMEM_LIMIT, collective_id=2, has_side_effects=True
        ),
        name="gather",
    )(*weights, out_grad)


class Reduce:
    def __init__(self, shards, g, r1, r2, r3, zu, zd, send, recv):
        self.n = shards
        self.g, self.r1, self.r2, self.r3, self.zu, self.zd = g, r1, r2, r3, zu, zd
        self.send, self.recv = send, recv
        self.s, self.c, self.t = (lax.axis_index(a) for a in ("shard", "ctx", "tp"))
        self.core = lax.rem(self.t, 2)
        self.x = lax.div(self.t, 2)
        self.partner = {"tp": self.t + 1 - 2 * self.core}
        self.across = {"tp": lax.rem(self.t + 2, 4)}
        self.beside = {"ctx": 1 - self.c}

    def copy(self, src, dst, sem, device):
        return pltpu.make_async_remote_copy(
            src_ref=src, dst_ref=dst, send_sem=self.send.at[sem], recv_sem=self.recv.at[sem],
            device_id=device, device_id_type=MESH,
        )

    def sem(self, kind, chunk):
        return chunk * 9 + kind

    def first(self, k, rows):
        src = self.g.at[:, :, :, 1 - self.core, rows]
        return self.copy(src, self.r1.at[:, :, :, rows], self.sem(0, k), self.partner)

    def second(self, k, rows):
        if k % 2 == 0:
            src, device = self.r1.at[:, :, 1 - self.x, rows], self.across
        else:
            src, device = self.r1.at[:, 1 - self.c, :, rows], self.beside
        return self.copy(src, self.r2.at[:, :, rows], self.sem(1, k), device)

    def third(self, k, rows):
        if k % 2 == 0:
            src, device = self.r2.at[:, 1 - self.c, rows], self.beside
        else:
            src, device = self.r2.at[:, 1 - self.x, rows], self.across
        return self.copy(src, self.r3.at[:, rows], self.sem(2, k), device)

    def add_first(self, k, rows):
        self.first(k, rows).wait_recv()
        for i in range(self.r1.shape[0]):
            for j in range(2):
                for x in range(2):
                    self.r1[i, j, x, rows] += self.g[i, j, x, self.core, rows]
        self.second(k, rows).start()

    def add_second(self, k, rows):
        self.second(k, rows).wait_recv()
        for i in range(self.n):
            for j in range(2):
                if k % 2 == 0:
                    self.r2[i, j, rows] += self.r1[i, j, self.x, rows]
                else:
                    self.r2[i, j, rows] += self.r1[i, self.c, j, rows]
        self.third(k, rows).start()

    def add_third(self, k, rows):
        self.third(k, rows).wait_recv()
        own = self.c if k % 2 == 0 else self.x
        for i in range(self.n):
            self.r3[i, rows] += self.r2[i, own, rows]

    def line(self, k, rows, d, up, first):
        buf = self.zu if up else self.zd
        src = self.r3 if first else buf
        device = {"shard": self.s + 1} if up else {"shard": self.s - 1}
        sem = self.sem(3 + (0 if up else 3) + (d - 1 if up else d), k)
        return self.copy(src.at[d, rows], buf.at[d, rows], sem, device)

    def along(self, k, rows, drain=False):
        s, n = self.s, self.n

        def send(d, up, first):
            copy = self.line(k, rows, d, up, first)
            if drain:
                copy.wait_send()
                return
            if not first:
                self.line(k, rows, d, up, first).wait_recv()
                buf = self.zu if up else self.zd
                buf[d, rows] += self.r3[d, rows]
            copy.start()

        for d in range(n - 1, 0, -1):
            e = n - 1 - d

            @pl.when(s == 0)
            def _(d=d):
                send(d, True, True)

            @pl.when(s == n - 1)
            def _(e=e):
                send(e, False, True)

        for d in range(n - 1, 0, -1):
            e = n - 1 - d

            @pl.when(jnp.logical_and(s > 0, s < d))
            def _(d=d):
                send(d, True, False)

            @pl.when(jnp.logical_and(s < n - 1, s > e))
            def _(e=e):
                send(e, False, False)

    def arrive(self, k, rows):
        s, n = self.s, self.n
        for d in range(n):
            if d > 0:

                @pl.when(s == d)
                def _(d=d):
                    self.line(k, rows, d, True, False).wait_recv()
                    self.r3[d, rows] += self.zu[d, rows]

            if d < n - 1:

                @pl.when(s == d)
                def _(d=d):
                    self.line(k, rows, d, False, False).wait_recv()
                    self.r3[d, rows] += self.zd[d, rows]

    def drain(self, k, rows):
        self.first(k, rows).wait_send()
        self.second(k, rows).wait_send()
        self.third(k, rows).wait_send()
        self.along(k, rows, drain=True)


class SmallSum:
    def __init__(self, shards, own, got, send, recv):
        self.n, self.own, self.got, self.send, self.recv = shards, own, got, send, recv
        self.s, self.c, self.t = (lax.axis_index(a) for a in ("shard", "ctx", "tp"))

    def copy(self, i):
        device = [
            {"tp": self.t + 1 - 2 * lax.rem(self.t, 2)},
            {"tp": lax.rem(self.t + 2, 4)},
            {"ctx": 1 - self.c},
            {"shard": self.s + 1},
            {"shard": self.s - 1},
        ][i]
        return pltpu.make_async_remote_copy(
            src_ref=self.own.at[i], dst_ref=self.got.at[i], send_sem=self.send.at[i],
            recv_sem=self.recv.at[i], device_id=device, device_id_type=MESH,
        )

    def start(self, value):
        self.own[0] = value
        self.copy(0).start()

    def step(self, i):
        self.copy(i).wait_recv()
        self.own[i + 1] = self.own[i] + self.got[i]
        if i < 2:
            self.copy(i + 1).start()

    def line(self, out):
        s, n = self.s, self.n
        mine = self.own[3]
        self.own[4] = mine
        out[...] = mine

        @pl.when(s > 0)
        def _():
            self.copy(3).wait_recv()
            self.own[3] = mine + self.got[3]
            out[...] += self.got[3]

        @pl.when(s < n - 1)
        def _():
            self.copy(3).start()
            self.copy(4).wait_recv()
            self.own[4] = mine + self.got[4]
            out[...] += self.got[4]

        @pl.when(s > 0)
        def _():
            self.copy(4).start()

    def drain(self):
        for i in range(3):
            self.copy(i).wait_send()

        @pl.when(self.s < self.n - 1)
        def _():
            self.copy(3).wait_send()

        @pl.when(self.s > 0)
        def _():
            self.copy(4).wait_send()


class Spread:
    def __init__(self, refs, send, recv):
        self.refs, self.send, self.recv = refs, send, recv
        self.t = lax.axis_index("tp")

    def copy(self, i, d):
        src, dst, split = self.refs[i]
        to = lax.rem(self.t + d, 4)
        if split:
            share = dst.shape[1]
            src = src.at[pl.ds(pl.multiple_of(to * share, share), share)]
        dst = dst.at[self.t]
        if d == 0:
            return pltpu.make_async_copy(src, dst, self.send.at[i, d])
        return pltpu.make_async_remote_copy(
            src_ref=src, dst_ref=dst, send_sem=self.send.at[i, d], recv_sem=self.recv.at[i, d],
            device_id={"tp": to}, device_id_type=MESH,
        )

    def start(self, i):
        for d in (1, 2, 3, 0):
            self.copy(i, d).start()

    def finish(self, i):
        for d in (1, 2, 3):
            self.copy(i, d).wait_recv()
            self.copy(i, d).wait_send()
        self.copy(i, 0).wait()


def store_owned(pk, total, outs):
    wq, wk, wv, wo, up, down, uq, uk, uv, uo, ugate = outs
    h = pk.head_rows
    for name, ref in dict(wq=wq, wk=wk, wv=wv, uq=uq, uk=uk, uv=uv).items():
        at = pk.at_heads + pk.HEADS[name] * h
        ref[...] = total(at, h)
    for name, ref in dict(uo=uo, ugate=ugate).items():
        at = pk.at_heads + pk.HEADS[name] * h
        ref[...] = total(at, h).T
    for at, r, ref in ((pk.at_wo, pk.row_rows, wo), (pk.at_up, pk.row_rows, up), (pk.at_down, pk.down_rows, down)):
        for j in range(ref.shape[1] // 128):
            ref[:, j * 128 : j * 128 + 128] = total(at + j * r, r)


def reduce_kernel(shards, pk, chunks, grads, small, y, mem, xg, mig, *refs):
    spread_outs, small_out, weight_outs = refs[:4], refs[4], refs[5:16]
    r1, r2, r3, zu, zd, own, got, send, recv, s_send, s_recv, o_send, o_recv = refs[16:]
    c = lax.axis_index("ctx")
    greet(line_peers(shards) + tp_peers() + [(c >= 0, {"ctx": 1 - c})])
    red = Reduce(shards, grads, r1, r2, r3, zu, zd, send, recv)
    rows = [pl.ds(lo, hi - lo) for lo, hi in chunks]
    n = len(rows)
    for k in range(n):
        red.first(k, rows[k]).start()
    sums = SmallSum(shards, own, got, s_send, s_recv)
    sums.start(small[...])
    spread = Spread(
        [(y, spread_outs[0], True), (mem, spread_outs[1], False), (xg, spread_outs[2], True), (mig, spread_outs[3], False)],
        o_send, o_recv,
    )
    for i in range(4):
        spread.start(i)
    for step in range(n + 4):
        if step < n:
            red.add_first(step, rows[step])
        if step < 3:
            sums.step(step)
        if 0 <= step - 1 < n:
            red.add_second(step - 1, rows[step - 1])
        if 0 <= step - 2 < n:
            red.add_third(step - 2, rows[step - 2])
            red.along(step - 2, rows[step - 2])
        if 0 <= step - 4 < n:
            red.arrive(step - 4, rows[step - 4])
    sums.line(small_out)
    s = lax.axis_index("shard")
    store_owned(pk, lambda at, size: r3[s, at : at + size, :].astype(F32), weight_outs)
    for i in range(4):
        spread.finish(i)
    sums.drain()
    for k in range(n):
        red.drain(k, rows[k])


def run_reduce(shards, pk, chunks, grads, small, y, mem, xg, mig):
    vm = pl.BlockSpec(memory_space=pltpu.VMEM)
    hbm = pl.BlockSpec(memory_space=pl.ANY)
    dma = pltpu.SemaphoreType.DMA
    shape = jax.ShapeDtypeStruct
    tokens, width = y.shape
    slots = mem.shape[0]
    h = pk.head_rows
    head, turned = shape((h, 128), F32), shape((128, h), F32)
    outs = (
        shape((4, tokens // 4, width), BF), shape((4, slots, width), F32),
        shape((4, tokens // 4, width), BF), shape((4, slots, width), F32),
        shape((8, width), F32),
        head, head, head, shape((pk.row_rows, width), F32), shape((pk.row_rows, pk.ff), F32),
        shape((pk.down_rows, width), F32), head, head, head, turned, turned,
    )
    v = pltpu.VMEM
    n = shards
    return pl.pallas_call(
        partial(reduce_kernel, shards, pk, chunks),
        out_shape=outs,
        in_specs=[vm] * 6,
        out_specs=(hbm,) * 4 + (vm,) * 12,
        scratch_shapes=[
            v((n, 2, 2, pk.rows, 128), BF), v((n, 2, pk.rows, 128), BF), v((n, pk.rows, 128), BF),
            v((n, pk.rows, 128), BF), v((n, pk.rows, 128), BF),
            v((5, 8, width), F32), v((5, 8, width), F32),
            dma((9 * len(chunks),)), dma((9 * len(chunks),)), dma((5,)), dma((5,)), dma((4, 4)), dma((4, 4)),
        ],
        compiler_params=pltpu.CompilerParams(
            vmem_limit_bytes=VMEM_LIMIT, collective_id=3, has_side_effects=True
        ),
        name="reduce",
    )(grads, small, y, mem, xg, mig)


def full_gradients(pk, grads):
    groups, owners = pk.shards * pk.ctxs, pk.shards * pk.ctxs * 4
    by_head = grads.reshape(groups, 4, pk.rows, 128)
    by_owner = grads.reshape(owners, pk.rows, 128)

    def head(name):
        at = pk.at_heads + pk.HEADS[name] * pk.head_rows
        got = by_head[:, :, at : at + pk.head_rows]
        return got.transpose(0, 2, 1, 3).reshape(pk.width, pk.width).astype(F32)

    def rows(at, h, n):
        got = by_owner[:, at : at + h * n].reshape(owners, n, h, 128)
        return got.transpose(0, 2, 1, 3).reshape(owners * h, n * 128).astype(F32)

    return (
        head("wq"), head("wk"), head("wv"),
        rows(pk.at_wo, pk.row_rows, pk.width // 128),
        rows(pk.at_up, pk.row_rows, pk.ff // 128),
        rows(pk.at_down, pk.down_rows, pk.width // 128),
        head("uq"), head("uk"), head("uv"), head("uo").T, head("ugate").T,
    )


def local(
    inputs, first_memory, piece_start, piece_len,
    w_query, w_key, w_value, w_out, w_up, w_down, u_query, u_key, u_value, u_out, u_gate,
    gain_attn, gain_ffn, gain_write, gate_bias, out_grad, memory_grad,
):
    shards, ctxs, tps = (lax.axis_size(a) for a in ("shard", "ctx", "tp"))
    s, c, t = (lax.axis_index(a) for a in ("shard", "ctx", "tp"))
    seqs, tokens, width = inputs.shape
    ff = w_up.shape[1]
    assert seqs == tps == 4 and tokens == width == 512 and ff == 2048

    def mine(array):
        return lax.dynamic_index_in_dim(array, t, 0, keepdims=False)

    weights = (w_query, w_key, w_value, w_out, w_up, w_down, u_query, u_key, u_value, u_out, u_gate)
    gathered, og = run_gather(shards, weights, out_grad)
    gains = jnp.stack([gain_attn, gain_ffn, gain_write, gate_bias] * 2)
    direct = ctxs == 2 and width % (shards * ctxs * tps * 16) == 0
    pk = Packing(shards if direct else 4, 2, width, ff)
    y, mem, xg, mig, grads, small = run_unit(
        ctxs, pk, mine(piece_start), mine(piece_len), gathered, mine(inputs), mine(first_memory),
        gains, og.reshape(tokens, width), mine(memory_grad),
    )
    every = ("shard", "ctx", "tp")
    if direct:
        bounds = [pk.rows * i // 4 // 16 * 16 for i in range(5)]
        chunks = tuple(zip(bounds[:-1], bounds[1:]))
        got = run_reduce(shards, pk, chunks, grads, small, y, mem, xg, mig)
        owner = (s * ctxs + c) * tps + t
        share = width // (shards * ctxs * tps)
        vectors = lax.dynamic_slice_in_dim(got[4][:4], owner * share, share, 1)
        return got[:4] + got[5:16] + tuple(vectors[i] for i in range(4))
    share = tokens // tps

    def rows_out(array):
        return lax.all_to_all(array.reshape(tps, share, width), "tp", 0, 0, tiled=True)

    full = full_gradients(pk, grads)
    out = [rows_out(y), lax.all_gather(mem, "tp"), rows_out(xg), lax.all_gather(mig, "tp")]
    for i, g in enumerate(full):
        if i in (3, 4, 5):
            out.append(lax.psum_scatter(g, every, scatter_dimension=0, tiled=True))
            continue
        sum_dim = 1 if i >= 9 else 0
        cut = lax.psum_scatter(g, "tp", scatter_dimension=1 - sum_dim, tiled=True)
        out.append(lax.psum_scatter(cut, ("shard", "ctx"), scatter_dimension=sum_dim, tiled=True))
    for i in range(4):
        out.append(lax.psum_scatter(small[i], every, scatter_dimension=0, tiled=True))
    return tuple(out)


def solution(mesh):
    cut = P(("shard", "tp"), None)
    head, rows, turned = P(("shard", "ctx"), "tp"), P(("shard", "ctx", "tp"), None), P("tp", ("shard", "ctx"))
    vector = P(("shard", "ctx", "tp"))
    over_rows, over_ctx = P("shard", ("ctx", "tp"), None), P("shard", "ctx", None)
    return jax.shard_map(
        local,
        mesh=mesh,
        in_specs=(over_ctx, P("shard", None, None), P("shard", "ctx"), P("shard", "ctx"))
        + (cut,) * 11 + (P(),) * 4 + (over_rows, over_ctx),
        out_specs=(over_rows, over_ctx, over_rows, over_ctx)
        + (head,) * 3 + (rows,) * 3 + (head,) * 3 + (turned,) * 2 + (vector,) * 4,
        check_vma=False,
    )
```

```python
from functools import partial

import jax
import jax.numpy as jnp
from jax import lax
from jax.experimental import pallas as pl
from jax.experimental.pallas import tpu as pltpu
from jax.sharding import PartitionSpec as P

F32 = jnp.float32
BF = jnp.bfloat16
MESH = pl.DeviceIdType.MESH
HEAD = 64
EPS = 1e-05
NEG = -1e30
VMEM_LIMIT = 67000000

WQ, WK, WV, WO, WUP, WDOWN, UQ, UK, UV, UO, UGATE = 0, 1, 2, 3, 4, 8, 12, 13, 14, 15, 16
TILES = 17


def dot(a, b):
    return lax.dot_general(a, b, (((1,), (0,)), ((), ())), preferred_element_type=F32)


def dot_nt(a, b):
    return lax.dot_general(a, b, (((1,), (1,)), ((), ())), preferred_element_type=F32)


def dot_tn(a, b):
    return lax.dot_general(a, b, (((0,), (0,)), ((), ())), preferred_element_type=F32)


def rows_at(i, size):
    return pl.ds(pl.multiple_of(i * size, size), size)


def loop(count, unroll=1):
    def run(body):
        def step(i, carry):
            body(i)
            return carry

        lax.fori_loop(0, count, step, 0, unroll=unroll)

    return run


def normed(v):
    mean = jnp.mean(v, axis=-1, keepdims=True)
    centered = v - mean
    inv = lax.rsqrt(jnp.mean(centered * centered, axis=-1, keepdims=True) + EPS)
    return centered * inv, inv


def norm_pull(e, gain, hat, inv):
    h = e * gain
    m0 = jnp.mean(h, axis=-1, keepdims=True)
    m1 = jnp.mean(h * hat, axis=-1, keepdims=True)
    return inv * (h - m0 - hat * m1)


def lane_block(width, block):
    return lax.broadcasted_iota(jnp.int32, (1, width), 1) // block


class Weights:
    def __init__(self, ref):
        self.ref = ref
        self.blocks, _, self.rows, self.width = ref.shape

    def cols(self, tile, start, size):
        got = self.ref[:, tile, :, pl.ds(start, size)]
        return got.reshape(self.blocks * self.rows, size)

    def row_part(self, tile, part, parts):
        count = self.blocks // parts
        got = self.ref[pl.ds(part * count, count), tile]
        return got.reshape(count * self.rows, self.width)

    def down_cols(self, chunk, chunks, start, size):
        count = self.blocks // chunks
        got = self.ref[pl.ds(chunk * count, count), WDOWN : WDOWN + 4, :, pl.ds(start, size)]
        return got.reshape(count * 4 * self.rows, size)

    def down_rows(self, part, parts):
        count = self.blocks // parts
        got = self.ref[pl.ds(part * count, count), WDOWN : WDOWN + 4]
        return got.reshape(count * 4 * self.rows, self.width)


def unit_scratch(tokens, slots, width, ff):
    r = tokens + slots
    heads = width // HEAD
    quads = width // 256
    v = pltpu.VMEM
    return dict(
        mem=v((slots, width), F32),
        xh=v((r, width), F32),
        xr=v((r, 1), F32),
        enc=v((r, width), BF),
        q=v((tokens, width), BF),
        k=v((r, width), BF),
        v=v((r, width), BF),
        kt=v((width, r), BF),
        vt=v((width, r), BF),
        pt=v((heads, r, tokens), BF),
        mixt=v((width, tokens), BF),
        af=v((tokens, width), F32),
        ah=v((tokens, width), F32),
        ar=v((tokens, 1), F32),
        fin=v((tokens, width), BF),
        act=v((ff // 512, tokens, 512), BF),
        dg=v((ff // 512, tokens, 512), BF),
        yh=v((tokens, width), F32),
        yr=v((tokens, 1), F32),
        wri=v((r, width), BF),
        sq=v((slots, width), BF),
        sk=v((r, width), BF),
        sv=v((r, width), BF),
        spt=v((quads, r, 256), BF),
        wrt=v((slots, width), BF),
        gate=v((slots, width), F32),
        f1=v((slots, width), F32),
        f2=v((slots, width), F32),
        gm=v((slots, width), F32),
        gup=v((slots, width), BF),
        ggl=v((slots, width), BF),
        dsq=v((slots, width), BF),
        dsk=v((r, width), BF),
        dsv=v((r, width), BF),
        e=v((r, width), F32),
        gy=v((tokens, width), F32),
        gyb=v((tokens, width), BF),
        bwm=v((slots, width), F32),
        gpre=v((ff // 512, tokens, 512), BF),
        gab=v((tokens, width), BF),
        gmx=v((tokens, width), BF),
        dst=v((2, r, tokens), BF),
        dqt=v((width, tokens), BF),
        dq=v((tokens, width), BF),
        dk=v((r, width), BF),
        dv=v((r, width), BF),
    )


class Unit:
    def __init__(self, refs, w, x, gains, small):
        self.__dict__.update(refs)
        self.w = w
        self.x = x
        self.gains = gains
        self.small = small
        self.tokens, self.width = x.shape
        self.slots = self.mem.shape[0]
        self.r = self.tokens + self.slots
        self.ff = self.act.shape[0] * 512

    def gain(self, i):
        return self.gains[i : i + 1, :]

    def make_bias(self, first, length):
        t = self.tokens

        @loop(t // 64)
        def _(i):
            key = lax.broadcasted_iota(jnp.int32, (64, t), 0) + i * 64
            query = lax.broadcasted_iota(jnp.int32, (64, t), 1)
            last = first + length
            inside = (key >= first) & (key < last) & (query >= first) & (query < last)
            seen = (key <= query) | inside
            self.e[rows_at(i, 64), :] = jnp.where(seen, 0.0, NEG).astype(F32)

    def norm_in(self, rows, values):
        hat, inv = normed(values)
        self.xh[rows, :] = hat
        self.xr[rows, :] = inv
        self.enc[rows, :] = (hat * self.gain(0)).astype(BF)

    def tokens_in(self):
        @loop(self.tokens // 32, unroll=2)
        def _(i):
            rows = rows_at(i, 32)
            self.norm_in(rows, self.x[rows, :].astype(F32))

    def project_tokens(self):
        t = self.tokens

        @loop(self.width // 256)
        def _(n):
            cols = rows_at(n, 256)
            enc = self.enc[0:t, :]
            got = dot(enc, self.w.cols(WQ, n * 256, 256)).astype(BF)
            self.q[:, cols] = got * BF(HEAD**-0.5)
            self.k[0:t, cols] = dot(enc, self.w.cols(WK, n * 256, 256)).astype(BF)
            self.v[0:t, cols] = dot(enc, self.w.cols(WV, n * 256, 256)).astype(BF)

    def memory_in(self):
        t, r = self.tokens, self.r
        self.norm_in(slice(t, r), self.mem[...])
        enc = self.enc[t:r, :]
        self.k[t:r, :] = dot(enc, self.w.cols(WK, 0, self.width)).astype(BF)
        self.v[t:r, :] = dot(enc, self.w.cols(WV, 0, self.width)).astype(BF)
        self.vt[...] = self.v[...].T

    def attend(self, first, count):
        t, r = self.tokens, self.r

        @loop(count)
        def _(i):
            p = i + first
            cols = rows_at(p, 128)
            keys = self.k[:, cols]
            half = lane_block(128, HEAD)
            for hh in range(2):
                feats = pl.ds(pl.multiple_of(p * 128 + hh * HEAD, HEAD), HEAD)
                values = self.vt[feats, :]
                for n in range(t // 256):
                    qc = slice(n * 256, n * 256 + 256)
                    q = self.q[qc, cols]
                    q = jnp.where(half == hh, q, jnp.zeros_like(q))
                    s = dot_nt(keys, q)
                    s_tok = s[0:t] + self.e[0:t, qc]
                    s_mem = s[t:r]
                    peak = jnp.maximum(
                        jnp.max(s_tok, axis=0, keepdims=True), jnp.max(s_mem, axis=0, keepdims=True)
                    )
                    e_tok = jnp.exp(s_tok - peak)
                    e_mem = jnp.exp(s_mem - peak)
                    inv = 1.0 / (
                        jnp.sum(e_tok, axis=0, keepdims=True)
                        + jnp.sum(e_mem, axis=0, keepdims=True)
                    )
                    probs = jnp.concatenate([e_tok * inv, e_mem * inv], axis=0).astype(BF)
                    self.pt[2 * p + hh, :, qc] = probs
                    self.mixt[feats, qc] = dot(values, probs).astype(BF)

    def after_attention(self):
        t = self.tokens
        self.gmx[...] = self.mixt[...].T

        @loop(self.width // 256)
        def _(n):
            cols = rows_at(n, 256)
            got = dot(self.gmx[...], self.w.cols(WO, n * 256, 256))
            self.af[:, cols] = self.x[:, cols].astype(F32) + got

        @loop(t // 32, unroll=2)
        def _(i):
            rows = rows_at(i, 32)
            hat, inv = normed(self.af[rows, :])
            self.ah[rows, :] = hat
            self.ar[rows, :] = inv
            self.fin[rows, :] = (hat * self.gain(1)).astype(BF)

    def feed_forward_up(self):
        t = self.tokens
        for j in range(self.ff // 512):

            @loop(2)
            def _(n, j=j):
                cols = rows_at(n, 256)
                weights = self.w.cols(WUP + j, n * 256, 256)
                for m in range(t // 128):
                    rows = slice(m * 128, m * 128 + 128)
                    pre = dot(self.fin[rows, :], weights)
                    c = 0.7978845608028654
                    sq = pre * pre
                    th = jnp.tanh(pre * (c + (c * 0.044715) * sq))
                    half = 0.5 + 0.5 * th
                    self.act[j, rows, cols] = (pre * half).astype(BF)
                    slope = half + (0.5 * pre) * (1.0 - th * th) * (c + (3 * c * 0.044715) * sq)
                    self.dg[j, rows, cols] = slope.astype(BF)

    def feed_forward_down(self):
        t = self.tokens

        @loop(self.width // 256)
        def _(n):
            cols = rows_at(n, 256)
            total = self.af[:, cols]
            for j in range(self.ff // 512):
                total = total + dot(
                    self.act[j], self.w.down_cols(j, self.ff // 512, n * 256, 256)
                )
            self.af[:, cols] = total

        @loop(t // 32, unroll=2)
        def _(i):
            rows = rows_at(i, 32)
            hat, inv = normed(self.af[rows, :])
            self.yh[rows, :] = hat
            self.yr[rows, :] = inv
            self.wri[rows, :] = (hat * self.gain(2)).astype(BF)

        self.wri[t : self.r, :] = (self.xh[t : self.r, :] * self.gain(2)).astype(BF)

    def spread_heads(self, rows, g):
        part = rows[:, g * 256 : g * 256 + 256]
        block = lane_block(256, HEAD)
        return jnp.concatenate(
            [jnp.where(block == h, part, jnp.zeros_like(part)) for h in range(4)], axis=0
        )

    def gather_heads(self, stacked):
        block = lane_block(256, HEAD)
        s = self.slots
        total = jnp.where(block == 0, stacked[0:s], 0.0)
        for h in range(1, 4):
            total = total + jnp.where(block == h, stacked[h * s : h * s + s], 0.0)
        return total

    def write_memory(self):
        t, r = self.tokens, self.r

        @loop(self.width // 256)
        def _(n):
            cols = rows_at(n, 256)
            wri = self.wri[...]
            self.sk[:, cols] = dot(wri, self.w.cols(UK, n * 256, 256)).astype(BF)
            self.sv[:, cols] = dot(wri, self.w.cols(UV, n * 256, 256)).astype(BF)

        wm = self.wri[t:r, :]
        sq = dot(wm, self.w.cols(UQ, 0, self.width)).astype(BF)
        self.sq[...] = sq * BF(HEAD**-0.5)
        for g in range(self.width // 256):
            cols = slice(g * 256, g * 256 + 256)
            s = dot_nt(self.sk[:, cols], self.spread_heads(self.sq[...], g))
            e = jnp.exp(s - jnp.max(s, axis=0, keepdims=True))
            probs = (e * (1.0 / jnp.sum(e, axis=0, keepdims=True))).astype(BF)
            self.spt[g] = probs
            self.wrt[:, cols] = self.gather_heads(dot_tn(probs, self.sv[:, cols])).astype(BF)
        th = jnp.tanh(dot(self.wrt[...], self.w.cols(UO, 0, self.width)))
        pre = dot(wm, self.w.cols(UGATE, 0, self.width))
        gate = jax.nn.sigmoid(pre + self.gain(3))
        mem = self.mem[...]
        self.gate[...] = gate
        self.f1[...] = (mem - th) * gate * (1.0 - gate)
        self.f2[...] = (1.0 - gate) * (1.0 - th * th)
        return gate * mem + (1.0 - gate) * th

    def backward_early(self):
        self.kt[...] = self.k[...].T

    def write_back(self, out_grad):
        t, r, s = self.tokens, self.r, self.slots
        gm = self.gm[...]
        ggp = gm * self.f1[...]
        gup = (gm * self.f2[...]).astype(BF)
        ggl = ggp.astype(BF)
        self.gup[...] = gup
        self.ggl[...] = ggl
        self.small[3:4, :] = jnp.sum(ggp, axis=0, keepdims=True)
        gwr = dot_nt(gup, self.w.row_part(UO, 0, 1)).astype(BF)
        for g in range(self.width // 256):
            cols = slice(g * 256, g * 256 + 256)
            grads = self.spread_heads(gwr, g)
            dp = dot_nt(self.sv[:, cols], grads)
            probs = self.spt[g]
            pf = probs.astype(F32)
            ds = (pf * (dp - jnp.sum(pf * dp, axis=0, keepdims=True))).astype(BF)
            self.dsv[:, cols] = dot(probs, grads).astype(BF)
            self.dsk[:, cols] = dot(ds, self.spread_heads(self.sq[...], g)).astype(BF)
            dq = self.gather_heads(dot_tn(ds, self.sk[:, cols])) * HEAD**-0.5
            self.dsq[:, cols] = dq.astype(BF)

        @loop(2)
        def _(n):
            cols = rows_at(n, self.width // 2)
            self.e[:, cols] = dot_nt(self.dsk[...], self.w.row_part(UK, n, 2)) + dot_nt(
                self.dsv[...], self.w.row_part(UV, n, 2)
            )

        em = self.e[t:r, :] + dot_nt(self.dsq[...], self.w.row_part(UQ, 0, 1))
        em = em + dot_nt(ggl, self.w.row_part(UGATE, 0, 1))
        hat = self.xh[t:r, :]
        self.bwm[...] = norm_pull(em, self.gain(2), hat, self.xr[t:r, :])
        self.small[2:3, :] = jnp.sum(em * hat, axis=0, keepdims=True)

        @loop(t // 32, unroll=2)
        def _(i):
            rows = rows_at(i, 32)
            e = self.e[rows, :]
            hat = self.yh[rows, :]
            self.small[2:3, :] += jnp.sum(e * hat, axis=0, keepdims=True)
            grad = out_grad(i) + norm_pull(e, self.gain(2), hat, self.yr[rows, :])
            self.gy[rows, :] = grad
            self.gyb[rows, :] = grad.astype(BF)

    def feed_forward_back(self):
        t = self.tokens
        chunks = self.ff // 512

        for j in range(chunks):

            @loop(2)
            def _(n, j=j):
                cols = rows_at(n, 256)
                weights = self.w.down_rows(2 * j + n, 2 * chunks)
                for m in range(t // 128):
                    rows = slice(m * 128, m * 128 + 128)
                    got = dot_nt(self.gyb[rows, :], weights)
                    self.gpre[j, rows, cols] = (got * self.dg[j, rows, cols].astype(F32)).astype(BF)

        @loop(2)
        def _(n):
            cols = rows_at(n, self.width // 2)
            total = dot_nt(self.gpre[0], self.w.row_part(WUP, n, 2))
            for j in range(1, chunks):
                total = total + dot_nt(self.gpre[j], self.w.row_part(WUP + j, n, 2))
            self.e[0:t, cols] = total

        self.small[1:2, :] = jnp.zeros((1, self.width), F32)

        @loop(t // 32, unroll=2)
        def _(i):
            rows = rows_at(i, 32)
            e = self.e[rows, :]
            hat = self.ah[rows, :]
            self.small[1:2, :] += jnp.sum(e * hat, axis=0, keepdims=True)
            grad = self.gy[rows, :] + norm_pull(e, self.gain(1), hat, self.ar[rows, :])
            self.gy[rows, :] = grad
            self.gab[rows, :] = grad.astype(BF)

    def project_back(self):
        @loop(2)
        def _(n):
            cols = rows_at(n, self.width // 2)
            self.gmx[:, cols] = dot_nt(self.gab[...], self.w.row_part(WO, n, 2)).astype(BF)

    def attend_back(self, first, count):
        t, r = self.tokens, self.r

        @loop(count)
        def _(i):
            p = i + first
            cols = rows_at(p, 128)
            values = self.v[:, cols]
            half = lane_block(128, HEAD)
            for hh in range(2):
                feats = pl.ds(pl.multiple_of(p * 128 + hh * HEAD, HEAD), HEAD)
                keys = self.kt[feats, :]
                for n in range(t // 256):
                    qc = slice(n * 256, n * 256 + 256)
                    g = self.gmx[qc, cols]
                    g = jnp.where(half == hh, g, jnp.zeros_like(g))
                    dp = dot_nt(values, g)
                    pf = self.pt[2 * p + hh, :, qc].astype(F32)
                    ds = (pf * (dp - jnp.sum(pf * dp, axis=0, keepdims=True))).astype(BF)
                    self.dst[hh, :, qc] = ds
                    self.dqt[feats, qc] = (dot(keys, ds) * HEAD**-0.5).astype(BF)
            g = self.gmx[:, cols]
            q = self.q[:, cols]
            dv = jnp.where(half == 0, dot(self.pt[2 * p], g), dot(self.pt[2 * p + 1], g))
            self.dv[:, cols] = dv.astype(BF)
            dk = jnp.where(half == 0, dot(self.dst[0], q), dot(self.dst[1], q))
            self.dk[:, cols] = dk.astype(BF)

    def enter_back(self, input_grad):
        t, r = self.tokens, self.r
        self.dq[...] = self.dqt[...].T

        @loop(2)
        def _(n):
            cols = rows_at(n, self.width // 2)
            self.e[:, cols] = dot_nt(self.dk[...], self.w.row_part(WK, n, 2)) + dot_nt(
                self.dv[...], self.w.row_part(WV, n, 2)
            )
            self.e[0:t, cols] += dot_nt(self.dq[...], self.w.row_part(WQ, n, 2))

        e = self.e[t:r, :]
        hat = self.xh[t:r, :]
        self.small[0:1, :] = jnp.sum(e * hat, axis=0, keepdims=True)
        mem_grad = self.gm[...] * self.gate[...] + self.bwm[...]
        mem_grad = mem_grad + norm_pull(e, self.gain(0), hat, self.xr[t:r, :])

        @loop(t // 32, unroll=2)
        def _(i):
            rows = rows_at(i, 32)
            e = self.e[rows, :]
            hat = self.xh[rows, :]
            self.small[0:1, :] += jnp.sum(e * hat, axis=0, keepdims=True)
            grad = self.gy[rows, :] + norm_pull(e, self.gain(0), hat, self.xr[rows, :])
            input_grad[rows, :] = grad.astype(BF)

        return mem_grad


class Packing:
    def __init__(self, shards, ctxs, width, ff):
        self.shards, self.ctxs, self.width, self.ff = shards, ctxs, width, ff
        self.head_rows = h = width // (shards * ctxs)
        self.row_rows = width // (shards * ctxs * 4)
        self.down_rows = ff // (shards * ctxs * 4)
        self.heads = dict(uq=0, uk=h, uv=2 * h, uo=3 * h, ugate=4 * h)
        self.at_down = 5 * h
        self.at_up = self.at_down + self.down_rows * (width // 128)
        self.at_wo = self.at_up + self.row_rows * (ff // 128)
        at = self.at_wo + self.row_rows * (width // 128)
        self.heads.update(wq=at, wk=at + h, wv=at + 2 * h)
        self.rows = at + 3 * h
        bounds = (0, self.at_down, self.at_up, self.at_wo, at + h, self.rows)
        self.chunks = tuple(zip(bounds[:-1], bounds[1:]))

    @property
    def shape(self):
        return (self.shards, self.ctxs, 2, 2, self.rows, 128)


def weight_grads(u, g, pk, names):
    width = u.width
    tile = 256

    def store_head(at, m, got):
        h = pk.head_rows
        per = tile // h
        for i in range(per):
            s = m * (per // pk.ctxs) + i // pk.ctxs
            for t in range(4):
                g[s, i % pk.ctxs, t // 2, t % 2, at : at + h, :] = got[
                    i * h : i * h + h, t * 128 : t * 128 + 128
                ]

    def store_rows(at, h, m, got, chunk0):
        per = tile // h
        for i in range(per):
            if per % (pk.ctxs * 4) == 0:
                s, c = m * (per // (pk.ctxs * 4)) + i // (pk.ctxs * 4), (i // 4) % pk.ctxs
            else:
                owner = m * (per // 4) + i // 4
                s, c = lax.div(owner, pk.ctxs), lax.rem(owner, pk.ctxs)
            for j in range(got.shape[1] // 128):
                lo = at + (chunk0 + j) * h
                g[s, c, (i // 2) % 2, i % 2, lo : lo + h, :] = got[
                    i * h : i * h + h, j * 128 : j * 128 + 128
                ]

    def head(name, left, right):
        at = pk.heads[name]

        @loop(width // tile)
        def _(m):
            lt = left[:, rows_at(m, tile)].T
            store_head(at, m, dot(lt, right[...]).astype(BF))

    t, r = u.tokens, u.r
    if "down" in names:
        for j in range(u.ff // 512):

            @loop(512 // tile)
            def _(m, j=j):
                lt = u.act[j, :, rows_at(m, tile)].T
                got = dot(lt, u.gyb[...]).astype(BF)
                store_rows(pk.at_down, pk.down_rows, m + j * (512 // tile), got, 0)

    if "up" in names:

        @loop(width // tile)
        def _(m):
            lt = u.fin[:, rows_at(m, tile)].T
            for j in range(u.ff // 512):
                store_rows(pk.at_up, pk.row_rows, m, dot(lt, u.gpre[j]).astype(BF), 4 * j)

    if "wo" in names:

        @loop(width // tile)
        def _(m):
            got = dot(u.mixt[rows_at(m, tile), :], u.gab[...]).astype(BF)
            store_rows(pk.at_wo, pk.row_rows, m, got, 0)

    if "write" in names:
        head("uq", u.wri.at[t:r], u.dsq)
        head("uk", u.wri, u.dsk)
        head("uv", u.wri, u.dsv)
        head("uo", u.gup, u.wrt)
        head("ugate", u.ggl, u.wri.at[t:r])
    if "wq" in names:
        head("wq", u.enc.at[0:t], u.dq)
    if "wkv" in names:
        head("wk", u.enc, u.dk)
        head("wv", u.enc, u.dv)


GROUPS = ((0, 3), (3, 8), (8, 12), (12, 17))


def greet(peers):
    barrier = pltpu.get_barrier_semaphore()
    count = 0
    for cond, device in peers:

        @pl.when(cond)
        def _(device=device):
            pl.semaphore_signal(barrier, inc=1, device_id=device, device_id_type=MESH)

        count = count + jnp.where(cond, 1, 0)
    pl.semaphore_wait(barrier, count)


class Gather:
    UP, DOWN, PAIR, ACROSS, PAIR_ACROSS, BESIDE, PAIR_BESIDE, FAR, PAIR_FAR = range(9)

    def __init__(self, shards, halved, w, send, recv):
        self.n, self.halved, self.w, self.send, self.recv = shards, halved, w, send, recv
        self.s, self.c, self.t = (lax.axis_index(a) for a in ("shard", "ctx", "tp"))
        odd = lax.rem(self.t, 2)
        self.pair_tp = self.t + 1 - 2 * odd
        self.across_tp = lax.rem(self.t + 2, 4)
        self.pair = {"tp": self.pair_tp}
        self.across = {"tp": self.across_tp}
        self.beside = {"ctx": self.c + 1 - 2 * lax.rem(self.c, 2)}

    def copy(self, kind, source, tp, g, device, half=None):
        lo, hi = GROUPS[g]
        block = self.w.at[source * 4 + tp, lo:hi]
        if half is not None:
            size = self.w.shape[2] // 2
            block = self.w.at[source * 4 + tp, lo:hi, pl.ds(pl.multiple_of(half * size, size), size)]
        return pltpu.make_async_remote_copy(
            src_ref=block, dst_ref=block, send_sem=self.send.at[kind, source, g],
            recv_sem=self.recv.at[kind, source, g], device_id=device, device_id_type=MESH,
        )

    @property
    def mine(self):
        return self.c if self.halved else None

    @property
    def others(self):
        return 1 - self.c

    def up(self, source, g, far):
        return self.copy(self.UP, source, self.t, g, {"shard": self.s + 1}, self.mine if far else None)

    def down(self, source, g, far):
        return self.copy(self.DOWN, source, self.t, g, {"shard": self.s - 1}, self.mine if far else None)

    def to_across(self, source, g, tp=None):
        return self.copy(self.ACROSS, source, self.t if tp is None else tp, g, self.across, self.mine)

    def to_pair(self, source, g, far, tp=None):
        return self.copy(self.PAIR, source, self.t if tp is None else tp, g, self.pair, self.mine if far else None)

    def far(self, d):
        return self.halved and d == self.n - 1

    def start_own(self, g):
        s, n = self.s, self.n
        if n > 1:

            @pl.when(s < n - 1)
            def _():
                self.up(s, g, self.far(1)).start()

            @pl.when(s > 0)
            def _():
                self.down(s, g, self.far(1)).start()

        self.to_across(s, g).start()
        self.to_pair(s, g, False).start()

    def came(self, source, g, d):
        self.to_across(source, g).start()
        self.to_pair(source, g, self.far(d)).start()
        if self.far(d):
            self.copy(self.FAR, source, self.t, g, self.beside, self.c).start()

    def line_step(self, d, g):
        s, n = self.s, self.n

        @pl.when(s - d >= 0)
        def _():
            self.up(s - d, g, self.far(d)).wait_recv()

            @pl.when(s < n - 1)
            def _():
                self.up(s - d, g, self.far(d + 1)).start()

            self.came(s - d, g, d)

        @pl.when(s + d <= n - 1)
        def _():
            self.down(s + d, g, self.far(d)).wait_recv()

            @pl.when(s > 0)
            def _():
                self.down(s + d, g, self.far(d + 1)).start()

            self.came(s + d, g, d)

    def sources(self, d):
        s, n = self.s, self.n
        both = ((s - d, s - d >= 0), (s + d, s + d <= n - 1))
        return both[:1] if d == 0 else both

    def across_step(self, d, g):
        for source, cond in self.sources(d):

            @pl.when(cond)
            def _(source=source):
                tp = self.across_tp
                self.to_across(source, g, tp).wait_recv()
                self.copy(self.PAIR_ACROSS, source, tp, g, self.pair, self.mine).start()
                if self.halved:
                    self.copy(self.BESIDE, source, tp, g, self.beside, self.c).start()

    def beside_step(self, d, g):
        if not self.halved:
            return
        for source, cond in self.sources(d):

            @pl.when(cond)
            def _(source=source):
                tp = self.across_tp
                self.copy(self.BESIDE, source, tp, g, self.beside, self.others).wait_recv()
                self.copy(self.PAIR_BESIDE, source, tp, g, self.pair, self.others).start()

    def far_step(self, g):
        if not self.halved:
            return
        for source, cond in self.sources(self.n - 1):

            @pl.when(cond)
            def _(source=source):
                self.copy(self.FAR, source, self.t, g, self.beside, self.others).wait_recv()
                self.copy(self.PAIR_FAR, source, self.t, g, self.pair, self.others).start()

    def finish(self, g, own=False):
        tp = self.t if own else self.pair_tp
        other = self.across_tp if own else lax.rem(self.pair_tp + 2, 4)
        for d in range(self.n):
            for source, cond in self.sources(d):

                @pl.when(cond)
                def _(source=source, d=d):
                    copies = [
                        self.to_pair(source, g, self.far(d), tp),
                        self.copy(self.PAIR_ACROSS, source, other, g, self.pair, self.mine),
                    ]
                    if self.halved:
                        copies.append(self.copy(self.PAIR_BESIDE, source, other, g, self.pair, self.others))
                    if self.far(d):
                        copies.append(self.copy(self.PAIR_FAR, source, tp, g, self.pair, self.others))
                    if own:
                        copies.append(self.to_across(source, g))
                        if self.halved:
                            copies.append(self.copy(self.BESIDE, source, other, g, self.beside, self.c))
                        if self.far(d):
                            copies.append(self.copy(self.FAR, source, tp, g, self.beside, self.c))
                    for copy in copies:
                        if own:
                            copy.wait_send()
                        else:
                            copy.wait_recv()

    def drain(self, g):
        s, n = self.s, self.n
        self.finish(g, own=True)
        for d in range(n - 1):

            @pl.when(jnp.logical_and(s - d >= 0, s < n - 1))
            def _(d=d):
                self.up(s - d, g, self.far(d + 1)).wait_send()

            @pl.when(jnp.logical_and(s + d <= n - 1, s > 0))
            def _(d=d):
                self.down(s + d, g, self.far(d + 1)).wait_send()

    def events(self, time, ready):
        n = self.n
        groups = range(len(GROUPS))
        for g in groups:
            if time == max(2 * g - 2, 0):
                ready(g)
                self.start_own(g)
        for g in groups:
            d = time - 2 * g
            if 1 <= d <= n - 1:
                self.line_step(d, g)
            if 0 <= d - 1 <= n - 1:
                self.across_step(d - 1, g)
            if 0 <= d - 2 <= n - 1:
                self.beside_step(d - 2, g)
            if d == n + 1:
                self.far_step(g)
                self.finish(g)

    @property
    def last(self):
        return 2 * (len(GROUPS) - 1) + self.n + 1


def line_peers(n):
    s = lax.axis_index("shard")
    return [(s > 0, {"shard": s - 1}), (s < n - 1, {"shard": s + 1})] if n > 1 else []


def tp_peers():
    t = lax.axis_index("tp")
    return [(t >= 0, {"tp": lax.rem(t + d, 4)}) for d in (1, 2, 3)]


def own_tiles(weights, w, own, sems):
    names = [WQ, WK, WV, WO, WUP, WDOWN, UQ, UK, UV, UO, UGATE]
    rows = w.shape[2]
    out = []
    for name, ref in zip(names, weights):
        parts = {WUP: 4, WDOWN: 4}.get(name, 1)
        for j in range(parts):
            src = ref
            if name == WUP:
                src = ref.at[:, j * 512 : j * 512 + 512]
            if name == WDOWN:
                src = ref.at[j * rows : j * rows + rows]
            out.append(pltpu.make_async_copy(src, w.at[own, name + j], sems.at[name + j]))
    return out


class Reduce:
    ORDER = (0, 0, 1, 0, 1)

    def __init__(self, shards, g, r1, r2, r3, zu, zd, send, recv):
        self.n = shards
        self.g, self.r1, self.r2, self.r3, self.zu, self.zd = g, r1, r2, r3, zu, zd
        self.send, self.recv = send, recv
        self.s, self.c, self.t = (lax.axis_index(a) for a in ("shard", "ctx", "tp"))
        self.core = lax.rem(self.t, 2)
        self.x = lax.div(self.t, 2)
        self.partner = {"tp": self.t + 1 - 2 * self.core}
        self.across = {"tp": lax.rem(self.t + 2, 4)}
        self.beside = {"ctx": 1 - self.c}

    def copy(self, src, dst, sem, device):
        return pltpu.make_async_remote_copy(
            src_ref=src, dst_ref=dst, send_sem=self.send.at[sem], recv_sem=self.recv.at[sem],
            device_id=device, device_id_type=MESH,
        )

    def sem(self, kind, chunk):
        return chunk * 9 + kind

    def first(self, k, rows):
        src = self.g.at[:, :, :, 1 - self.core, rows]
        return self.copy(src, self.r1.at[:, :, :, rows], self.sem(0, k), self.partner)

    def second(self, k, rows):
        if self.ORDER[k] == 0:
            src, device = self.r1.at[:, :, 1 - self.x, rows], self.across
        else:
            src, device = self.r1.at[:, 1 - self.c, :, rows], self.beside
        return self.copy(src, self.r2.at[:, :, rows], self.sem(1, k), device)

    def third(self, k, rows):
        if self.ORDER[k] == 0:
            src, device = self.r2.at[:, 1 - self.c, rows], self.beside
        else:
            src, device = self.r2.at[:, 1 - self.x, rows], self.across
        return self.copy(src, self.r3.at[:, rows], self.sem(2, k), device)

    def add_first(self, k, rows):
        self.first(k, rows).wait_recv()
        for i in range(self.r1.shape[0]):
            for j in range(2):
                for x in range(2):
                    self.r1[i, j, x, rows] += self.g[i, j, x, self.core, rows]
        self.second(k, rows).start()

    def add_second(self, k, rows):
        self.second(k, rows).wait_recv()
        for i in range(self.n):
            for j in range(2):
                if self.ORDER[k] == 0:
                    self.r2[i, j, rows] += self.r1[i, j, self.x, rows]
                else:
                    self.r2[i, j, rows] += self.r1[i, self.c, j, rows]
        self.third(k, rows).start()

    def add_third(self, k, rows):
        self.third(k, rows).wait_recv()
        own = self.c if self.ORDER[k] == 0 else self.x
        for i in range(self.n):
            self.r3[i, rows] += self.r2[i, own, rows]

    def line(self, k, rows, d, up, first):
        buf = self.zu if up else self.zd
        src = self.r3 if first else buf
        device = {"shard": self.s + 1} if up else {"shard": self.s - 1}
        sem = self.sem(3 + (0 if up else 3) + (d - 1 if up else d), k)
        return self.copy(src.at[d, rows], buf.at[d, rows], sem, device)

    def along(self, k, rows, drain=False):
        s, n = self.s, self.n

        def send(d, up, first):
            copy = self.line(k, rows, d, up, first)
            if drain:
                copy.wait_send()
                return
            if not first:
                self.line(k, rows, d, up, first).wait_recv()
                buf = self.zu if up else self.zd
                buf[d, rows] += self.r3[d, rows]
            copy.start()

        for d in range(n - 1, 0, -1):
            e = n - 1 - d

            @pl.when(s == 0)
            def _(d=d):
                send(d, True, True)

            @pl.when(s == n - 1)
            def _(e=e):
                send(e, False, True)

        for d in range(n - 1, 0, -1):
            e = n - 1 - d

            @pl.when(jnp.logical_and(s > 0, s < d))
            def _(d=d):
                send(d, True, False)

            @pl.when(jnp.logical_and(s < n - 1, s > e))
            def _(e=e):
                send(e, False, False)

    def arrive(self, k, rows):
        s, n = self.s, self.n
        for d in range(n):
            if d > 0:

                @pl.when(s == d)
                def _(d=d):
                    self.line(k, rows, d, True, False).wait_recv()
                    self.r3[d, rows] += self.zu[d, rows]

            if d < n - 1:

                @pl.when(s == d)
                def _(d=d):
                    self.line(k, rows, d, False, False).wait_recv()
                    self.r3[d, rows] += self.zd[d, rows]

    def drain(self, k, rows):
        self.first(k, rows).wait_send()
        self.second(k, rows).wait_send()
        self.third(k, rows).wait_send()
        self.along(k, rows, drain=True)


class SmallSum:
    def __init__(self, shards, own, got, send, recv):
        self.n, self.own, self.got, self.send, self.recv = shards, own, got, send, recv
        self.s, self.c, self.t = (lax.axis_index(a) for a in ("shard", "ctx", "tp"))

    def copy(self, i):
        device = [
            {"tp": self.t + 1 - 2 * lax.rem(self.t, 2)},
            {"tp": lax.rem(self.t + 2, 4)},
            {"ctx": 1 - self.c},
            {"shard": self.s + 1},
            {"shard": self.s - 1},
        ][i]
        return pltpu.make_async_remote_copy(
            src_ref=self.own.at[i], dst_ref=self.got.at[i], send_sem=self.send.at[i],
            recv_sem=self.recv.at[i], device_id=device, device_id_type=MESH,
        )

    def start(self, value):
        self.own[0] = value
        self.copy(0).start()

    def step(self, i):
        self.copy(i).wait_recv()
        self.own[i + 1] = self.own[i] + self.got[i]
        if i < 2:
            self.copy(i + 1).start()

    def line(self, out):
        s, n = self.s, self.n
        mine = self.own[3]
        self.own[4] = mine
        out[...] = mine

        @pl.when(s > 0)
        def _():
            self.copy(3).wait_recv()
            self.own[3] = mine + self.got[3]
            out[...] += self.got[3]

        @pl.when(s < n - 1)
        def _():
            self.copy(3).start()
            self.copy(4).wait_recv()
            self.own[4] = mine + self.got[4]
            out[...] += self.got[4]

        @pl.when(s > 0)
        def _():
            self.copy(4).start()

    def drain(self):
        for i in range(3):
            self.copy(i).wait_send()

        @pl.when(self.s < self.n - 1)
        def _():
            self.copy(3).wait_send()

        @pl.when(self.s > 0)
        def _():
            self.copy(4).wait_send()


class Spread:
    def __init__(self, refs, send, recv):
        self.refs, self.send, self.recv = refs, send, recv
        self.t = lax.axis_index("tp")

    def copy(self, i, d):
        src, dst, split = self.refs[i]
        to = lax.rem(self.t + d, 4)
        if split:
            share = dst.shape[1]
            src = src.at[pl.ds(pl.multiple_of(to * share, share), share)]
        dst = dst.at[self.t]
        if d == 0:
            return pltpu.make_async_copy(src, dst, self.send.at[i, d])
        return pltpu.make_async_remote_copy(
            src_ref=src, dst_ref=dst, send_sem=self.send.at[i, d], recv_sem=self.recv.at[i, d],
            device_id={"tp": to}, device_id_type=MESH,
        )

    def start(self, i):
        for d in (1, 2, 3, 0):
            self.copy(i, d).start()

    def finish(self, i):
        for d in (1, 2, 3):
            self.copy(i, d).wait_recv()
            self.copy(i, d).wait_send()
        self.copy(i, 0).wait()


class Comm:
    pass


def step_scratch(shards, pk, direct, tokens, slots, width):
    v, dma = pltpu.VMEM, pltpu.SemaphoreType.DMA
    n = shards
    out = dict(
        w=v((n * 4, TILES, width // (n * 4), width), BF),
        x=v((tokens, width), BF),
        m0=v((slots, width), F32),
        og=v((4, tokens // 4, width), BF),
        y=v((tokens, width), BF),
        xg=v((tokens, width), BF),
        mem_out=v((slots, width), F32),
        mig=v((slots, width), F32),
        small=v((8, width), F32),
        m_send=v((slots, width), BF),
        m_recv=v((slots, width), BF),
        g_send=v((slots, width), BF),
        g_recv=v((slots, width), BF),
        chain=dma((4,)),
        loads=dma((3,)),
        local=dma((TILES,)),
        w_send=dma((9, n, len(GROUPS))),
        w_recv=dma((9, n, len(GROUPS))),
        og_send=dma((4,)),
        og_recv=dma((4,)),
        o_send=dma((4, 4)),
        o_recv=dma((4, 4)),
    )
    if direct:
        c = len(pk.chunks)
        out.update(
            g=v(pk.shape, BF),
            r1=v((n, 2, 2, pk.rows, 128), BF),
            r2=v((n, 2, pk.rows, 128), BF),
            r3=v((n, pk.rows, 128), BF),
            zu=v((n, pk.rows, 128), BF),
            zd=v((n, pk.rows, 128), BF),
            own=v((5, 8, width), F32),
            got=v((5, 8, width), F32),
            r_send=dma((9 * c,)),
            r_recv=dma((9 * c,)),
            s_send=dma((5,)),
            s_recv=dma((5,)),
        )
    return out


def step_kernel(dims, pk, direct, names, unit_names, *refs):
    shards, ctxs, halved = dims
    first, length, inputs, first_memory, memory_grad, out_grad = refs[:6]
    weights, gains, outs = refs[6:17], refs[17], refs[18:24]
    scratch = refs[24:]
    b = Comm()
    b.__dict__.update(zip(names, scratch))
    unit_refs = dict(zip(unit_names, scratch[len(names) :]))
    if not direct:
        b.g = outs[4]
    s, c, t = (lax.axis_index(a) for a in ("shard", "ctx", "tp"))
    u = Unit(unit_refs, Weights(b.w), b.x, gains, b.small)

    loads = [
        pltpu.make_async_copy(inputs.at[t], b.x, b.loads.at[0]),
        pltpu.make_async_copy(first_memory.at[t], b.m0, b.loads.at[1]),
        pltpu.make_async_copy(memory_grad.at[t], u.gm, b.loads.at[2]),
    ]
    copies = own_tiles(weights, b.w, s * 4 + t, b.local)
    for copy in copies + loads:
        copy.start()
    mine = pltpu.make_async_copy(out_grad.at[t], b.og.at[t], b.og_send.at[0])
    mine.start()
    peers = line_peers(shards) + tp_peers()
    if ctxs > 1:
        peers += [(c > 0, {"ctx": c - 1}), (c < ctxs - 1, {"ctx": c + 1})]
    greet(peers)
    gather = Gather(shards, halved, b.w, b.w_send, b.w_recv)

    def ready(g):
        for copy in copies[GROUPS[g][0] : GROUPS[g][1]]:
            copy.wait()

    def gather_until(start, stop):
        for time in range(start, stop):
            gather.events(time, ready)

    def chain_copy(i, to):
        src, dst = ((b.m_send, b.m_recv), (b.g_send, b.g_recv))[i]
        return pltpu.make_async_remote_copy(
            src_ref=src, dst_ref=dst, send_sem=b.chain.at[2 * i], recv_sem=b.chain.at[2 * i + 1],
            device_id={"ctx": to}, device_id_type=MESH,
        )

    def og_copy(d):
        to = lax.rem(t + d, 4)
        return pltpu.make_async_remote_copy(
            src_ref=out_grad.at[to], dst_ref=b.og.at[t], send_sem=b.og_send.at[d],
            recv_sem=b.og_recv.at[d], device_id={"tp": to}, device_id_type=MESH,
        )

    spread = Spread(
        [(b.y, outs[0], True), (b.mem_out, outs[1], False), (b.xg, outs[2], True), (b.mig, outs[3], False)],
        b.o_send, b.o_recv,
    )
    lead, follow = pl.when(c == 0), pl.when(c > 0)
    pairs = u.width // 128

    gather_until(0, 1)
    for copy in loads:
        copy.wait()
    u.make_bias(first[t, 0], length[t, 0])
    gather_until(1, 2)
    u.tokens_in()
    at_first = shards + 2
    gather_until(2, at_first)
    u.project_tokens()

    @lead
    def _():
        u.mem[...] = b.m0[...]
        u.memory_in()
        u.attend(0, pairs // 2)

    gather_until(at_first, at_first + 1)

    @lead
    def _():
        u.attend(pairs // 2, pairs - pairs // 2)

    gather_until(at_first + 1, at_first + 2)

    @lead
    def _():
        u.after_attention()
        u.feed_forward_up()

    gather_until(at_first + 2, at_first + 4)

    @lead
    def _():
        u.feed_forward_down()

    gather_until(at_first + 4, gather.last + 1)
    for d in (1, 2, 3):
        og_copy(d).start()

    if ctxs > 1:

        @follow
        def _():
            chain_copy(0, c - 1).wait_recv()
            u.mem[...] = b.m_recv[...].astype(F32)
            u.memory_in()
            u.attend(0, pairs)
            u.after_attention()
            u.feed_forward_up()
            u.feed_forward_down()

    after = u.write_memory()
    b.mem_out[...] = after
    b.y[...] = u.af[...].astype(BF)
    if ctxs > 1:
        b.m_send[...] = after.astype(BF)

        @pl.when(c < ctxs - 1)
        def _():
            chain_copy(0, c + 1).start()

    spread.start(0)
    spread.start(1)
    u.backward_early()
    mine.wait()
    for d in (1, 2, 3):
        og_copy(d).wait_recv()

    if ctxs > 1:

        @pl.when(c < ctxs - 1)
        def _():
            chain_copy(1, c + 1).wait_recv()
            u.gm[...] += b.g_recv[...].astype(F32)

    def out_grad_rows(i):
        per = b.og.shape[1] // 32
        return b.og[lax.div(i, per), pl.ds(lax.rem(i, per) * 32, 32), :].astype(F32)

    def grads(*which):
        weight_grads(u, b.g, pk, which)

    if direct:
        red = Reduce(shards, b.g, b.r1, b.r2, b.r3, b.zu, b.zd, b.r_send, b.r_recv)
        rows = [pl.ds(lo, hi - lo) for lo, hi in pk.chunks]
        sums = SmallSum(shards, b.own, b.got, b.s_send, b.s_recv)

    def reduce(*todo):
        if direct:
            for what, k in todo:
                if what == "first":
                    red.first(k, rows[k]).start()
                else:
                    getattr(red, what)(k, rows[k])

    A, DOWN, UP, C0, C1 = range(5)
    u.write_back(out_grad_rows)

    @lead
    def _():
        grads("write")
        reduce(("first", A))

    u.feed_forward_back()

    @lead
    def _():
        reduce(("add_first", A))
        grads("down")
        reduce(("first", DOWN))
        grads("up")
        reduce(("first", UP))

    u.project_back()

    @lead
    def _():
        reduce(("add_first", DOWN), ("add_second", A))

    u.attend_back(0, pairs // 2)

    @lead
    def _():
        reduce(("add_first", UP), ("add_second", DOWN))

    u.attend_back(pairs // 2, pairs - pairs // 2)

    @lead
    def _():
        reduce(("add_third", A), ("along", A), ("add_second", UP))

    back = u.enter_back(b.xg)
    b.mig[...] = back

    if ctxs > 1:

        @follow
        def _():
            b.g_send[...] = back.astype(BF)
            chain_copy(1, c - 1).start()
            grads("write")
            reduce(("first", A))
            grads("down")
            reduce(("first", DOWN))
            grads("up")
            reduce(("first", UP))

    grads("wo", "wq")
    reduce(("first", C0))
    grads("wkv")
    reduce(("first", C1))
    spread.start(2)
    spread.start(3)
    if direct:
        sums.start(b.small[...])

    @lead
    def _():
        reduce(("add_third", DOWN), ("along", DOWN), ("add_third", UP), ("along", UP), ("arrive", A))
        reduce(("add_first", C0), ("add_first", C1), ("arrive", DOWN), ("arrive", UP))
        reduce(("add_second", C0), ("add_second", C1))

    @follow
    def _():
        reduce(*(("add_first", k) for k in range(5)))
        reduce(*(("add_second", k) for k in (A, DOWN, C0)))
        reduce(("add_third", A), ("along", A), ("add_second", UP), ("add_third", DOWN), ("along", DOWN))
        reduce(("add_third", UP), ("along", UP), ("arrive", A), ("arrive", DOWN), ("arrive", UP), ("add_second", C1))

    reduce(("add_third", C0), ("along", C0), ("add_third", C1), ("along", C1))
    if direct:
        for i in range(3):
            sums.step(i)
        sums.line(outs[5])
    reduce(("arrive", C0), ("arrive", C1))
    if direct:
        outs[4][...] = b.r3[s]
    else:
        outs[5][...] = b.small[...]

    for i in range(4):
        spread.finish(i)
    for d in (1, 2, 3):
        og_copy(d).wait_send()
    for g in range(len(GROUPS)):
        gather.drain(g)
    if ctxs > 1:

        @pl.when(c < ctxs - 1)
        def _():
            chain_copy(0, c + 1).wait_send()

        @pl.when(c > 0)
        def _():
            chain_copy(1, c - 1).wait_send()

    if direct:
        sums.drain()
    reduce(*(("drain", k) for k in range(5)))


def run_step(dims, pk, direct, first, length, inputs, first_memory, memory_grad, out_grad, weights, gains):
    _, tokens, width = inputs.shape
    slots = first_memory.shape[1]
    vm = pl.BlockSpec(memory_space=pltpu.VMEM)
    sm = pl.BlockSpec(memory_space=pltpu.SMEM)
    hbm = pl.BlockSpec(memory_space=pl.ANY)
    scratch = step_scratch(dims[0], pk, direct, tokens, slots, width)
    unit = unit_scratch(tokens, slots, width, pk.ff)
    shape = jax.ShapeDtypeStruct
    return pl.pallas_call(
        partial(step_kernel, dims, pk, direct, tuple(scratch), tuple(unit)),
        out_shape=(
            shape((4, tokens // 4, width), BF), shape((4, slots, width), F32),
            shape((4, tokens // 4, width), BF), shape((4, slots, width), F32),
            shape((pk.rows, 128) if direct else pk.shape, BF), shape((8, width), F32),
        ),
        in_specs=[sm, sm] + [hbm] * 15 + [vm],
        out_specs=(hbm,) * 4 + (vm, vm),
        scratch_shapes=list(scratch.values()) + list(unit.values()),
        compiler_params=pltpu.CompilerParams(
            vmem_limit_bytes=VMEM_LIMIT, collective_id=1, has_side_effects=True
        ),
        name="step",
    )(first, length, inputs, first_memory, memory_grad, out_grad, *weights, gains)


def store_kernel(pk, owners, *refs):
    rows_in, total, small = refs[:4], refs[4], refs[5]
    rows_out, (wq, wk, wv, wo, up, down, uq, uk, uv, uo, ugate), vectors = refs[6:10], refs[10:21], refs[21:]
    for src, dst in zip(rows_in, rows_out):
        dst[...] = src[...]

    def part(at, size):
        return total[at : at + size, :].astype(F32)

    h = pk.head_rows
    for name, ref in dict(wq=wq, wk=wk, wv=wv, uq=uq, uk=uk, uv=uv).items():
        ref[...] = part(pk.heads[name], h)
    for name, ref in dict(uo=uo, ugate=ugate).items():
        ref[...] = part(pk.heads[name], h).T
    for at, r, ref in ((pk.at_wo, pk.row_rows, wo), (pk.at_up, pk.row_rows, up), (pk.at_down, pk.down_rows, down)):
        for j in range(ref.shape[1] // 128):
            ref[:, j * 128 : j * 128 + 128] = part(at + j * r, r)
    share = small.shape[1] // owners
    owner = lax.axis_index("shard")
    for axis in ("ctx", "tp"):
        owner = owner * lax.axis_size(axis) + lax.axis_index(axis)
    turned = pltpu.roll(small[...], small.shape[1] - owner * share, 1)
    for i, ref in enumerate(vectors):
        ref[...] = turned[i : i + 1, 0:share]


def run_store(pk, owners, rows, total, small):
    vm = pl.BlockSpec(memory_space=pltpu.VMEM)
    shape = jax.ShapeDtypeStruct
    width = small.shape[1]
    h = pk.head_rows
    head, turned = shape((h, 128), F32), shape((128, h), F32)
    outs = tuple(shape(r.shape, r.dtype) for r in rows) + (
        head, head, head, shape((pk.row_rows, width), F32), shape((pk.row_rows, pk.ff), F32),
        shape((pk.down_rows, width), F32), head, head, head, turned, turned,
    ) + (shape((1, width // owners), F32),) * 4
    return pl.pallas_call(
        partial(store_kernel, pk, owners),
        out_shape=outs,
        in_specs=[vm] * 6,
        out_specs=(vm,) * len(outs),
        compiler_params=pltpu.CompilerParams(vmem_limit_bytes=VMEM_LIMIT),
        name="store",
    )(*rows, total, small)


def full_gradients(pk, grads):
    groups, owners = pk.shards * pk.ctxs, pk.shards * pk.ctxs * 4
    by_head = grads.reshape(groups, 4, pk.rows, 128)
    by_owner = grads.reshape(owners, pk.rows, 128)

    def head(name):
        at = pk.heads[name]
        got = by_head[:, :, at : at + pk.head_rows]
        return got.transpose(0, 2, 1, 3).reshape(pk.width, pk.width).astype(F32)

    def rows(at, h, n):
        got = by_owner[:, at : at + h * n].reshape(owners, n, h, 128)
        return got.transpose(0, 2, 1, 3).reshape(owners * h, n * 128).astype(F32)

    return (
        head("wq"), head("wk"), head("wv"),
        rows(pk.at_wo, pk.row_rows, pk.width // 128),
        rows(pk.at_up, pk.row_rows, pk.ff // 128),
        rows(pk.at_down, pk.down_rows, pk.width // 128),
        head("uq"), head("uk"), head("uv"), head("uo").T, head("ugate").T,
    )


def local(
    inputs, first_memory, piece_start, piece_len,
    w_query, w_key, w_value, w_out, w_up, w_down, u_query, u_key, u_value, u_out, u_gate,
    gain_attn, gain_ffn, gain_write, gate_bias, out_grad, memory_grad,
):
    shards, ctxs, tps = (lax.axis_size(a) for a in ("shard", "ctx", "tp"))
    seqs, tokens, width = inputs.shape
    ff = w_up.shape[1]
    assert seqs == tps == 4 and tokens == width == 512 and ff == 2048
    weights = (w_query, w_key, w_value, w_out, w_up, w_down, u_query, u_key, u_value, u_out, u_gate)
    gains = jnp.stack([gain_attn, gain_ffn, gain_write, gate_bias] * 2)
    owners = shards * ctxs * tps
    direct = ctxs == 2 and width % (owners * 16) == 0
    halved = ctxs == 2 and w_query.shape[0] % 32 == 0
    pk = Packing(shards if direct else 4, 2, width, ff)
    got = run_step(
        (shards, ctxs, halved), pk, direct, piece_start, piece_len, inputs, first_memory, memory_grad,
        out_grad, weights, gains,
    )
    if direct:
        out = run_store(pk, owners, got[:4], got[4], got[5])
        return out[:15] + tuple(v.reshape(-1) for v in out[15:])
    every = ("shard", "ctx", "tp")
    out = list(got[:4])
    for i, g in enumerate(full_gradients(pk, got[4])):
        if i in (3, 4, 5):
            out.append(lax.psum_scatter(g, every, scatter_dimension=0, tiled=True))
            continue
        sum_dim = 1 if i >= 9 else 0
        cut = lax.psum_scatter(g, "tp", scatter_dimension=1 - sum_dim, tiled=True)
        out.append(lax.psum_scatter(cut, ("shard", "ctx"), scatter_dimension=sum_dim, tiled=True))
    for i in range(4):
        out.append(lax.psum_scatter(got[5][i], every, scatter_dimension=0, tiled=True))
    return tuple(out)


def solution(mesh):
    cut = P(("shard", "tp"), None)
    head, rows, turned = P(("shard", "ctx"), "tp"), P(("shard", "ctx", "tp"), None), P("tp", ("shard", "ctx"))
    vector = P(("shard", "ctx", "tp"))
    over_rows, over_ctx = P("shard", ("ctx", "tp"), None), P("shard", "ctx", None)
    return jax.shard_map(
        local,
        mesh=mesh,
        in_specs=(over_ctx, P("shard", None, None), P("shard", "ctx"), P("shard", "ctx"))
        + (cut,) * 11 + (P(),) * 4 + (over_rows, over_ctx),
        out_specs=(over_rows, over_ctx, over_rows, over_ctx)
        + (head,) * 3 + (rows,) * 3 + (head,) * 3 + (turned,) * 2 + (vector,) * 4,
        check_vma=False,
    )
```

```python
from functools import partial

import jax
import jax.numpy as jnp
from jax import lax
from jax.experimental import pallas as pl
from jax.experimental.pallas import tpu as pltpu
from jax.sharding import PartitionSpec as P

F32 = jnp.float32
BF = jnp.bfloat16
MESH = pl.DeviceIdType.MESH
HEAD = 64
EPS = 1e-05
NEG = -1e30
VMEM_LIMIT = 67000000

WQ, WK, WV, WO, WUP, WDOWN, UQ, UK, UV, UO, UGATE = 0, 1, 2, 3, 4, 8, 12, 13, 14, 15, 16
TILES = 17


def dot(a, b):
    return lax.dot_general(a, b, (((1,), (0,)), ((), ())), preferred_element_type=F32)


def dot_nt(a, b):
    return lax.dot_general(a, b, (((1,), (1,)), ((), ())), preferred_element_type=F32)


def dot_tn(a, b):
    return lax.dot_general(a, b, (((0,), (0,)), ((), ())), preferred_element_type=F32)


def rows_at(i, size):
    return pl.ds(pl.multiple_of(i * size, size), size)


def loop(count, unroll=1):
    def run(body):
        def step(i, carry):
            body(i)
            return carry

        lax.fori_loop(0, count, step, 0, unroll=unroll)

    return run


def normed(v):
    mean = jnp.mean(v, axis=-1, keepdims=True)
    centered = v - mean
    inv = lax.rsqrt(jnp.mean(centered * centered, axis=-1, keepdims=True) + EPS)
    return centered * inv, inv


def norm_pull(e, gain, hat, inv):
    h = e * gain
    m0 = jnp.mean(h, axis=-1, keepdims=True)
    m1 = jnp.mean(h * hat, axis=-1, keepdims=True)
    return inv * (h - m0 - hat * m1)


def lane_block(width, block):
    return lax.broadcasted_iota(jnp.int32, (1, width), 1) // block


class Weights:
    def __init__(self, ref):
        self.ref = ref
        self.blocks, _, self.rows, self.width = ref.shape

    def cols(self, tile, start, size):
        got = self.ref[:, tile, :, pl.ds(start, size)]
        return got.reshape(self.blocks * self.rows, size)

    def row_part(self, tile, part, parts):
        count = self.blocks // parts
        got = self.ref[pl.ds(part * count, count), tile]
        return got.reshape(count * self.rows, self.width)

    def down_cols(self, chunk, chunks, start, size):
        count = self.blocks // chunks
        got = self.ref[pl.ds(chunk * count, count), WDOWN : WDOWN + 4, :, pl.ds(start, size)]
        return got.reshape(count * 4 * self.rows, size)

    def down_rows(self, part, parts):
        count = self.blocks // parts
        got = self.ref[pl.ds(part * count, count), WDOWN : WDOWN + 4]
        return got.reshape(count * 4 * self.rows, self.width)


def unit_scratch(tokens, slots, width, ff):
    r = tokens + slots
    heads = width // HEAD
    quads = width // 256
    v = pltpu.VMEM
    return dict(
        mem=v((slots, width), F32),
        xh=v((r, width), F32),
        xr=v((r, 1), F32),
        enc=v((r, width), BF),
        q=v((tokens, width), BF),
        k=v((r, width), BF),
        v=v((r, width), BF),
        kt=v((width, r), BF),
        vt=v((width, r), BF),
        pt=v((heads, r, tokens), BF),
        mixt=v((width, tokens), BF),
        af=v((tokens, width), F32),
        ah=v((tokens, width), F32),
        ar=v((tokens, 1), F32),
        fin=v((tokens, width), BF),
        act=v((ff // 512, tokens, 512), BF),
        dg=v((ff // 512, tokens, 512), BF),
        yh=v((tokens, width), F32),
        yr=v((tokens, 1), F32),
        wri=v((r, width), BF),
        sq=v((slots, width), BF),
        sk=v((r, width), BF),
        sv=v((r, width), BF),
        spt=v((quads, r, 256), BF),
        wrt=v((slots, width), BF),
        gate=v((slots, width), F32),
        f1=v((slots, width), F32),
        f2=v((slots, width), F32),
        gm=v((slots, width), F32),
        gup=v((slots, width), BF),
        ggl=v((slots, width), BF),
        dsq=v((slots, width), BF),
        dsk=v((r, width), BF),
        dsv=v((r, width), BF),
        e=v((r, width), F32),
        gy=v((tokens, width), F32),
        gyb=v((tokens, width), BF),
        bwm=v((slots, width), F32),
        gpre=v((ff // 512, tokens, 512), BF),
        gab=v((tokens, width), BF),
        gmx=v((tokens, width), BF),
        dst=v((2, r, tokens), BF),
        dqt=v((width, tokens), BF),
        dq=v((tokens, width), BF),
        dk=v((r, width), BF),
        dv=v((r, width), BF),
    )


class Unit:
    def __init__(self, refs, w, x, gains, small):
        self.__dict__.update(refs)
        self.w = w
        self.x = x
        self.gains = gains
        self.small = small
        self.tokens, self.width = x.shape
        self.slots = self.mem.shape[0]
        self.r = self.tokens + self.slots
        self.ff = self.act.shape[0] * 512

    def gain(self, i):
        return self.gains[i][...]

    def make_bias(self, first, length):
        t = self.tokens

        @loop(t // 64)
        def _(i):
            key = lax.broadcasted_iota(jnp.int32, (64, t), 0) + i * 64
            query = lax.broadcasted_iota(jnp.int32, (64, t), 1)
            last = first + length
            inside = (key >= first) & (key < last) & (query >= first) & (query < last)
            seen = (key <= query) | inside
            self.e[rows_at(i, 64), :] = jnp.where(seen, 0.0, NEG).astype(F32)

    def norm_in(self, rows, values):
        hat, inv = normed(values)
        self.xh[rows, :] = hat
        self.xr[rows, :] = inv
        self.enc[rows, :] = (hat * self.gain(0)).astype(BF)

    def tokens_in(self):
        @loop(self.tokens // 32, unroll=2)
        def _(i):
            rows = rows_at(i, 32)
            self.norm_in(rows, self.x[rows, :].astype(F32))

    def project_tokens(self):
        t = self.tokens

        @loop(self.width // 256)
        def _(n):
            cols = rows_at(n, 256)
            enc = self.enc[0:t, :]
            got = dot(enc, self.w.cols(WQ, n * 256, 256)).astype(BF)
            self.q[:, cols] = got * BF(HEAD**-0.5)
            self.k[0:t, cols] = dot(enc, self.w.cols(WK, n * 256, 256)).astype(BF)
            self.v[0:t, cols] = dot(enc, self.w.cols(WV, n * 256, 256)).astype(BF)

    def memory_in(self):
        t, r = self.tokens, self.r
        self.norm_in(slice(t, r), self.mem[...])
        enc = self.enc[t:r, :]
        self.k[t:r, :] = dot(enc, self.w.cols(WK, 0, self.width)).astype(BF)
        self.v[t:r, :] = dot(enc, self.w.cols(WV, 0, self.width)).astype(BF)
        self.vt[...] = self.v[...].T

    def attend(self, first, count):
        t, r = self.tokens, self.r

        @loop(count)
        def _(i):
            p = i + first
            cols = rows_at(p, 128)
            keys = self.k[:, cols]
            half = lane_block(128, HEAD)
            for hh in range(2):
                feats = pl.ds(pl.multiple_of(p * 128 + hh * HEAD, HEAD), HEAD)
                values = self.vt[feats, :]
                for n in range(t // 256):
                    qc = slice(n * 256, n * 256 + 256)
                    q = self.q[qc, cols]
                    q = jnp.where(half == hh, q, jnp.zeros_like(q))
                    s = dot_nt(keys, q)
                    s_tok = s[0:t] + self.e[0:t, qc]
                    s_mem = s[t:r]
                    peak = jnp.maximum(
                        jnp.max(s_tok, axis=0, keepdims=True), jnp.max(s_mem, axis=0, keepdims=True)
                    )
                    e_tok = jnp.exp(s_tok - peak)
                    e_mem = jnp.exp(s_mem - peak)
                    inv = 1.0 / (
                        jnp.sum(e_tok, axis=0, keepdims=True)
                        + jnp.sum(e_mem, axis=0, keepdims=True)
                    )
                    probs = jnp.concatenate([e_tok * inv, e_mem * inv], axis=0).astype(BF)
                    self.pt[2 * p + hh, :, qc] = probs
                    self.mixt[feats, qc] = dot(values, probs).astype(BF)

    def after_attention(self):
        t = self.tokens
        self.gmx[...] = self.mixt[...].T

        @loop(self.width // 256)
        def _(n):
            cols = rows_at(n, 256)
            got = dot(self.gmx[...], self.w.cols(WO, n * 256, 256))
            self.af[:, cols] = self.x[:, cols].astype(F32) + got

        @loop(t // 32, unroll=2)
        def _(i):
            rows = rows_at(i, 32)
            hat, inv = normed(self.af[rows, :])
            self.ah[rows, :] = hat
            self.ar[rows, :] = inv
            self.fin[rows, :] = (hat * self.gain(1)).astype(BF)

    def feed_forward_up(self):
        t = self.tokens
        for j in range(self.ff // 512):

            @loop(2)
            def _(n, j=j):
                cols = rows_at(n, 256)
                weights = self.w.cols(WUP + j, n * 256, 256)
                for m in range(t // 128):
                    rows = slice(m * 128, m * 128 + 128)
                    pre = dot(self.fin[rows, :], weights)
                    c = 0.7978845608028654
                    sq = pre * pre
                    th = jnp.tanh(pre * (c + (c * 0.044715) * sq))
                    half = 0.5 + 0.5 * th
                    self.act[j, rows, cols] = (pre * half).astype(BF)
                    slope = half + (0.5 * pre) * (1.0 - th * th) * (c + (3 * c * 0.044715) * sq)
                    self.dg[j, rows, cols] = slope.astype(BF)

    def feed_forward_down(self):
        t = self.tokens

        @loop(self.width // 256)
        def _(n):
            cols = rows_at(n, 256)
            total = self.af[:, cols]
            for j in range(self.ff // 512):
                total = total + dot(
                    self.act[j], self.w.down_cols(j, self.ff // 512, n * 256, 256)
                )
            self.af[:, cols] = total

        @loop(t // 32, unroll=2)
        def _(i):
            rows = rows_at(i, 32)
            hat, inv = normed(self.af[rows, :])
            self.yh[rows, :] = hat
            self.yr[rows, :] = inv
            self.wri[rows, :] = (hat * self.gain(2)).astype(BF)

        self.wri[t : self.r, :] = (self.xh[t : self.r, :] * self.gain(2)).astype(BF)

    def spread_heads(self, rows, g):
        part = rows[:, g * 256 : g * 256 + 256]
        block = lane_block(256, HEAD)
        return jnp.concatenate(
            [jnp.where(block == h, part, jnp.zeros_like(part)) for h in range(4)], axis=0
        )

    def gather_heads(self, stacked):
        block = lane_block(256, HEAD)
        s = self.slots
        total = jnp.where(block == 0, stacked[0:s], 0.0)
        for h in range(1, 4):
            total = total + jnp.where(block == h, stacked[h * s : h * s + s], 0.0)
        return total

    def write_memory(self):
        t, r = self.tokens, self.r

        @loop(self.width // 256)
        def _(n):
            cols = rows_at(n, 256)
            wri = self.wri[...]
            self.sk[:, cols] = dot(wri, self.w.cols(UK, n * 256, 256)).astype(BF)
            self.sv[:, cols] = dot(wri, self.w.cols(UV, n * 256, 256)).astype(BF)

        wm = self.wri[t:r, :]
        sq = dot(wm, self.w.cols(UQ, 0, self.width)).astype(BF)
        self.sq[...] = sq * BF(HEAD**-0.5)
        for g in range(self.width // 256):
            cols = slice(g * 256, g * 256 + 256)
            s = dot_nt(self.sk[:, cols], self.spread_heads(self.sq[...], g))
            e = jnp.exp(s - jnp.max(s, axis=0, keepdims=True))
            probs = (e * (1.0 / jnp.sum(e, axis=0, keepdims=True))).astype(BF)
            self.spt[g] = probs
            self.wrt[:, cols] = self.gather_heads(dot_tn(probs, self.sv[:, cols])).astype(BF)
        th = jnp.tanh(dot(self.wrt[...], self.w.cols(UO, 0, self.width)))
        pre = dot(wm, self.w.cols(UGATE, 0, self.width))
        gate = jax.nn.sigmoid(pre + self.gain(3))
        mem = self.mem[...]
        self.gate[...] = gate
        self.f1[...] = (mem - th) * gate * (1.0 - gate)
        self.f2[...] = (1.0 - gate) * (1.0 - th * th)
        return gate * mem + (1.0 - gate) * th

    def backward_early(self):
        self.kt[...] = self.k[...].T

    def write_back(self, out_grad):
        t, r, s = self.tokens, self.r, self.slots
        gm = self.gm[...]
        ggp = gm * self.f1[...]
        gup = (gm * self.f2[...]).astype(BF)
        ggl = ggp.astype(BF)
        self.gup[...] = gup
        self.ggl[...] = ggl
        self.small[3:4, :] = jnp.sum(ggp, axis=0, keepdims=True)
        gwr = dot_nt(gup, self.w.row_part(UO, 0, 1)).astype(BF)
        for g in range(self.width // 256):
            cols = slice(g * 256, g * 256 + 256)
            grads = self.spread_heads(gwr, g)
            dp = dot_nt(self.sv[:, cols], grads)
            probs = self.spt[g]
            pf = probs.astype(F32)
            ds = (pf * (dp - jnp.sum(pf * dp, axis=0, keepdims=True))).astype(BF)
            self.dsv[:, cols] = dot(probs, grads).astype(BF)
            self.dsk[:, cols] = dot(ds, self.spread_heads(self.sq[...], g)).astype(BF)
            dq = self.gather_heads(dot_tn(ds, self.sk[:, cols])) * HEAD**-0.5
            self.dsq[:, cols] = dq.astype(BF)

        @loop(2)
        def _(n):
            cols = rows_at(n, self.width // 2)
            self.e[:, cols] = dot_nt(self.dsk[...], self.w.row_part(UK, n, 2)) + dot_nt(
                self.dsv[...], self.w.row_part(UV, n, 2)
            )

        em = self.e[t:r, :] + dot_nt(self.dsq[...], self.w.row_part(UQ, 0, 1))
        em = em + dot_nt(ggl, self.w.row_part(UGATE, 0, 1))
        hat = self.xh[t:r, :]
        self.bwm[...] = norm_pull(em, self.gain(2), hat, self.xr[t:r, :])
        self.small[2:3, :] = jnp.sum(em * hat, axis=0, keepdims=True)

        @loop(t // 32, unroll=2)
        def _(i):
            rows = rows_at(i, 32)
            e = self.e[rows, :]
            hat = self.yh[rows, :]
            self.small[2:3, :] += jnp.sum(e * hat, axis=0, keepdims=True)
            grad = out_grad(i) + norm_pull(e, self.gain(2), hat, self.yr[rows, :])
            self.gy[rows, :] = grad
            self.gyb[rows, :] = grad.astype(BF)

    def feed_forward_back(self):
        t = self.tokens
        chunks = self.ff // 512

        for j in range(chunks):

            @loop(2)
            def _(n, j=j):
                cols = rows_at(n, 256)
                weights = self.w.down_rows(2 * j + n, 2 * chunks)
                for m in range(t // 128):
                    rows = slice(m * 128, m * 128 + 128)
                    got = dot_nt(self.gyb[rows, :], weights)
                    self.gpre[j, rows, cols] = (got * self.dg[j, rows, cols].astype(F32)).astype(BF)

    def feed_forward_enter(self):
        t = self.tokens
        chunks = self.ff // 512

        @loop(2)
        def _(n):
            cols = rows_at(n, self.width // 2)
            total = dot_nt(self.gpre[0], self.w.row_part(WUP, n, 2))
            for j in range(1, chunks):
                total = total + dot_nt(self.gpre[j], self.w.row_part(WUP + j, n, 2))
            self.e[0:t, cols] = total

        self.small[1:2, :] = jnp.zeros((1, self.width), F32)

        @loop(t // 32, unroll=2)
        def _(i):
            rows = rows_at(i, 32)
            e = self.e[rows, :]
            hat = self.ah[rows, :]
            self.small[1:2, :] += jnp.sum(e * hat, axis=0, keepdims=True)
            grad = self.gy[rows, :] + norm_pull(e, self.gain(1), hat, self.ar[rows, :])
            self.gy[rows, :] = grad
            self.gab[rows, :] = grad.astype(BF)

    def project_back(self):
        @loop(2)
        def _(n):
            cols = rows_at(n, self.width // 2)
            self.gmx[:, cols] = dot_nt(self.gab[...], self.w.row_part(WO, n, 2)).astype(BF)

    def attend_back(self, first, count):
        t, r = self.tokens, self.r

        @loop(count)
        def _(i):
            p = i + first
            cols = rows_at(p, 128)
            values = self.v[:, cols]
            half = lane_block(128, HEAD)
            for hh in range(2):
                feats = pl.ds(pl.multiple_of(p * 128 + hh * HEAD, HEAD), HEAD)
                keys = self.kt[feats, :]
                for n in range(t // 256):
                    qc = slice(n * 256, n * 256 + 256)
                    g = self.gmx[qc, cols]
                    g = jnp.where(half == hh, g, jnp.zeros_like(g))
                    dp = dot_nt(values, g)
                    pf = self.pt[2 * p + hh, :, qc].astype(F32)
                    ds = (pf * (dp - jnp.sum(pf * dp, axis=0, keepdims=True))).astype(BF)
                    self.dst[hh, :, qc] = ds
                    self.dqt[feats, qc] = (dot(keys, ds) * HEAD**-0.5).astype(BF)
            g = self.gmx[:, cols]
            q = self.q[:, cols]
            dv = jnp.where(half == 0, dot(self.pt[2 * p], g), dot(self.pt[2 * p + 1], g))
            self.dv[:, cols] = dv.astype(BF)
            dk = jnp.where(half == 0, dot(self.dst[0], q), dot(self.dst[1], q))
            self.dk[:, cols] = dk.astype(BF)

    def queries_back(self):
        self.dq[...] = self.dqt[...].T

    def enter_back(self):
        t = self.tokens

        @loop(2)
        def _(n):
            cols = rows_at(n, self.width // 2)
            self.e[:, cols] = dot_nt(self.dk[...], self.w.row_part(WK, n, 2)) + dot_nt(
                self.dv[...], self.w.row_part(WV, n, 2)
            )
            self.e[0:t, cols] += dot_nt(self.dq[...], self.w.row_part(WQ, n, 2))

    def norm_enter(self, input_grad):
        t, r = self.tokens, self.r
        e = self.e[t:r, :]
        hat = self.xh[t:r, :]
        self.small[0:1, :] = jnp.sum(e * hat, axis=0, keepdims=True)
        mem_grad = self.gm[...] * self.gate[...] + self.bwm[...]
        mem_grad = mem_grad + norm_pull(e, self.gain(0), hat, self.xr[t:r, :])

        @loop(t // 32, unroll=2)
        def _(i):
            rows = rows_at(i, 32)
            e = self.e[rows, :]
            hat = self.xh[rows, :]
            self.small[0:1, :] += jnp.sum(e * hat, axis=0, keepdims=True)
            grad = self.gy[rows, :] + norm_pull(e, self.gain(0), hat, self.xr[rows, :])
            input_grad[rows, :] = grad.astype(BF)

        return mem_grad


class Packing:
    def __init__(self, shards, ctxs, width, ff):
        self.shards, self.ctxs, self.width, self.ff = shards, ctxs, width, ff
        self.head_rows = h = width // (shards * ctxs)
        self.row_rows = width // (shards * ctxs * 4)
        self.down_rows = ff // (shards * ctxs * 4)
        self.at_down = 0
        at = self.down_rows * (width // 128)
        self.heads = {}
        for name in ("uq", "uk", "uv", "uo", "ugate"):
            self.heads[name] = at
            at += h
        self.at_up = at
        self.at_wo = at + self.row_rows * (ff // 128)
        last = at = self.at_wo + self.row_rows * (width // 128)
        for name in ("wq", "wk", "wv"):
            self.heads[name] = at
            at += h
        self.rows = at
        middle = last + (at - last) // 2 // 16 * 16
        bounds = (0, self.heads["uq"], self.at_up, self.at_wo, last, middle, at)
        self.chunks = tuple(zip(bounds[:-1], bounds[1:]))

    @property
    def shape(self):
        return (self.shards, self.ctxs, 2, 2, self.rows, 128)


def weight_grads(u, g, pk, names):
    width = u.width
    tile = 256

    def store_head(at, m, got):
        h = pk.head_rows
        per = tile // h
        for i in range(per):
            s = m * (per // pk.ctxs) + i // pk.ctxs
            for t in range(4):
                g[s, i % pk.ctxs, t // 2, t % 2, at : at + h, :] = got[
                    i * h : i * h + h, t * 128 : t * 128 + 128
                ]

    def store_rows(at, h, m, got, chunk0):
        per = tile // h
        for i in range(per):
            if per % (pk.ctxs * 4) == 0:
                s, c = m * (per // (pk.ctxs * 4)) + i // (pk.ctxs * 4), (i // 4) % pk.ctxs
            else:
                owner = m * (per // 4) + i // 4
                s, c = lax.div(owner, pk.ctxs), lax.rem(owner, pk.ctxs)
            for j in range(got.shape[1] // 128):
                lo = at + (chunk0 + j) * h
                g[s, c, (i // 2) % 2, i % 2, lo : lo + h, :] = got[
                    i * h : i * h + h, j * 128 : j * 128 + 128
                ]

    def head(name, left, right):
        at = pk.heads[name]

        @loop(width // tile)
        def _(m):
            lt = left[:, rows_at(m, tile)].T
            store_head(at, m, dot(lt, right[...]).astype(BF))

    t, r = u.tokens, u.r
    if "down" in names:
        for j in range(u.ff // 512):

            @loop(512 // tile)
            def _(m, j=j):
                lt = u.act[j, :, rows_at(m, tile)].T
                got = dot(lt, u.gyb[...]).astype(BF)
                store_rows(pk.at_down, pk.down_rows, m + j * (512 // tile), got, 0)

    if "up" in names:

        @loop(width // tile)
        def _(m):
            lt = u.fin[:, rows_at(m, tile)].T
            for j in range(u.ff // 512):
                store_rows(pk.at_up, pk.row_rows, m, dot(lt, u.gpre[j]).astype(BF), 4 * j)

    if "wo" in names:

        @loop(width // tile)
        def _(m):
            got = dot(u.mixt[rows_at(m, tile), :], u.gab[...]).astype(BF)
            store_rows(pk.at_wo, pk.row_rows, m, got, 0)

    if "write" in names:
        head("uq", u.wri.at[t:r], u.dsq)
        head("uk", u.wri, u.dsk)
        head("uv", u.wri, u.dsv)
        head("uo", u.gup, u.wrt)
        head("ugate", u.ggl, u.wri.at[t:r])
    if "enter" in names:
        head("wq", u.enc.at[0:t], u.dq)
        head("wk", u.enc, u.dk)
        head("wv", u.enc, u.dv)


GROUPS = ((0, 3), (3, 8), (8, 12), (12, 17))


def greet(peers):
    barrier = pltpu.get_barrier_semaphore()
    count = 0
    for cond, device in peers:

        @pl.when(cond)
        def _(device=device):
            pl.semaphore_signal(barrier, inc=1, device_id=device, device_id_type=MESH)

        count = count + jnp.where(cond, 1, 0)
    pl.semaphore_wait(barrier, count)


class Gather:
    UP, DOWN, PAIR, ACROSS, PAIR_ACROSS, BESIDE, PAIR_BESIDE, FAR, PAIR_FAR = range(9)

    def __init__(self, shards, halved, w, send, recv):
        self.n, self.halved, self.w, self.send, self.recv = shards, halved, w, send, recv
        self.s, self.c, self.t = (lax.axis_index(a) for a in ("shard", "ctx", "tp"))
        odd = lax.rem(self.t, 2)
        self.pair_tp = self.t + 1 - 2 * odd
        self.across_tp = lax.rem(self.t + 2, 4)
        self.pair = {"tp": self.pair_tp}
        self.across = {"tp": self.across_tp}
        self.beside = {"ctx": self.c + 1 - 2 * lax.rem(self.c, 2)}

    def copy(self, kind, source, tp, g, device, half=None):
        lo, hi = GROUPS[g]
        block = self.w.at[source * 4 + tp, lo:hi]
        if half is not None:
            size = self.w.shape[2] // 2
            block = self.w.at[source * 4 + tp, lo:hi, pl.ds(pl.multiple_of(half * size, size), size)]
        return pltpu.make_async_remote_copy(
            src_ref=block, dst_ref=block, send_sem=self.send.at[kind, source, g],
            recv_sem=self.recv.at[kind, source, g], device_id=device, device_id_type=MESH,
        )

    @property
    def mine(self):
        return self.c if self.halved else None

    @property
    def others(self):
        return 1 - self.c

    def up(self, source, g, far):
        return self.copy(self.UP, source, self.t, g, {"shard": self.s + 1}, self.mine if far else None)

    def down(self, source, g, far):
        return self.copy(self.DOWN, source, self.t, g, {"shard": self.s - 1}, self.mine if far else None)

    def to_across(self, source, g, tp=None):
        return self.copy(self.ACROSS, source, self.t if tp is None else tp, g, self.across, self.mine)

    def to_pair(self, source, g, far, tp=None):
        return self.copy(self.PAIR, source, self.t if tp is None else tp, g, self.pair, self.mine if far else None)

    def far(self, d):
        return self.halved and d == self.n - 1

    def start_own(self, g):
        s, n = self.s, self.n
        if n > 1:

            @pl.when(s < n - 1)
            def _():
                self.up(s, g, self.far(1)).start()

            @pl.when(s > 0)
            def _():
                self.down(s, g, self.far(1)).start()

        self.to_across(s, g).start()
        self.to_pair(s, g, False).start()

    def came(self, source, g, d):
        self.to_across(source, g).start()
        self.to_pair(source, g, self.far(d)).start()
        if self.far(d):
            self.copy(self.FAR, source, self.t, g, self.beside, self.c).start()

    def line_step(self, d, g):
        s, n = self.s, self.n

        @pl.when(s - d >= 0)
        def _():
            self.up(s - d, g, self.far(d)).wait_recv()

            @pl.when(s < n - 1)
            def _():
                self.up(s - d, g, self.far(d + 1)).start()

            self.came(s - d, g, d)

        @pl.when(s + d <= n - 1)
        def _():
            self.down(s + d, g, self.far(d)).wait_recv()

            @pl.when(s > 0)
            def _():
                self.down(s + d, g, self.far(d + 1)).start()

            self.came(s + d, g, d)

    def sources(self, d):
        s, n = self.s, self.n
        both = ((s - d, s - d >= 0), (s + d, s + d <= n - 1))
        return both[:1] if d == 0 else both

    def across_step(self, d, g):
        for source, cond in self.sources(d):

            @pl.when(cond)
            def _(source=source):
                tp = self.across_tp
                self.to_across(source, g, tp).wait_recv()
                self.copy(self.PAIR_ACROSS, source, tp, g, self.pair, self.mine).start()
                if self.halved:
                    self.copy(self.BESIDE, source, tp, g, self.beside, self.c).start()

    def beside_step(self, d, g):
        if not self.halved:
            return
        for source, cond in self.sources(d):

            @pl.when(cond)
            def _(source=source):
                tp = self.across_tp
                self.copy(self.BESIDE, source, tp, g, self.beside, self.others).wait_recv()
                self.copy(self.PAIR_BESIDE, source, tp, g, self.pair, self.others).start()

    def far_step(self, g):
        if not self.halved:
            return
        for source, cond in self.sources(self.n - 1):

            @pl.when(cond)
            def _(source=source):
                self.copy(self.FAR, source, self.t, g, self.beside, self.others).wait_recv()
                self.copy(self.PAIR_FAR, source, self.t, g, self.pair, self.others).start()

    def finish(self, g, own=False):
        tp = self.t if own else self.pair_tp
        other = self.across_tp if own else lax.rem(self.pair_tp + 2, 4)
        for d in range(self.n):
            for source, cond in self.sources(d):

                @pl.when(cond)
                def _(source=source, d=d):
                    copies = [
                        self.to_pair(source, g, self.far(d), tp),
                        self.copy(self.PAIR_ACROSS, source, other, g, self.pair, self.mine),
                    ]
                    if self.halved:
                        copies.append(self.copy(self.PAIR_BESIDE, source, other, g, self.pair, self.others))
                    if self.far(d):
                        copies.append(self.copy(self.PAIR_FAR, source, tp, g, self.pair, self.others))
                    if own:
                        copies.append(self.to_across(source, g))
                        if self.halved:
                            copies.append(self.copy(self.BESIDE, source, other, g, self.beside, self.c))
                        if self.far(d):
                            copies.append(self.copy(self.FAR, source, tp, g, self.beside, self.c))
                    for copy in copies:
                        if own:
                            copy.wait_send()
                        else:
                            copy.wait_recv()

    def drain(self, g):
        s, n = self.s, self.n
        self.finish(g, own=True)
        for d in range(n - 1):

            @pl.when(jnp.logical_and(s - d >= 0, s < n - 1))
            def _(d=d):
                self.up(s - d, g, self.far(d + 1)).wait_send()

            @pl.when(jnp.logical_and(s + d <= n - 1, s > 0))
            def _(d=d):
                self.down(s + d, g, self.far(d + 1)).wait_send()

    def events(self, time, ready):
        n = self.n
        groups = range(len(GROUPS))
        for g in groups:
            if time == max(2 * g - 2, 0):
                ready(g)
                self.start_own(g)
        for g in groups:
            d = time - 2 * g
            if 1 <= d <= n - 1:
                self.line_step(d, g)
            if 0 <= d - 1 <= n - 1:
                self.across_step(d - 1, g)
            if 0 <= d - 2 <= n - 1:
                self.beside_step(d - 2, g)
            if d == n + 1:
                self.far_step(g)
                self.finish(g)

    @property
    def last(self):
        return 2 * (len(GROUPS) - 1) + self.n + 1


def line_peers(n):
    s = lax.axis_index("shard")
    return [(s >= 0, {"shard": lax.rem(s + d, n)}) for d in range(1, n)]


def tp_peers():
    t = lax.axis_index("tp")
    return [(t >= 0, {"tp": lax.rem(t + d, 4)}) for d in (1, 2, 3)]


def own_tiles(weights, w, own, sems):
    names = [WQ, WK, WV, WO, WUP, WDOWN, UQ, UK, UV, UO, UGATE]
    rows = w.shape[2]
    out = []
    for name, ref in zip(names, weights):
        parts = {WUP: 4, WDOWN: 4}.get(name, 1)
        for j in range(parts):
            src = ref
            if name == WUP:
                src = ref.at[:, j * 512 : j * 512 + 512]
            if name == WDOWN:
                src = ref.at[j * rows : j * rows + rows]
            out.append(pltpu.make_async_copy(src, w.at[own, name + j], sems.at[name + j]))
    return out


class Reduce:
    ORDER = (0, 1, 0, 1, 0, 1)

    def __init__(self, shards, chunks, g, r1, r2, r3, z, send, recv):
        self.n = shards
        self.rows = [pl.ds(lo, hi - lo) for lo, hi in chunks]
        self.g, self.r1, self.r2, self.r3, self.z = g, r1, r2, r3, z
        self.send, self.recv = send, recv
        self.s, self.c, self.t = (lax.axis_index(a) for a in ("shard", "ctx", "tp"))
        self.core = lax.rem(self.t, 2)
        self.x = lax.div(self.t, 2)
        self.pair = {"tp": self.t + 1 - 2 * self.core}
        self.across = {"tp": lax.rem(self.t + 2, 4)}
        self.beside = {"ctx": 1 - self.c}

    def copy(self, src, dst, k, kind, device):
        return pltpu.make_async_remote_copy(
            src_ref=src, dst_ref=dst, send_sem=self.send.at[k, kind], recv_sem=self.recv.at[k, kind],
            device_id=device, device_id_type=MESH,
        )

    def one(self, k):
        rows = self.rows[k]
        return self.copy(self.g.at[:, :, :, 1 - self.core, rows], self.r1.at[:, :, :, rows], k, 0, self.pair)

    def two(self, k):
        rows = self.rows[k]
        if self.ORDER[k] == 0:
            src, device = self.r1.at[:, :, 1 - self.x, rows], self.across
        else:
            src, device = self.r1.at[:, 1 - self.c, :, rows], self.beside
        return self.copy(src, self.r2.at[:, :, rows], k, 1, device)

    def three(self, k):
        rows = self.rows[k]
        if self.ORDER[k] == 0:
            src, device = self.r2.at[:, 1 - self.c, rows], self.beside
        else:
            src, device = self.r2.at[:, 1 - self.x, rows], self.across
        return self.copy(src, self.r3.at[:, rows], k, 2, device)

    def along(self, k, d):
        to = lax.rem(self.s + d, self.n)
        rows = self.rows[k]
        return self.copy(self.r3.at[to, rows], self.z.at[d - 1, rows], k, 2 + d, {"shard": to})

    def start(self, k):
        self.one(k).start()

    def to_second(self, k):
        self.one(k).wait_recv()
        rows = self.rows[k]
        for j in range(2):
            for x in range(2):
                self.r1[:, j, x, rows] += self.g[:, j, x, self.core, rows]
        self.two(k).start()

    def to_third(self, k):
        self.two(k).wait_recv()
        rows = self.rows[k]
        for j in range(2):
            own = self.r1[:, j, self.x, rows] if self.ORDER[k] == 0 else self.r1[:, self.c, j, rows]
            self.r2[:, j, rows] += own
        self.three(k).start()

    def to_last(self, k):
        self.three(k).wait_recv()
        rows = self.rows[k]
        own = self.c if self.ORDER[k] == 0 else self.x
        self.r3[:, rows] += self.r2[:, own, rows]
        for d in range(1, self.n):
            self.along(k, d).start()

    def arrive(self, k, out):
        for d in range(1, self.n):
            self.along(k, d).wait_recv()
        rows = self.rows[k]
        total = self.r3[self.s, rows].astype(F32)
        for d in range(1, self.n):
            total = total + self.z[d - 1, rows].astype(F32)
        out[rows, :] = total.astype(out.dtype)

    def drain(self, k):
        for copy in [self.one(k), self.two(k), self.three(k)] + [self.along(k, d) for d in range(1, self.n)]:
            copy.wait_send()


class SmallSum:
    def __init__(self, shards, own, got, send, recv):
        self.n, self.own, self.got, self.send, self.recv = shards, own, got, send, recv
        self.s, self.c, self.t = (lax.axis_index(a) for a in ("shard", "ctx", "tp"))

    def copy(self, i):
        near = [{"tp": self.t + 1 - 2 * lax.rem(self.t, 2)}, {"tp": lax.rem(self.t + 2, 4)}, {"ctx": 1 - self.c}]
        device = near[i] if i < 3 else {"shard": lax.rem(self.s + i - 2, self.n)}
        return pltpu.make_async_remote_copy(
            src_ref=self.own.at[min(i, 3)], dst_ref=self.got.at[i], send_sem=self.send.at[i],
            recv_sem=self.recv.at[i], device_id=device, device_id_type=MESH,
        )

    def start(self, value):
        self.own[0] = value
        self.copy(0).start()

    def step(self, i):
        self.copy(i).wait_recv()
        self.own[i + 1] = self.own[i] + self.got[i]
        if i < 2:
            self.copy(i + 1).start()
        else:
            for d in range(1, self.n):
                self.copy(2 + d).start()

    def arrive(self, out):
        total = self.own[3]
        for d in range(1, self.n):
            self.copy(2 + d).wait_recv()
            total = total + self.got[2 + d]
        out[...] = total

    def drain(self):
        for i in range(2 + self.n):
            self.copy(i).wait_send()


class Spread:
    def __init__(self, src, dst, send, recv):
        self.src, self.dst, self.send, self.recv = src, dst, send, recv
        self.t = lax.axis_index("tp")

    def copy(self, d):
        to = lax.rem(self.t + d, 4)
        share = self.dst.shape[1]
        src = self.src.at[pl.ds(pl.multiple_of(to * share, share), share)]
        dst = self.dst.at[self.t]
        if d == 0:
            return pltpu.make_async_copy(src, dst, self.send.at[d])
        return pltpu.make_async_remote_copy(
            src_ref=src, dst_ref=dst, send_sem=self.send.at[d], recv_sem=self.recv.at[d],
            device_id={"tp": to}, device_id_type=MESH,
        )

    def start(self):
        for d in (2, 3, 1, 0):
            self.copy(d).start()

    def finish(self):
        for d in (1, 2, 3):
            self.copy(d).wait_recv()
            self.copy(d).wait_send()
        self.copy(0).wait()


class Share:
    def __init__(self, held, send, recv):
        self.held, self.send, self.recv = held, send, recv
        self.t = lax.axis_index("tp")
        self.pair_tp = self.t + 1 - 2 * lax.rem(self.t, 2)
        self.across_tp = lax.rem(self.t + 2, 4)

    def copy(self, i, tp, to):
        return pltpu.make_async_remote_copy(
            src_ref=self.held.at[tp], dst_ref=self.held.at[tp], send_sem=self.send.at[i],
            recv_sem=self.recv.at[i], device_id={"tp": to}, device_id_type=MESH,
        )

    def start(self):
        self.copy(0, self.t, self.across_tp).start()
        self.copy(1, self.t, self.pair_tp).start()

    def relay(self):
        self.copy(0, self.across_tp, self.across_tp).wait_recv()
        self.copy(2, self.across_tp, self.pair_tp).start()

    def finish(self):
        self.copy(1, self.pair_tp, self.pair_tp).wait_recv()
        self.copy(2, lax.rem(self.pair_tp + 2, 4), self.pair_tp).wait_recv()
        self.copy(0, self.t, self.across_tp).wait_send()
        self.copy(1, self.t, self.pair_tp).wait_send()
        self.copy(2, self.across_tp, self.pair_tp).wait_send()


class Comm:
    pass


def step_scratch(shards, pk, direct, tokens, slots, width):
    v, dma = pltpu.VMEM, pltpu.SemaphoreType.DMA
    n = shards
    out = dict(
        w=v((n * 4, TILES, width // (n * 4), width), BF),
        x=v((tokens, width), BF),
        m0=v((slots, width), F32),
        og=v((4, tokens // 4, width), BF),
        y=v((tokens, width), BF),
        xg=v((tokens, width), BF),
        mems=v((4, slots, width), BF),
        migs=v((4, slots, width), BF),
        small=v((8, width), F32),
        m_send=v((slots, width), BF),
        m_recv=v((slots, width), BF),
        g_send=v((slots, width), BF),
        g_recv=v((slots, width), BF),
        chain=dma((4,)),
        loads=dma((3,)),
        local=dma((TILES,)),
        w_send=dma((9, n, len(GROUPS))),
        w_recv=dma((9, n, len(GROUPS))),
        og_send=dma((4,)),
        og_recv=dma((4,)),
        y_send=dma((4,)),
        y_recv=dma((4,)),
        xg_send=dma((4,)),
        xg_recv=dma((4,)),
        mem_send=dma((3,)),
        mem_recv=dma((3,)),
        mig_send=dma((3,)),
        mig_recv=dma((3,)),
    )
    if direct:
        c = len(pk.chunks)
        out.update(
            g=v(pk.shape, BF),
            r1=v((n, 2, 2, pk.rows, 128), BF),
            r2=v((n, 2, pk.rows, 128), BF),
            r3=v((n, pk.rows, 128), BF),
            z=v((n - 1, pk.rows, 128), BF),
            own=v((4, 8, width), F32),
            got=v((2 + n, 8, width), F32),
            r_send=dma((c, 2 + n)),
            r_recv=dma((c, 2 + n)),
            s_send=dma((2 + n,)),
            s_recv=dma((2 + n,)),
        )
    return out


def step_kernel(dims, pk, direct, names, unit_names, *refs):
    shards, ctxs, halved = dims
    first, length, inputs, first_memory, memory_grad, out_grad = refs[:6]
    weights, gains, outs = refs[6:17], refs[17:21], refs[21:27]
    scratch = refs[27:]
    b = Comm()
    b.__dict__.update(zip(names, scratch))
    unit_refs = dict(zip(unit_names, scratch[len(names) :]))
    if not direct:
        b.g = outs[4]
    s, c, t = (lax.axis_index(a) for a in ("shard", "ctx", "tp"))
    u = Unit(unit_refs, Weights(b.w), b.x, gains, b.small)

    loads = [
        pltpu.make_async_copy(inputs.at[t], b.x, b.loads.at[0]),
        pltpu.make_async_copy(first_memory.at[t], b.m0, b.loads.at[1]),
        pltpu.make_async_copy(memory_grad.at[t], u.gm, b.loads.at[2]),
    ]
    copies = own_tiles(weights, b.w, s * 4 + t, b.local)
    for copy in copies + loads:
        copy.start()
    mine = pltpu.make_async_copy(out_grad.at[t], b.og.at[t], b.og_send.at[0])
    mine.start()
    peers = line_peers(shards) + tp_peers()
    if ctxs > 1:
        peers += [(c > 0, {"ctx": c - 1}), (c < ctxs - 1, {"ctx": c + 1})]
    greet(peers)
    gather = Gather(shards, halved, b.w, b.w_send, b.w_recv)

    def ready(g):
        for copy in copies[GROUPS[g][0] : GROUPS[g][1]]:
            copy.wait()

    def gather_until(start, stop):
        for time in range(start, stop):
            gather.events(time, ready)

    def chain_copy(i, to):
        src, dst = ((b.m_send, b.m_recv), (b.g_send, b.g_recv))[i]
        return pltpu.make_async_remote_copy(
            src_ref=src, dst_ref=dst, send_sem=b.chain.at[2 * i], recv_sem=b.chain.at[2 * i + 1],
            device_id={"ctx": to}, device_id_type=MESH,
        )

    def og_copy(d):
        to = lax.rem(t + d, 4)
        return pltpu.make_async_remote_copy(
            src_ref=out_grad.at[to], dst_ref=b.og.at[t], send_sem=b.og_send.at[d],
            recv_sem=b.og_recv.at[d], device_id={"tp": to}, device_id_type=MESH,
        )

    spread_y = Spread(b.y, outs[0], b.y_send, b.y_recv)
    spread_xg = Spread(b.xg, outs[2], b.xg_send, b.xg_recv)
    share_mem = Share(b.mems, b.mem_send, b.mem_recv)
    share_mig = Share(b.migs, b.mig_send, b.mig_recv)
    lead, follow = pl.when(c == 0), pl.when(c > 0)
    pairs = u.width // 128

    gather_until(0, 1)
    for copy in loads:
        copy.wait()
    u.make_bias(first[0, t], length[0, t])
    gather_until(1, 2)
    u.tokens_in()
    at_first = shards + 2
    gather_until(2, at_first)
    u.project_tokens()

    @lead
    def _():
        u.mem[...] = b.m0[...]
        u.memory_in()
        u.attend(0, pairs // 2)

    gather_until(at_first, at_first + 1)

    @lead
    def _():
        u.attend(pairs // 2, pairs - pairs // 2)

    gather_until(at_first + 1, at_first + 2)

    @lead
    def _():
        u.after_attention()
        u.feed_forward_up()

    gather_until(at_first + 2, at_first + 4)

    @lead
    def _():
        u.feed_forward_down()

    gather_until(at_first + 4, gather.last + 1)
    for d in (1, 2, 3):
        og_copy(d).start()

    if ctxs > 1:

        @follow
        def _():
            chain_copy(0, c - 1).wait_recv()
            u.mem[...] = b.m_recv[...].astype(F32)
            u.memory_in()
            u.attend(0, pairs)
            u.after_attention()
            u.feed_forward_up()
            u.feed_forward_down()

    after = u.write_memory()
    b.m_send[...] = after.astype(BF)
    if ctxs > 1:

        @pl.when(c < ctxs - 1)
        def _():
            chain_copy(0, c + 1).start()

    b.mems[t] = after.astype(BF)
    b.y[...] = u.af[...].astype(BF)
    share_mem.start()
    spread_y.start()
    u.backward_early()
    mine.wait()
    for d in (1, 2, 3):
        og_copy(d).wait_recv()
    share_mem.relay()

    if ctxs > 1:

        @pl.when(c < ctxs - 1)
        def _():
            chain_copy(1, c + 1).wait_recv()
            u.gm[...] += b.g_recv[...].astype(F32)

    def out_grad_rows(i):
        per = b.og.shape[1] // 32
        return b.og[lax.div(i, per), pl.ds(lax.rem(i, per) * 32, 32), :].astype(F32)

    def grads(*which):
        weight_grads(u, b.g, pk, which)

    red = Reduce(shards, pk.chunks, b.g, b.r1, b.r2, b.r3, b.z, b.r_send, b.r_recv) if direct else None
    sums = SmallSum(shards, b.own, b.got, b.s_send, b.s_recv) if direct else None
    DOWN, WRITE, UP, OUT, IN0, IN1 = range(6)

    def reduce(*todo):
        for what, k in todo if direct else ():
            getattr(red, what)(k)

    u.write_back(out_grad_rows)

    @lead
    def _():
        grads("down")
        reduce(("start", DOWN))
        grads("write")
        reduce(("start", WRITE), ("to_second", DOWN))

    u.feed_forward_back()

    @lead
    def _():
        grads("up")
        reduce(("start", UP), ("to_second", WRITE))

    u.feed_forward_enter()

    @lead
    def _():
        grads("wo")
        reduce(("start", OUT), ("to_second", UP), ("to_third", DOWN))

    u.project_back()
    u.attend_back(0, pairs // 2)

    @lead
    def _():
        reduce(("to_second", OUT), ("to_third", WRITE))

    u.attend_back(pairs // 2, pairs - pairs // 2)
    u.queries_back()

    @lead
    def _():
        grads("enter")
        reduce(("start", IN0), ("start", IN1), ("to_last", DOWN), ("to_third", UP), ("to_third", OUT))

    u.enter_back()

    @lead
    def _():
        reduce(("to_second", IN0), ("to_second", IN1), ("to_last", WRITE), ("to_last", UP))

    back = u.norm_enter(b.xg)
    b.migs[t] = back.astype(BF)

    if ctxs > 1:

        @follow
        def _():
            b.g_send[...] = back.astype(BF)
            chain_copy(1, c - 1).start()
            grads("down")
            reduce(("start", DOWN))
            grads("write")
            reduce(("start", WRITE))
            grads("up")
            reduce(("start", UP), ("to_second", DOWN))
            grads("wo")
            reduce(("start", OUT), ("to_second", WRITE))
            grads("enter")
            reduce(("start", IN0), ("start", IN1))
            reduce(*(("to_second", k) for k in (UP, OUT, IN0, IN1)))

    share_mig.start()
    if direct:
        sums.start(b.small[...])
    spread_xg.start()

    @lead
    def _():
        reduce(("to_third", IN0), ("to_third", IN1), ("to_last", OUT))

    if ctxs > 1:

        @follow
        def _():
            reduce(*(("to_third", k) for k in (DOWN, UP, IN0, WRITE)))
            reduce(("to_last", DOWN), ("to_third", OUT), ("to_last", WRITE), ("to_last", UP))
            reduce(("to_last", OUT), ("to_third", IN1))

    share_mig.relay()
    reduce(("to_last", IN0), ("to_last", IN1))
    if direct:
        for i in range(3):
            sums.step(i)
        for k in range(6):
            red.arrive(k, outs[4])
        sums.arrive(outs[5])
    else:
        outs[5][...] = b.small[...]

    for spread in (spread_y, spread_xg, share_mem, share_mig):
        spread.finish()
    outs[1][...] = b.mems[...].astype(F32)
    outs[3][...] = b.migs[...].astype(F32)
    for d in (1, 2, 3):
        og_copy(d).wait_send()
    for g in range(len(GROUPS)):
        gather.drain(g)
    if ctxs > 1:

        @pl.when(c < ctxs - 1)
        def _():
            chain_copy(0, c + 1).wait_send()

        @pl.when(c > 0)
        def _():
            chain_copy(1, c - 1).wait_send()

    if direct:
        sums.drain()
    reduce(*(("drain", k) for k in range(6)))


def run_step(dims, pk, direct, first, length, inputs, first_memory, memory_grad, out_grad, weights, gains):
    _, tokens, width = inputs.shape
    slots = first_memory.shape[1]
    vm = pl.BlockSpec(memory_space=pltpu.VMEM)
    sm = pl.BlockSpec(memory_space=pltpu.SMEM)
    hbm = pl.BlockSpec(memory_space=pl.ANY)
    scratch = step_scratch(dims[0], pk, direct, tokens, slots, width)
    unit = unit_scratch(tokens, slots, width, pk.ff)
    shape = jax.ShapeDtypeStruct
    return pl.pallas_call(
        partial(step_kernel, dims, pk, direct, tuple(scratch), tuple(unit)),
        out_shape=(
            shape((4, tokens // 4, width), BF), shape((4, slots, width), F32),
            shape((4, tokens // 4, width), BF), shape((4, slots, width), F32),
            shape((pk.rows, 128) if direct else pk.shape, BF), shape((8, width), F32),
        ),
        in_specs=[sm, sm] + [hbm] * 15 + [vm] * 4,
        out_specs=(hbm, vm, hbm, vm, vm, vm),
        scratch_shapes=list(scratch.values()) + list(unit.values()),
        compiler_params=pltpu.CompilerParams(
            vmem_limit_bytes=VMEM_LIMIT, collective_id=1, has_side_effects=True
        ),
        name="step",
    )(first, length, inputs, first_memory, memory_grad, out_grad, *weights, *gains)


def store_kernel(pk, owners, *refs):
    rows_in, total, small = refs[:4], refs[4], refs[5]
    rows_out, (wq, wk, wv, wo, up, down, uq, uk, uv, uo, ugate), vectors = refs[6:10], refs[10:21], refs[21:]
    for src, dst in zip(rows_in, rows_out):
        dst[...] = src[...]

    def part(at, size):
        return total[at : at + size, :].astype(F32)

    h = pk.head_rows
    for name, ref in dict(wq=wq, wk=wk, wv=wv, uq=uq, uk=uk, uv=uv).items():
        ref[...] = part(pk.heads[name], h)
    for name, ref in dict(uo=uo, ugate=ugate).items():
        ref[...] = part(pk.heads[name], h)
    for at, r, ref in ((pk.at_wo, pk.row_rows, wo), (pk.at_up, pk.row_rows, up), (pk.at_down, pk.down_rows, down)):
        for j in range(ref.shape[1] // 128):
            ref[:, j * 128 : j * 128 + 128] = part(at + j * r, r)
    share = small.shape[1] // owners
    owner = lax.axis_index("shard")
    for axis in ("ctx", "tp"):
        owner = owner * lax.axis_size(axis) + lax.axis_index(axis)
    turned = pltpu.roll(small[...], small.shape[1] - owner * share, 1)
    for i, ref in enumerate(vectors):
        ref[...] = turned[i : i + 1, 0:share]


def run_store(pk, owners, rows, total, small):
    vm = pl.BlockSpec(memory_space=pltpu.VMEM)
    shape = jax.ShapeDtypeStruct
    width = small.shape[1]
    h = pk.head_rows
    head = shape((h, 128), F32)
    outs = tuple(shape(r.shape, r.dtype) for r in rows) + (
        head, head, head, shape((pk.row_rows, width), F32), shape((pk.row_rows, pk.ff), F32),
        shape((pk.down_rows, width), F32), head, head, head, head, head,
    ) + (shape((1, width // owners), F32),) * 4
    return pl.pallas_call(
        partial(store_kernel, pk, owners),
        out_shape=outs,
        in_specs=[vm] * 6,
        out_specs=(vm,) * len(outs),
        compiler_params=pltpu.CompilerParams(vmem_limit_bytes=VMEM_LIMIT),
        name="store",
    )(*rows, total, small)


def full_gradients(pk, grads):
    groups, owners = pk.shards * pk.ctxs, pk.shards * pk.ctxs * 4
    by_head = grads.reshape(groups, 4, pk.rows, 128)
    by_owner = grads.reshape(owners, pk.rows, 128)

    def head(name):
        at = pk.heads[name]
        got = by_head[:, :, at : at + pk.head_rows]
        return got.transpose(0, 2, 1, 3).reshape(pk.width, pk.width).astype(F32)

    def rows(at, h, n):
        got = by_owner[:, at : at + h * n].reshape(owners, n, h, 128)
        return got.transpose(0, 2, 1, 3).reshape(owners * h, n * 128).astype(F32)

    return (
        head("wq"), head("wk"), head("wv"),
        rows(pk.at_wo, pk.row_rows, pk.width // 128),
        rows(pk.at_up, pk.row_rows, pk.ff // 128),
        rows(pk.at_down, pk.down_rows, pk.width // 128),
        head("uq"), head("uk"), head("uv"), head("uo").T, head("ugate").T,
    )


def local(
    inputs, first_memory, piece_start, piece_len,
    w_query, w_key, w_value, w_out, w_up, w_down, u_query, u_key, u_value, u_out, u_gate,
    gain_attn, gain_ffn, gain_write, gate_bias, out_grad, memory_grad,
):
    shards, ctxs, tps = (lax.axis_size(a) for a in ("shard", "ctx", "tp"))
    seqs, tokens, width = inputs.shape
    ff = w_up.shape[1]
    assert seqs == tps == 4 and tokens == width == 512 and ff == 2048
    weights = (w_query, w_key, w_value, w_out, w_up, w_down, u_query, u_key, u_value, u_out, u_gate)
    gains = [v.reshape(1, -1) for v in (gain_attn, gain_ffn, gain_write, gate_bias)]
    owners = shards * ctxs * tps
    direct = ctxs == 2 and width % (owners * 16) == 0
    halved = ctxs == 2 and w_query.shape[0] % 32 == 0
    pk = Packing(shards if direct else 4, 2, width, ff)
    got = run_step(
        (shards, ctxs, halved), pk, direct, piece_start.T, piece_len.T, inputs, first_memory, memory_grad,
        out_grad, weights, gains,
    )
    if direct:
        out = run_store(pk, owners, got[:4], got[4], got[5])
        return out[:13] + (out[13].T, out[14].T) + tuple(v.reshape(-1) for v in out[15:])
    every = ("shard", "ctx", "tp")
    out = list(got[:4])
    for i, g in enumerate(full_gradients(pk, got[4])):
        if i in (3, 4, 5):
            out.append(lax.psum_scatter(g, every, scatter_dimension=0, tiled=True))
            continue
        sum_dim = 1 if i >= 9 else 0
        cut = lax.psum_scatter(g, "tp", scatter_dimension=1 - sum_dim, tiled=True)
        out.append(lax.psum_scatter(cut, ("shard", "ctx"), scatter_dimension=sum_dim, tiled=True))
    for i in range(4):
        out.append(lax.psum_scatter(got[5][i], every, scatter_dimension=0, tiled=True))
    return tuple(out)


def solution(mesh):
    cut = P(("shard", "tp"), None)
    head, rows, turned = P(("shard", "ctx"), "tp"), P(("shard", "ctx", "tp"), None), P("tp", ("shard", "ctx"))
    vector = P(("shard", "ctx", "tp"))
    over_rows, over_ctx = P("shard", ("ctx", "tp"), None), P("shard", "ctx", None)
    return jax.shard_map(
        local,
        mesh=mesh,
        in_specs=(over_ctx, P("shard", None, None), P("shard", "ctx"), P("shard", "ctx"))
        + (cut,) * 11 + (P(),) * 4 + (over_rows, over_ctx),
        out_specs=(over_rows, over_ctx, over_rows, over_ctx)
        + (head,) * 3 + (rows,) * 3 + (head,) * 3 + (turned,) * 2 + (vector,) * 4,
        check_vma=False,
    )
```

```python
from functools import partial

import jax
import jax.numpy as jnp
from jax import lax
from jax.experimental import pallas as pl
from jax.experimental.pallas import tpu as pltpu
from jax.sharding import PartitionSpec as P

F32 = jnp.float32
BF = jnp.bfloat16
MESH = pl.DeviceIdType.MESH
HEAD = 64
EPS = 1e-05
NEG = -1e30
VMEM_LIMIT = 67000000

WQ, WK, WV, WO, WUP, WDOWN, UQ, UK, UV, UO, UGATE = 0, 1, 2, 3, 4, 8, 12, 13, 14, 15, 16
TILES = 17


def dot(a, b):
    return lax.dot_general(a, b, (((1,), (0,)), ((), ())), preferred_element_type=F32)


def dot_nt(a, b):
    return lax.dot_general(a, b, (((1,), (1,)), ((), ())), preferred_element_type=F32)


def dot_tn(a, b):
    return lax.dot_general(a, b, (((0,), (0,)), ((), ())), preferred_element_type=F32)


def rows_at(i, size):
    return pl.ds(pl.multiple_of(i * size, size), size)


def loop(count, unroll=1):
    def run(body):
        def step(i, carry):
            body(i)
            return carry

        lax.fori_loop(0, count, step, 0, unroll=unroll)

    return run


BLOCK = 64
UNROLL = 4


def blocks(total, body, carry=None):
    def step(n, carry):
        for k in range(UNROLL):
            i = n * UNROLL + k
            carry = body(rows_at(i, BLOCK), i, carry)
        return carry

    return lax.fori_loop(0, total // (BLOCK * UNROLL), step, carry)


def fold(values):
    return jnp.sum(values.reshape(values.shape[0] // 8, 8, values.shape[1]), axis=0)


def normed(v):
    mean = jnp.mean(v, axis=-1, keepdims=True)
    centered = v - mean
    inv = lax.rsqrt(jnp.mean(centered * centered, axis=-1, keepdims=True) + EPS)
    return centered * inv, inv


def norm_pull(e, gain, hat, inv):
    h = e * gain
    m0 = jnp.mean(h, axis=-1, keepdims=True)
    m1 = jnp.mean(h * hat, axis=-1, keepdims=True)
    return inv * (h - m0 - hat * m1)


def lane_block(width, block):
    return lax.broadcasted_iota(jnp.int32, (1, width), 1) // block


class Weights:
    def __init__(self, ref):
        self.ref = ref
        self.blocks, _, self.rows, self.width = ref.shape

    def cols(self, tile, start, size):
        got = self.ref[:, tile, :, pl.ds(start, size)]
        return got.reshape(self.blocks * self.rows, size)

    def row_part(self, tile, part, parts):
        count = self.blocks // parts
        got = self.ref[pl.ds(part * count, count), tile]
        return got.reshape(count * self.rows, self.width)

    def down_cols(self, chunk, chunks, start, size):
        count = self.blocks // chunks
        got = self.ref[pl.ds(chunk * count, count), WDOWN : WDOWN + 4, :, pl.ds(start, size)]
        return got.reshape(count * 4 * self.rows, size)

    def down_rows(self, part, parts):
        count = self.blocks // parts
        got = self.ref[pl.ds(part * count, count), WDOWN : WDOWN + 4]
        return got.reshape(count * 4 * self.rows, self.width)


def unit_scratch(tokens, slots, width, ff):
    r = tokens + slots
    heads = width // HEAD
    quads = width // 256
    v = pltpu.VMEM
    return dict(
        mem=v((slots, width), F32),
        xh=v((r, width), F32),
        xr=v((r, 1), F32),
        enc=v((r, width), BF),
        q=v((tokens, width), BF),
        k=v((r, width), BF),
        v=v((r, width), BF),
        kt=v((width, r), BF),
        vt=v((width, r), BF),
        pt=v((heads, r, tokens), BF),
        mixt=v((width, tokens), BF),
        af=v((tokens, width), F32),
        ah=v((tokens, width), F32),
        ar=v((tokens, 1), F32),
        fin=v((tokens, width), BF),
        act=v((ff // 512, tokens, 512), BF),
        dg=v((ff // 512, tokens, 512), BF),
        yh=v((tokens, width), F32),
        yr=v((tokens, 1), F32),
        wri=v((r, width), BF),
        sq=v((slots, width), BF),
        sk=v((r, width), BF),
        sv=v((r, width), BF),
        spt=v((quads, r, 256), BF),
        wrt=v((slots, width), BF),
        gate=v((slots, width), F32),
        f1=v((slots, width), F32),
        f2=v((slots, width), F32),
        gm=v((slots, width), F32),
        gup=v((slots, width), BF),
        ggl=v((slots, width), BF),
        dsq=v((slots, width), BF),
        dsk=v((r, width), BF),
        dsv=v((r, width), BF),
        e=v((r, width), F32),
        gy=v((tokens, width), F32),
        gyb=v((tokens, width), BF),
        bwm=v((slots, width), F32),
        gpre=v((ff // 512, tokens, 512), BF),
        gab=v((tokens, width), BF),
        gmx=v((tokens, width), BF),
        dst=v((2, r, tokens), BF),
        dqt=v((width, tokens), BF),
        dq=v((tokens, width), BF),
        dk=v((r, width), BF),
        dv=v((r, width), BF),
    )


class Unit:
    def __init__(self, refs, w, x, gains, small):
        self.__dict__.update(refs)
        self.w = w
        self.x = x
        self.gains = gains
        self.small = small
        self.tokens, self.width = x.shape
        self.slots = self.mem.shape[0]
        self.r = self.tokens + self.slots
        self.ff = self.act.shape[0] * 512

    def gain(self, i):
        return self.gains[i][...]

    def make_bias(self, first, length):
        t = self.tokens

        @loop(t // 64)
        def _(i):
            key = lax.broadcasted_iota(jnp.int32, (64, t), 0) + i * 64
            query = lax.broadcasted_iota(jnp.int32, (64, t), 1)
            last = first + length
            inside = (key >= first) & (key < last) & (query >= first) & (query < last)
            seen = (key <= query) | inside
            self.e[rows_at(i, 64), :] = jnp.where(seen, 0.0, NEG).astype(F32)

    def norm_in(self, rows, values):
        hat, inv = normed(values)
        self.xh[rows, :] = hat
        self.xr[rows, :] = inv
        self.enc[rows, :] = (hat * self.gain(0)).astype(BF)

    def tokens_in(self):
        def body(rows, i, carry):
            self.norm_in(rows, self.x[rows, :].astype(F32))

        blocks(self.tokens, body)

    def project_tokens(self):
        t = self.tokens

        @loop(self.width // 256)
        def _(n):
            cols = rows_at(n, 256)
            enc = self.enc[0:t, :]
            got = dot(enc, self.w.cols(WQ, n * 256, 256)).astype(BF)
            self.q[:, cols] = got * BF(HEAD**-0.5)
            self.k[0:t, cols] = dot(enc, self.w.cols(WK, n * 256, 256)).astype(BF)
            self.v[0:t, cols] = dot(enc, self.w.cols(WV, n * 256, 256)).astype(BF)

    def memory_in(self):
        t, r = self.tokens, self.r
        self.norm_in(slice(t, r), self.mem[...])
        enc = self.enc[t:r, :]
        self.k[t:r, :] = dot(enc, self.w.cols(WK, 0, self.width)).astype(BF)
        self.v[t:r, :] = dot(enc, self.w.cols(WV, 0, self.width)).astype(BF)
        self.vt[...] = self.v[...].T

    def attend(self, first, count):
        t, r = self.tokens, self.r

        @loop(count)
        def _(i):
            p = i + first
            cols = rows_at(p, 128)
            keys = self.k[:, cols]
            half = lane_block(128, HEAD)
            for hh in range(2):
                feats = pl.ds(pl.multiple_of(p * 128 + hh * HEAD, HEAD), HEAD)
                values = self.vt[feats, :]
                for n in range(t // 256):
                    qc = slice(n * 256, n * 256 + 256)
                    q = self.q[qc, cols]
                    q = jnp.where(half == hh, q, jnp.zeros_like(q))
                    s = dot_nt(keys, q)
                    s_tok = s[0:t] + self.e[0:t, qc]
                    s_mem = s[t:r]
                    peak = jnp.maximum(
                        jnp.max(s_tok, axis=0, keepdims=True), jnp.max(s_mem, axis=0, keepdims=True)
                    )
                    e_tok = jnp.exp(s_tok - peak)
                    e_mem = jnp.exp(s_mem - peak)
                    inv = 1.0 / (
                        jnp.sum(e_tok, axis=0, keepdims=True)
                        + jnp.sum(e_mem, axis=0, keepdims=True)
                    )
                    probs = jnp.concatenate([e_tok * inv, e_mem * inv], axis=0).astype(BF)
                    self.pt[2 * p + hh, :, qc] = probs
                    self.mixt[feats, qc] = dot(values, probs).astype(BF)

    def after_attention(self):
        t = self.tokens
        self.gmx[...] = self.mixt[...].T

        @loop(self.width // 256)
        def _(n):
            cols = rows_at(n, 256)
            got = dot(self.gmx[...], self.w.cols(WO, n * 256, 256))
            self.af[:, cols] = self.x[:, cols].astype(F32) + got

        def body(rows, i, carry):
            hat, inv = normed(self.af[rows, :])
            self.ah[rows, :] = hat
            self.ar[rows, :] = inv
            self.fin[rows, :] = (hat * self.gain(1)).astype(BF)

        blocks(t, body)

    def feed_forward_up(self):
        t = self.tokens
        for j in range(self.ff // 512):

            @loop(2)
            def _(n, j=j):
                cols = rows_at(n, 256)
                weights = self.w.cols(WUP + j, n * 256, 256)
                for m in range(t // 128):
                    rows = slice(m * 128, m * 128 + 128)
                    pre = dot(self.fin[rows, :], weights)
                    c = 0.7978845608028654
                    sq = pre * pre
                    th = jnp.tanh(pre * (c + (c * 0.044715) * sq))
                    half = 0.5 + 0.5 * th
                    self.act[j, rows, cols] = (pre * half).astype(BF)
                    slope = half + (0.5 * pre) * (1.0 - th * th) * (c + (3 * c * 0.044715) * sq)
                    self.dg[j, rows, cols] = slope.astype(BF)

    def feed_forward_down(self):
        t = self.tokens

        @loop(self.width // 256)
        def _(n):
            cols = rows_at(n, 256)
            total = self.af[:, cols]
            for j in range(self.ff // 512):
                total = total + dot(
                    self.act[j], self.w.down_cols(j, self.ff // 512, n * 256, 256)
                )
            self.af[:, cols] = total

        def body(rows, i, carry):
            hat, inv = normed(self.af[rows, :])
            self.yh[rows, :] = hat
            self.yr[rows, :] = inv
            self.wri[rows, :] = (hat * self.gain(2)).astype(BF)

        blocks(t, body)

        self.wri[t : self.r, :] = (self.xh[t : self.r, :] * self.gain(2)).astype(BF)

    def spread_heads(self, rows, g):
        part = rows[:, g * 256 : g * 256 + 256]
        block = lane_block(256, HEAD)
        return jnp.concatenate(
            [jnp.where(block == h, part, jnp.zeros_like(part)) for h in range(4)], axis=0
        )

    def gather_heads(self, stacked):
        block = lane_block(256, HEAD)
        s = self.slots
        total = jnp.where(block == 0, stacked[0:s], 0.0)
        for h in range(1, 4):
            total = total + jnp.where(block == h, stacked[h * s : h * s + s], 0.0)
        return total

    def write_memory(self):
        t, r = self.tokens, self.r

        @loop(self.width // 256)
        def _(n):
            cols = rows_at(n, 256)
            wri = self.wri[...]
            self.sk[:, cols] = dot(wri, self.w.cols(UK, n * 256, 256)).astype(BF)
            self.sv[:, cols] = dot(wri, self.w.cols(UV, n * 256, 256)).astype(BF)

        wm = self.wri[t:r, :]
        sq = dot(wm, self.w.cols(UQ, 0, self.width)).astype(BF)
        self.sq[...] = sq * BF(HEAD**-0.5)
        for g in range(self.width // 256):
            cols = slice(g * 256, g * 256 + 256)
            s = dot_nt(self.sk[:, cols], self.spread_heads(self.sq[...], g))
            e = jnp.exp(s - jnp.max(s, axis=0, keepdims=True))
            probs = (e * (1.0 / jnp.sum(e, axis=0, keepdims=True))).astype(BF)
            self.spt[g] = probs
            self.wrt[:, cols] = self.gather_heads(dot_tn(probs, self.sv[:, cols])).astype(BF)
        th = jnp.tanh(dot(self.wrt[...], self.w.cols(UO, 0, self.width)))
        pre = dot(wm, self.w.cols(UGATE, 0, self.width))
        gate = jax.nn.sigmoid(pre + self.gain(3))
        mem = self.mem[...]
        self.gate[...] = gate
        self.f1[...] = (mem - th) * gate * (1.0 - gate)
        self.f2[...] = (1.0 - gate) * (1.0 - th * th)
        return gate * mem + (1.0 - gate) * th

    def backward_early(self):
        self.kt[...] = self.k[...].T

    def write_back(self, out_grad):
        t, r, s = self.tokens, self.r, self.slots
        gm = self.gm[...]
        ggp = gm * self.f1[...]
        gup = (gm * self.f2[...]).astype(BF)
        ggl = ggp.astype(BF)
        self.gup[...] = gup
        self.ggl[...] = ggl
        self.small[3:4, :] = jnp.sum(ggp, axis=0, keepdims=True)
        gwr = dot_nt(gup, self.w.row_part(UO, 0, 1)).astype(BF)
        for g in range(self.width // 256):
            cols = slice(g * 256, g * 256 + 256)
            grads = self.spread_heads(gwr, g)
            dp = dot_nt(self.sv[:, cols], grads)
            probs = self.spt[g]
            pf = probs.astype(F32)
            ds = (pf * (dp - jnp.sum(pf * dp, axis=0, keepdims=True))).astype(BF)
            self.dsv[:, cols] = dot(probs, grads).astype(BF)
            self.dsk[:, cols] = dot(ds, self.spread_heads(self.sq[...], g)).astype(BF)
            dq = self.gather_heads(dot_tn(ds, self.sk[:, cols])) * HEAD**-0.5
            self.dsq[:, cols] = dq.astype(BF)

        @loop(2)
        def _(n):
            cols = rows_at(n, self.width // 2)
            self.e[:, cols] = dot_nt(self.dsk[...], self.w.row_part(UK, n, 2)) + dot_nt(
                self.dsv[...], self.w.row_part(UV, n, 2)
            )

        em = self.e[t:r, :] + dot_nt(self.dsq[...], self.w.row_part(UQ, 0, 1))
        em = em + dot_nt(ggl, self.w.row_part(UGATE, 0, 1))
        hat = self.xh[t:r, :]
        self.bwm[...] = norm_pull(em, self.gain(2), hat, self.xr[t:r, :])

        def body(rows, i, carry):
            e = self.e[rows, :]
            hat = self.yh[rows, :]
            grad = out_grad(i) + norm_pull(e, self.gain(2), hat, self.yr[rows, :])
            self.gy[rows, :] = grad
            self.gyb[rows, :] = grad.astype(BF)
            return carry + fold(e * hat)

        total = blocks(t, body, fold(em * hat))
        self.small[2:3, :] = jnp.sum(total, axis=0, keepdims=True)

    def feed_forward_back(self):
        t = self.tokens
        chunks = self.ff // 512

        for j in range(chunks):

            @loop(2)
            def _(n, j=j):
                cols = rows_at(n, 256)
                weights = self.w.down_rows(2 * j + n, 2 * chunks)
                for m in range(t // 128):
                    rows = slice(m * 128, m * 128 + 128)
                    got = dot_nt(self.gyb[rows, :], weights)
                    self.gpre[j, rows, cols] = (got * self.dg[j, rows, cols].astype(F32)).astype(BF)

    def feed_forward_enter(self):
        t = self.tokens
        chunks = self.ff // 512

        @loop(2)
        def _(n):
            cols = rows_at(n, self.width // 2)
            total = dot_nt(self.gpre[0], self.w.row_part(WUP, n, 2))
            for j in range(1, chunks):
                total = total + dot_nt(self.gpre[j], self.w.row_part(WUP + j, n, 2))
            self.e[0:t, cols] = total

        def body(rows, i, carry):
            e = self.e[rows, :]
            hat = self.ah[rows, :]
            grad = self.gy[rows, :] + norm_pull(e, self.gain(1), hat, self.ar[rows, :])
            self.gy[rows, :] = grad
            self.gab[rows, :] = grad.astype(BF)
            return carry + fold(e * hat)

        total = blocks(t, body, jnp.zeros((8, self.width), F32))
        self.small[1:2, :] = jnp.sum(total, axis=0, keepdims=True)

    def project_back(self):
        @loop(2)
        def _(n):
            cols = rows_at(n, self.width // 2)
            self.gmx[:, cols] = dot_nt(self.gab[...], self.w.row_part(WO, n, 2)).astype(BF)

    def attend_back(self, first, count):
        t, r = self.tokens, self.r

        @loop(count)
        def _(i):
            p = i + first
            cols = rows_at(p, 128)
            values = self.v[:, cols]
            half = lane_block(128, HEAD)
            for hh in range(2):
                feats = pl.ds(pl.multiple_of(p * 128 + hh * HEAD, HEAD), HEAD)
                keys = self.kt[feats, :]
                for n in range(t // 256):
                    qc = slice(n * 256, n * 256 + 256)
                    g = self.gmx[qc, cols]
                    g = jnp.where(half == hh, g, jnp.zeros_like(g))
                    dp = dot_nt(values, g)
                    pf = self.pt[2 * p + hh, :, qc].astype(F32)
                    ds = (pf * (dp - jnp.sum(pf * dp, axis=0, keepdims=True))).astype(BF)
                    self.dst[hh, :, qc] = ds
                    self.dqt[feats, qc] = (dot(keys, ds) * HEAD**-0.5).astype(BF)
            g = self.gmx[:, cols]
            q = self.q[:, cols]
            dv = jnp.where(half == 0, dot(self.pt[2 * p], g), dot(self.pt[2 * p + 1], g))
            self.dv[:, cols] = dv.astype(BF)
            dk = jnp.where(half == 0, dot(self.dst[0], q), dot(self.dst[1], q))
            self.dk[:, cols] = dk.astype(BF)

    def queries_back(self):
        self.dq[...] = self.dqt[...].T

    def enter_back(self):
        t = self.tokens

        @loop(2)
        def _(n):
            cols = rows_at(n, self.width // 2)
            self.e[:, cols] = dot_nt(self.dk[...], self.w.row_part(WK, n, 2)) + dot_nt(
                self.dv[...], self.w.row_part(WV, n, 2)
            )
            self.e[0:t, cols] += dot_nt(self.dq[...], self.w.row_part(WQ, n, 2))

    def norm_enter(self, input_grad):
        t, r = self.tokens, self.r
        e = self.e[t:r, :]
        hat = self.xh[t:r, :]
        first = fold(e * hat)
        mem_grad = self.gm[...] * self.gate[...] + self.bwm[...]
        mem_grad = mem_grad + norm_pull(e, self.gain(0), hat, self.xr[t:r, :])

        def body(rows, i, carry):
            e = self.e[rows, :]
            hat = self.xh[rows, :]
            grad = self.gy[rows, :] + norm_pull(e, self.gain(0), hat, self.xr[rows, :])
            input_grad[rows, :] = grad.astype(BF)
            return carry + fold(e * hat)

        total = blocks(t, body, first)
        self.small[0:1, :] = jnp.sum(total, axis=0, keepdims=True)

        return mem_grad


class Packing:
    def __init__(self, shards, ctxs, width, ff):
        self.shards, self.ctxs, self.width, self.ff = shards, ctxs, width, ff
        self.head_rows = h = width // (shards * ctxs)
        self.row_rows = width // (shards * ctxs * 4)
        self.down_rows = ff // (shards * ctxs * 4)
        self.at_down = 0
        at = self.down_rows * (width // 128)
        self.heads = {}
        for name in ("uq", "uk", "uv", "uo", "ugate"):
            self.heads[name] = at
            at += h
        self.at_up = at
        self.at_wo = at + self.row_rows * (ff // 128)
        last = at = self.at_wo + self.row_rows * (width // 128)
        for name in ("wq", "wk", "wv"):
            self.heads[name] = at
            at += h
        self.rows = at
        middle = last + (at - last) // 2 // 16 * 16
        bounds = (0, self.heads["uq"], self.at_up, self.at_wo, last, middle, at)
        self.chunks = tuple(zip(bounds[:-1], bounds[1:]))

    @property
    def shape(self):
        return (self.shards, self.ctxs, 2, 2, self.rows, 128)


def weight_grads(u, g, pk, names):
    width = u.width
    tile = 256

    def store_head(at, m, got):
        h = pk.head_rows
        per = tile // h
        for i in range(per):
            s = m * (per // pk.ctxs) + i // pk.ctxs
            for t in range(4):
                g[s, i % pk.ctxs, t // 2, t % 2, at : at + h, :] = got[
                    i * h : i * h + h, t * 128 : t * 128 + 128
                ]

    def store_rows(at, h, m, got, chunk0):
        per = tile // h
        for i in range(per):
            if per % (pk.ctxs * 4) == 0:
                s, c = m * (per // (pk.ctxs * 4)) + i // (pk.ctxs * 4), (i // 4) % pk.ctxs
            else:
                owner = m * (per // 4) + i // 4
                s, c = lax.div(owner, pk.ctxs), lax.rem(owner, pk.ctxs)
            for j in range(got.shape[1] // 128):
                lo = at + (chunk0 + j) * h
                g[s, c, (i // 2) % 2, i % 2, lo : lo + h, :] = got[
                    i * h : i * h + h, j * 128 : j * 128 + 128
                ]

    def head(name, left, right):
        at = pk.heads[name]

        @loop(width // tile)
        def _(m):
            lt = left[:, rows_at(m, tile)].T
            store_head(at, m, dot(lt, right[...]).astype(BF))

    t, r = u.tokens, u.r
    if "down" in names:
        for j in range(u.ff // 512):

            @loop(512 // tile)
            def _(m, j=j):
                lt = u.act[j, :, rows_at(m, tile)].T
                got = dot(lt, u.gyb[...]).astype(BF)
                store_rows(pk.at_down, pk.down_rows, m + j * (512 // tile), got, 0)

    if "up" in names:

        @loop(width // tile)
        def _(m):
            lt = u.fin[:, rows_at(m, tile)].T
            for j in range(u.ff // 512):
                store_rows(pk.at_up, pk.row_rows, m, dot(lt, u.gpre[j]).astype(BF), 4 * j)

    if "wo" in names:

        @loop(width // tile)
        def _(m):
            got = dot(u.mixt[rows_at(m, tile), :], u.gab[...]).astype(BF)
            store_rows(pk.at_wo, pk.row_rows, m, got, 0)

    if "write" in names:
        head("uq", u.wri.at[t:r], u.dsq)
        head("uk", u.wri, u.dsk)
        head("uv", u.wri, u.dsv)
        head("uo", u.gup, u.wrt)
        head("ugate", u.ggl, u.wri.at[t:r])
    if "enter" in names:
        head("wq", u.enc.at[0:t], u.dq)
        head("wk", u.enc, u.dk)
        head("wv", u.enc, u.dv)


GROUPS = ((0, 3), (3, 8), (8, 12), (12, 17))


def greet(peers):
    barrier = pltpu.get_barrier_semaphore()
    count = 0
    for cond, device in peers:

        @pl.when(cond)
        def _(device=device):
            pl.semaphore_signal(barrier, inc=1, device_id=device, device_id_type=MESH)

        count = count + jnp.where(cond, 1, 0)
    pl.semaphore_wait(barrier, count)


class Gather:
    UP, DOWN, ACROSS, BESIDE, FAR, PAIR, PAIR_ACROSS, PAIR_BESIDE, PAIR_FAR = range(9)
    LINKS = {ACROSS: 0, BESIDE: 1, FAR: 2, PAIR: 3, PAIR_ACROSS: 3, PAIR_BESIDE: 3, PAIR_FAR: 3}

    def __init__(self, shards, halved, w, send, line_send, recv, pair_recv):
        self.n, self.halved, self.w = shards, halved, w
        self.send, self.line_send, self.recv, self.pair_recv = send, line_send, recv, pair_recv
        self.s, self.c, self.t = (lax.axis_index(a) for a in ("shard", "ctx", "tp"))
        odd = lax.rem(self.t, 2)
        self.pair_tp = self.t + 1 - 2 * odd
        self.across_tp = lax.rem(self.t + 2, 4)
        self.pair = {"tp": self.pair_tp}
        self.across = {"tp": self.across_tp}
        self.beside = {"ctx": self.c + 1 - 2 * lax.rem(self.c, 2)}

    def copy(self, kind, source, tp, g, device, half=None):
        lo, hi = GROUPS[g]
        block = self.w.at[source * 4 + tp, lo:hi]
        if half is not None:
            size = self.w.shape[2] // 2
            block = self.w.at[source * 4 + tp, lo:hi, pl.ds(pl.multiple_of(half * size, size), size)]
        return self.between(block, kind, source, g, device)

    def between(self, block, kind, source, g, device):
        if kind in (self.UP, self.DOWN):
            send = self.line_send.at[kind, source]
        else:
            send = self.send.at[self.LINKS[kind]]
        to_pair = kind in (self.PAIR, self.PAIR_ACROSS, self.PAIR_BESIDE, self.PAIR_FAR)
        recv = self.pair_recv.at[g] if to_pair else self.recv.at[kind, source, g]
        return pltpu.make_async_remote_copy(
            src_ref=block, dst_ref=block, send_sem=send, recv_sem=recv, device_id=device, device_id_type=MESH,
        )

    @property
    def mine(self):
        return self.c if self.halved else None

    @property
    def others(self):
        return 1 - self.c

    def up(self, source, g, far):
        return self.copy(self.UP, source, self.t, g, {"shard": self.s + 1}, self.mine if far else None)

    def down(self, source, g, far):
        return self.copy(self.DOWN, source, self.t, g, {"shard": self.s - 1}, self.mine if far else None)

    def to_across(self, source, g, tp=None):
        return self.copy(self.ACROSS, source, self.t if tp is None else tp, g, self.across, self.mine)

    def to_pair(self, source, g, far, tp=None):
        return self.copy(self.PAIR, source, self.t if tp is None else tp, g, self.pair, self.mine if far else None)

    def far(self, d):
        return self.halved and d == self.n - 1

    def start_own(self, g):
        s, n = self.s, self.n
        if n > 1:

            @pl.when(s < n - 1)
            def _():
                self.up(s, g, self.far(1)).start()

            @pl.when(s > 0)
            def _():
                self.down(s, g, self.far(1)).start()

        self.to_across(s, g).start()
        self.to_pair(s, g, False).start()

    def came(self, source, g, d):
        self.to_across(source, g).start()
        self.to_pair(source, g, self.far(d)).start()
        if self.far(d):
            self.copy(self.FAR, source, self.t, g, self.beside, self.c).start()

    def line_step(self, d, g):
        s, n = self.s, self.n

        @pl.when(s - d >= 0)
        def _():
            self.up(s - d, g, self.far(d)).wait_recv()

            @pl.when(s < n - 1)
            def _():
                self.up(s - d, g, self.far(d + 1)).start()

            self.came(s - d, g, d)

        @pl.when(s + d <= n - 1)
        def _():
            self.down(s + d, g, self.far(d)).wait_recv()

            @pl.when(s > 0)
            def _():
                self.down(s + d, g, self.far(d + 1)).start()

            self.came(s + d, g, d)

    def sources(self, d):
        s, n = self.s, self.n
        both = ((s - d, s - d >= 0), (s + d, s + d <= n - 1))
        return both[:1] if d == 0 else both

    def across_step(self, d, g):
        for source, cond in self.sources(d):

            @pl.when(cond)
            def _(source=source):
                tp = self.across_tp
                self.to_across(source, g, tp).wait_recv()
                self.copy(self.PAIR_ACROSS, source, tp, g, self.pair, self.mine).start()
                if self.halved:
                    self.copy(self.BESIDE, source, tp, g, self.beside, self.c).start()

    def beside_step(self, d, g):
        if not self.halved:
            return
        for source, cond in self.sources(d):

            @pl.when(cond)
            def _(source=source):
                tp = self.across_tp
                self.copy(self.BESIDE, source, tp, g, self.beside, self.others).wait_recv()
                self.copy(self.PAIR_BESIDE, source, tp, g, self.pair, self.others).start()

    def far_step(self, g):
        if not self.halved:
            return
        for source, cond in self.sources(self.n - 1):

            @pl.when(cond)
            def _(source=source):
                self.copy(self.FAR, source, self.t, g, self.beside, self.others).wait_recv()
                self.copy(self.PAIR_FAR, source, self.t, g, self.pair, self.others).start()

    def finish(self, g):
        lo, hi = GROUPS[g]
        self.between(self.w.at[0 : 2 * self.n, lo:hi], self.PAIR, 0, g, self.pair).wait_recv()

    def drain(self):
        s, n = self.s, self.n
        parts = n // 2 if self.halved else n
        half = self.w.at[0, :, 0 : self.w.shape[2] // 2]
        self.between(self.w.at[0 : 2 * n], self.PAIR, 0, 0, self.pair).wait_send()
        self.between(self.w.at[0:parts], self.ACROSS, 0, 0, self.across).wait_send()
        if self.halved:
            self.between(self.w.at[0:parts], self.BESIDE, 0, 0, self.beside).wait_send()

            @pl.when(jnp.logical_or(s == 0, s == n - 1))
            def _():
                self.between(half, self.FAR, 0, 0, self.beside).wait_send()

        for d in range(n - 1):
            block = half if self.far(d + 1) else self.w.at[0]

            @pl.when(jnp.logical_and(s - d >= 0, s < n - 1))
            def _(d=d, block=block):
                self.between(block, self.UP, s - d, 0, {"shard": s + 1}).wait_send()

            @pl.when(jnp.logical_and(s + d <= n - 1, s > 0))
            def _(d=d, block=block):
                self.between(block, self.DOWN, s + d, 0, {"shard": s - 1}).wait_send()

    def events(self, time, ready):
        n = self.n
        groups = range(len(GROUPS))
        for g in groups:
            if time == max(2 * g - 2, 0):
                ready(g)
                self.start_own(g)
        for g in groups:
            d = time - 2 * g
            if 1 <= d <= n - 1:
                self.line_step(d, g)
            if 0 <= d - 1 <= n - 1:
                self.across_step(d - 1, g)
            if 0 <= d - 2 <= n - 1:
                self.beside_step(d - 2, g)
            if d == n + 1:
                self.far_step(g)
                self.finish(g)

    @property
    def last(self):
        return 2 * (len(GROUPS) - 1) + self.n + 1


def line_peers(n):
    s = lax.axis_index("shard")
    return [(s >= 0, {"shard": lax.rem(s + d, n)}) for d in range(1, n)]


def tp_peers():
    t = lax.axis_index("tp")
    return [(t >= 0, {"tp": lax.rem(t + d, 4)}) for d in (1, 2, 3)]


def own_tiles(weights, w, own, sems):
    names = [WQ, WK, WV, WO, WUP, WDOWN, UQ, UK, UV, UO, UGATE]
    rows = w.shape[2]
    out = []
    for name, ref in zip(names, weights):
        parts = {WUP: 4, WDOWN: 4}.get(name, 1)
        for j in range(parts):
            src = ref
            if name == WUP:
                src = ref.at[:, j * 512 : j * 512 + 512]
            if name == WDOWN:
                src = ref.at[j * rows : j * rows + rows]
            out.append(pltpu.make_async_copy(src, w.at[own, name + j], sems.at[name + j]))
    return out


class Reduce:
    ORDER = (0, 1, 0, 1, 0, 1)

    def __init__(self, shards, chunks, g, r1, r2, r3, z, send, recv):
        self.n = shards
        self.rows = [pl.ds(lo, hi - lo) for lo, hi in chunks]
        self.g, self.r1, self.r2, self.r3, self.z = g, r1, r2, r3, z
        self.send, self.recv = send, recv
        self.s, self.c, self.t = (lax.axis_index(a) for a in ("shard", "ctx", "tp"))
        self.core = lax.rem(self.t, 2)
        self.x = lax.div(self.t, 2)
        self.pair = {"tp": self.t + 1 - 2 * self.core}
        self.across = {"tp": lax.rem(self.t + 2, 4)}
        self.beside = {"ctx": 1 - self.c}

    def copy(self, src, dst, k, kind, device):
        return pltpu.make_async_remote_copy(
            src_ref=src, dst_ref=dst, send_sem=self.send.at[kind], recv_sem=self.recv.at[k, kind],
            device_id=device, device_id_type=MESH,
        )

    def one(self, k):
        rows = self.rows[k]
        return self.copy(self.g.at[:, :, :, 1 - self.core, rows], self.r1.at[:, :, :, rows], k, 0, self.pair)

    def two(self, k):
        rows = self.rows[k]
        if self.ORDER[k] == 0:
            src, device = self.r1.at[:, :, 1 - self.x, rows], self.across
        else:
            src, device = self.r1.at[:, 1 - self.c, :, rows], self.beside
        return self.copy(src, self.r2.at[:, :, rows], k, 1, device)

    def three(self, k):
        rows = self.rows[k]
        if self.ORDER[k] == 0:
            src, device = self.r2.at[:, 1 - self.c, rows], self.beside
        else:
            src, device = self.r2.at[:, 1 - self.x, rows], self.across
        return self.copy(src, self.r3.at[:, rows], k, 2, device)

    def along(self, k, d):
        to = lax.rem(self.s + d, self.n)
        rows = self.rows[k]
        return self.copy(self.r3.at[to, rows], self.z.at[d - 1, rows], k, 2 + d, {"shard": to})

    def start(self, k):
        self.one(k).start()

    def to_second(self, k):
        self.one(k).wait_recv()
        rows = self.rows[k]
        for j in range(2):
            for x in range(2):
                self.r1[:, j, x, rows] += self.g[:, j, x, self.core, rows]
        self.two(k).start()

    def to_third(self, k):
        self.two(k).wait_recv()
        rows = self.rows[k]
        for j in range(2):
            own = self.r1[:, j, self.x, rows] if self.ORDER[k] == 0 else self.r1[:, self.c, j, rows]
            self.r2[:, j, rows] += own
        self.three(k).start()

    def to_last(self, k):
        self.three(k).wait_recv()
        rows = self.rows[k]
        own = self.c if self.ORDER[k] == 0 else self.x
        self.r3[:, rows] += self.r2[:, own, rows]
        for d in range(1, self.n):
            self.along(k, d).start()

    def arrive(self, k, out):
        for d in range(1, self.n):
            self.along(k, d).wait_recv()
        rows = self.rows[k]
        total = self.r3[self.s, rows].astype(F32)
        for d in range(1, self.n):
            total = total + self.z[d - 1, rows].astype(F32)
        out[rows, :] = total.astype(out.dtype)

    def drain(self):
        whole = [(self.r1, 0), (self.r1.at[:, :, 0], 1), (self.r1.at[:, 0, 0], 2)]
        whole += [(self.r3.at[0], 2 + d) for d in range(1, self.n)]
        for ref, kind in whole:
            self.copy(ref, ref, 0, kind, self.pair).wait_send()


class SmallSum:
    def __init__(self, shards, own, got, send, recv):
        self.n, self.own, self.got, self.send, self.recv = shards, own, got, send, recv
        self.s, self.c, self.t = (lax.axis_index(a) for a in ("shard", "ctx", "tp"))

    def copy(self, i):
        near = [{"tp": self.t + 1 - 2 * lax.rem(self.t, 2)}, {"tp": lax.rem(self.t + 2, 4)}, {"ctx": 1 - self.c}]
        device = near[i] if i < 3 else {"shard": lax.rem(self.s + i - 2, self.n)}
        return pltpu.make_async_remote_copy(
            src_ref=self.own.at[min(i, 3)], dst_ref=self.got.at[i], send_sem=self.send.at[i],
            recv_sem=self.recv.at[i], device_id=device, device_id_type=MESH,
        )

    def start(self, value):
        self.own[0] = value
        self.copy(0).start()

    def step(self, i):
        self.copy(i).wait_recv()
        self.own[i + 1] = self.own[i] + self.got[i]
        if i < 2:
            self.copy(i + 1).start()
        else:
            for d in range(1, self.n):
                self.copy(2 + d).start()

    def arrive(self, out):
        total = self.own[3]
        for d in range(1, self.n):
            self.copy(2 + d).wait_recv()
            total = total + self.got[2 + d]
        out[...] = total

    def drain(self):
        for i in range(2 + self.n):
            self.copy(i).wait_send()


class Spread:
    def __init__(self, src, dst, send, recv):
        self.src, self.dst, self.send, self.recv = src, dst, send, recv
        self.t = lax.axis_index("tp")

    def copy(self, d):
        to = lax.rem(self.t + d, 4)
        share = self.dst.shape[1]
        src = self.src.at[pl.ds(pl.multiple_of(to * share, share), share)]
        dst = self.dst.at[self.t]
        if d == 0:
            return pltpu.make_async_copy(src, dst, self.send.at[d])
        return pltpu.make_async_remote_copy(
            src_ref=src, dst_ref=dst, send_sem=self.send.at[d], recv_sem=self.recv.at[d],
            device_id={"tp": to}, device_id_type=MESH,
        )

    def start(self):
        for d in (2, 3, 1, 0):
            self.copy(d).start()

    def finish(self):
        for d in (1, 2, 3):
            self.copy(d).wait_recv()
            self.copy(d).wait_send()
        self.copy(0).wait()


class Share:
    def __init__(self, held, send, recv):
        self.held, self.send, self.recv = held, send, recv
        self.t = lax.axis_index("tp")
        self.pair_tp = self.t + 1 - 2 * lax.rem(self.t, 2)
        self.across_tp = lax.rem(self.t + 2, 4)

    def copy(self, i, tp, to):
        return pltpu.make_async_remote_copy(
            src_ref=self.held.at[tp], dst_ref=self.held.at[tp], send_sem=self.send.at[i],
            recv_sem=self.recv.at[i], device_id={"tp": to}, device_id_type=MESH,
        )

    def start(self):
        self.copy(0, self.t, self.across_tp).start()
        self.copy(1, self.t, self.pair_tp).start()

    def relay(self):
        self.copy(0, self.across_tp, self.across_tp).wait_recv()
        self.copy(2, self.across_tp, self.pair_tp).start()

    def finish(self):
        self.copy(1, self.pair_tp, self.pair_tp).wait_recv()
        self.copy(2, lax.rem(self.pair_tp + 2, 4), self.pair_tp).wait_recv()
        self.copy(0, self.t, self.across_tp).wait_send()
        self.copy(1, self.t, self.pair_tp).wait_send()
        self.copy(2, self.across_tp, self.pair_tp).wait_send()


class Comm:
    pass


def step_scratch(shards, pk, direct, tokens, slots, width):
    v, dma = pltpu.VMEM, pltpu.SemaphoreType.DMA
    n = shards
    out = dict(
        w=v((n * 4, TILES, width // (n * 4), width), BF),
        x=v((tokens, width), BF),
        m0=v((slots, width), F32),
        og=v((4, tokens // 4, width), BF),
        y=v((tokens, width), BF),
        xg=v((tokens, width), BF),
        mems=v((4, slots, width), BF),
        migs=v((4, slots, width), BF),
        small=v((8, width), F32),
        m_send=v((slots, width), BF),
        m_recv=v((slots, width), BF),
        g_send=v((slots, width), BF),
        g_recv=v((slots, width), BF),
        chain=dma((4,)),
        loads=dma((3,)),
        local=dma((TILES,)),
        w_send=dma((4,)),
        w_line_send=dma((2, n)),
        w_recv=dma((5, n, len(GROUPS))),
        w_pair_recv=dma((len(GROUPS),)),
        og_send=dma((4,)),
        og_recv=dma((4,)),
        y_send=dma((4,)),
        y_recv=dma((4,)),
        xg_send=dma((4,)),
        xg_recv=dma((4,)),
        mem_send=dma((3,)),
        mem_recv=dma((3,)),
        mig_send=dma((3,)),
        mig_recv=dma((3,)),
    )
    if direct:
        c = len(pk.chunks)
        out.update(
            g=v(pk.shape, BF),
            r1=v((n, 2, 2, pk.rows, 128), BF),
            r2=v((n, 2, pk.rows, 128), BF),
            r3=v((n, pk.rows, 128), BF),
            z=v((n - 1, pk.rows, 128), BF),
            own=v((4, 8, width), F32),
            got=v((2 + n, 8, width), F32),
            r_send=dma((2 + n,)),
            r_recv=dma((c, 2 + n)),
            s_send=dma((2 + n,)),
            s_recv=dma((2 + n,)),
        )
    return out


def step_kernel(dims, pk, direct, names, unit_names, *refs):
    shards, ctxs, halved = dims
    first, length, inputs, first_memory, memory_grad, out_grad = refs[:6]
    weights, gains, outs = refs[6:17], refs[17:21], refs[21:27]
    scratch = refs[27:]
    b = Comm()
    b.__dict__.update(zip(names, scratch))
    unit_refs = dict(zip(unit_names, scratch[len(names) :]))
    if not direct:
        b.g = outs[4]
    s, c, t = (lax.axis_index(a) for a in ("shard", "ctx", "tp"))
    u = Unit(unit_refs, Weights(b.w), b.x, gains, b.small)

    loads = [
        pltpu.make_async_copy(inputs.at[t], b.x, b.loads.at[0]),
        pltpu.make_async_copy(first_memory.at[t], b.m0, b.loads.at[1]),
        pltpu.make_async_copy(memory_grad.at[t], u.gm, b.loads.at[2]),
    ]
    copies = own_tiles(weights, b.w, s * 4 + t, b.local)
    for copy in copies + loads:
        copy.start()
    mine = pltpu.make_async_copy(out_grad.at[t], b.og.at[t], b.og_send.at[0])
    mine.start()
    peers = line_peers(shards) + tp_peers()
    if ctxs > 1:
        peers += [(c > 0, {"ctx": c - 1}), (c < ctxs - 1, {"ctx": c + 1})]
    greet(peers)
    gather = Gather(shards, halved, b.w, b.w_send, b.w_line_send, b.w_recv, b.w_pair_recv)

    def ready(g):
        for copy in copies[GROUPS[g][0] : GROUPS[g][1]]:
            copy.wait()

    def gather_until(start, stop):
        for time in range(start, stop):
            gather.events(time, ready)

    def chain_copy(i, to):
        src, dst = ((b.m_send, b.m_recv), (b.g_send, b.g_recv))[i]
        return pltpu.make_async_remote_copy(
            src_ref=src, dst_ref=dst, send_sem=b.chain.at[2 * i], recv_sem=b.chain.at[2 * i + 1],
            device_id={"ctx": to}, device_id_type=MESH,
        )

    def og_copy(d):
        to = lax.rem(t + d, 4)
        return pltpu.make_async_remote_copy(
            src_ref=out_grad.at[to], dst_ref=b.og.at[t], send_sem=b.og_send.at[d],
            recv_sem=b.og_recv.at[d], device_id={"tp": to}, device_id_type=MESH,
        )

    spread_y = Spread(b.y, outs[0], b.y_send, b.y_recv)
    spread_xg = Spread(b.xg, outs[2], b.xg_send, b.xg_recv)
    share_mem = Share(b.mems, b.mem_send, b.mem_recv)
    share_mig = Share(b.migs, b.mig_send, b.mig_recv)
    lead, follow = pl.when(c == 0), pl.when(c > 0)
    pairs = u.width // 128

    gather_until(0, 1)
    for copy in loads:
        copy.wait()
    u.make_bias(first[0, t], length[0, t])
    gather_until(1, 2)
    u.tokens_in()
    at_first = shards + 2
    gather_until(2, at_first)
    u.project_tokens()

    @lead
    def _():
        u.mem[...] = b.m0[...]
        u.memory_in()
        u.attend(0, pairs // 2)

    gather_until(at_first, at_first + 1)

    @lead
    def _():
        u.attend(pairs // 2, pairs - pairs // 2)

    gather_until(at_first + 1, at_first + 2)

    @lead
    def _():
        u.after_attention()
        u.feed_forward_up()

    gather_until(at_first + 2, at_first + 4)

    @lead
    def _():
        u.feed_forward_down()

    gather_until(at_first + 4, gather.last + 1)
    for d in (1, 2, 3):
        og_copy(d).start()

    if ctxs > 1:

        @follow
        def _():
            gather.drain()
            chain_copy(0, c - 1).wait_recv()
            u.mem[...] = b.m_recv[...].astype(F32)
            u.memory_in()
            u.attend(0, pairs)
            u.after_attention()
            u.feed_forward_up()
            u.feed_forward_down()

    after = u.write_memory()
    b.m_send[...] = after.astype(BF)
    if ctxs > 1:

        @pl.when(c < ctxs - 1)
        def _():
            chain_copy(0, c + 1).start()

    b.mems[t] = after.astype(BF)
    b.y[...] = u.af[...].astype(BF)
    share_mem.start()
    spread_y.start()
    u.backward_early()
    mine.wait()
    for d in (1, 2, 3):
        og_copy(d).wait_recv()
    share_mem.relay()

    @lead
    def _():
        gather.drain()

    if ctxs > 1:

        @pl.when(c < ctxs - 1)
        def _():
            chain_copy(1, c + 1).wait_recv()
            u.gm[...] += b.g_recv[...].astype(F32)

    def out_grad_rows(i):
        per = b.og.shape[1] // BLOCK
        return b.og[lax.div(i, per), pl.ds(lax.rem(i, per) * BLOCK, BLOCK), :].astype(F32)

    def grads(*which):
        weight_grads(u, b.g, pk, which)

    red = Reduce(shards, pk.chunks, b.g, b.r1, b.r2, b.r3, b.z, b.r_send, b.r_recv) if direct else None
    sums = SmallSum(shards, b.own, b.got, b.s_send, b.s_recv) if direct else None
    DOWN, WRITE, UP, OUT, IN0, IN1 = range(6)

    def reduce(*todo):
        for what, k in todo if direct else ():
            getattr(red, what)(k)

    u.write_back(out_grad_rows)

    @lead
    def _():
        grads("down")
        reduce(("start", DOWN))
        grads("write")
        reduce(("start", WRITE), ("to_second", DOWN))

    u.feed_forward_back()

    @lead
    def _():
        grads("up")
        reduce(("start", UP), ("to_second", WRITE))

    u.feed_forward_enter()

    @lead
    def _():
        grads("wo")
        reduce(("start", OUT), ("to_second", UP), ("to_third", DOWN))

    u.project_back()
    u.attend_back(0, pairs // 2)

    @lead
    def _():
        reduce(("to_second", OUT), ("to_third", WRITE))

    u.attend_back(pairs // 2, pairs - pairs // 2)
    u.queries_back()

    @lead
    def _():
        grads("enter")
        reduce(("start", IN0), ("start", IN1), ("to_last", DOWN), ("to_third", UP), ("to_third", OUT))

    u.enter_back()

    @lead
    def _():
        reduce(("to_second", IN0), ("to_second", IN1), ("to_last", WRITE), ("to_last", UP))

    back = u.norm_enter(b.xg)
    b.migs[t] = back.astype(BF)

    if ctxs > 1:

        @follow
        def _():
            b.g_send[...] = back.astype(BF)
            chain_copy(1, c - 1).start()
            grads("down")
            reduce(("start", DOWN))
            grads("write")
            reduce(("start", WRITE))
            grads("up")
            reduce(("start", UP), ("to_second", DOWN))
            grads("wo")
            reduce(("start", OUT), ("to_second", WRITE))
            grads("enter")
            reduce(("start", IN0), ("start", IN1))
            reduce(*(("to_second", k) for k in (UP, OUT, IN0, IN1)))

    share_mig.start()
    if direct:
        sums.start(b.small[...])
    spread_xg.start()

    @lead
    def _():
        reduce(("to_third", IN0), ("to_third", IN1), ("to_last", OUT))

    if ctxs > 1:

        @follow
        def _():
            reduce(*(("to_third", k) for k in (DOWN, UP, IN0, WRITE)))
            reduce(("to_last", DOWN), ("to_third", OUT), ("to_last", WRITE), ("to_last", UP))
            reduce(("to_last", OUT), ("to_third", IN1))

    share_mig.relay()
    reduce(("to_last", IN0), ("to_last", IN1))
    if direct:
        for i in range(3):
            sums.step(i)
        for k in range(6):
            red.arrive(k, outs[4])
        sums.arrive(outs[5])
    else:
        outs[5][...] = b.small[...]

    for spread in (spread_y, spread_xg, share_mem, share_mig):
        spread.finish()
    outs[1][...] = b.mems[...].astype(F32)
    outs[3][...] = b.migs[...].astype(F32)
    for d in (1, 2, 3):
        og_copy(d).wait_send()
    if ctxs > 1:

        @pl.when(c < ctxs - 1)
        def _():
            chain_copy(0, c + 1).wait_send()

        @pl.when(c > 0)
        def _():
            chain_copy(1, c - 1).wait_send()

    if direct:
        sums.drain()
        red.drain()


def run_step(dims, pk, direct, first, length, inputs, first_memory, memory_grad, out_grad, weights, gains):
    _, tokens, width = inputs.shape
    slots = first_memory.shape[1]
    vm = pl.BlockSpec(memory_space=pltpu.VMEM)
    sm = pl.BlockSpec(memory_space=pltpu.SMEM)
    hbm = pl.BlockSpec(memory_space=pl.ANY)
    scratch = step_scratch(dims[0], pk, direct, tokens, slots, width)
    unit = unit_scratch(tokens, slots, width, pk.ff)
    shape = jax.ShapeDtypeStruct
    return pl.pallas_call(
        partial(step_kernel, dims, pk, direct, tuple(scratch), tuple(unit)),
        out_shape=(
            shape((4, tokens // 4, width), BF), shape((4, slots, width), F32),
            shape((4, tokens // 4, width), BF), shape((4, slots, width), F32),
            shape((pk.rows, 128) if direct else pk.shape, BF), shape((8, width), F32),
        ),
        in_specs=[sm, sm] + [hbm] * 15 + [vm] * 4,
        out_specs=(hbm, vm, hbm, vm, vm, vm),
        scratch_shapes=list(scratch.values()) + list(unit.values()),
        compiler_params=pltpu.CompilerParams(
            vmem_limit_bytes=VMEM_LIMIT, collective_id=1, has_side_effects=True
        ),
        name="step",
    )(first, length, inputs, first_memory, memory_grad, out_grad, *weights, *gains)


def store_kernel(pk, owners, *refs):
    rows_in, total, small = refs[:4], refs[4], refs[5]
    rows_out, (wq, wk, wv, wo, up, down, uq, uk, uv, uo, ugate), vectors = refs[6:10], refs[10:21], refs[21:]
    for src, dst in zip(rows_in, rows_out):
        dst[...] = src[...]

    def part(at, size):
        return total[at : at + size, :].astype(F32)

    h = pk.head_rows
    for name, ref in dict(wq=wq, wk=wk, wv=wv, uq=uq, uk=uk, uv=uv).items():
        ref[...] = part(pk.heads[name], h)
    for name, ref in dict(uo=uo, ugate=ugate).items():
        ref[...] = part(pk.heads[name], h)
    for at, r, ref in ((pk.at_wo, pk.row_rows, wo), (pk.at_up, pk.row_rows, up), (pk.at_down, pk.down_rows, down)):
        for j in range(ref.shape[1] // 128):
            ref[:, j * 128 : j * 128 + 128] = part(at + j * r, r)
    share = small.shape[1] // owners
    owner = lax.axis_index("shard")
    for axis in ("ctx", "tp"):
        owner = owner * lax.axis_size(axis) + lax.axis_index(axis)
    turned = pltpu.roll(small[...], small.shape[1] - owner * share, 1)
    for i, ref in enumerate(vectors):
        ref[...] = turned[i : i + 1, 0:share]


def run_store(pk, owners, rows, total, small):
    vm = pl.BlockSpec(memory_space=pltpu.VMEM)
    shape = jax.ShapeDtypeStruct
    width = small.shape[1]
    h = pk.head_rows
    head = shape((h, 128), F32)
    outs = tuple(shape(r.shape, r.dtype) for r in rows) + (
        head, head, head, shape((pk.row_rows, width), F32), shape((pk.row_rows, pk.ff), F32),
        shape((pk.down_rows, width), F32), head, head, head, head, head,
    ) + (shape((1, width // owners), F32),) * 4
    return pl.pallas_call(
        partial(store_kernel, pk, owners),
        out_shape=outs,
        in_specs=[vm] * 6,
        out_specs=(vm,) * len(outs),
        compiler_params=pltpu.CompilerParams(vmem_limit_bytes=VMEM_LIMIT),
        name="store",
    )(*rows, total, small)


def full_gradients(pk, grads):
    groups, owners = pk.shards * pk.ctxs, pk.shards * pk.ctxs * 4
    by_head = grads.reshape(groups, 4, pk.rows, 128)
    by_owner = grads.reshape(owners, pk.rows, 128)

    def head(name):
        at = pk.heads[name]
        got = by_head[:, :, at : at + pk.head_rows]
        return got.transpose(0, 2, 1, 3).reshape(pk.width, pk.width).astype(F32)

    def rows(at, h, n):
        got = by_owner[:, at : at + h * n].reshape(owners, n, h, 128)
        return got.transpose(0, 2, 1, 3).reshape(owners * h, n * 128).astype(F32)

    return (
        head("wq"), head("wk"), head("wv"),
        rows(pk.at_wo, pk.row_rows, pk.width // 128),
        rows(pk.at_up, pk.row_rows, pk.ff // 128),
        rows(pk.at_down, pk.down_rows, pk.width // 128),
        head("uq"), head("uk"), head("uv"), head("uo").T, head("ugate").T,
    )


def local(
    inputs, first_memory, piece_start, piece_len,
    w_query, w_key, w_value, w_out, w_up, w_down, u_query, u_key, u_value, u_out, u_gate,
    gain_attn, gain_ffn, gain_write, gate_bias, out_grad, memory_grad,
):
    shards, ctxs, tps = (lax.axis_size(a) for a in ("shard", "ctx", "tp"))
    seqs, tokens, width = inputs.shape
    ff = w_up.shape[1]
    assert seqs == tps == 4 and tokens == width == 512 and ff == 2048
    weights = (w_query, w_key, w_value, w_out, w_up, w_down, u_query, u_key, u_value, u_out, u_gate)
    gains = [v.reshape(1, -1) for v in (gain_attn, gain_ffn, gain_write, gate_bias)]
    owners = shards * ctxs * tps
    direct = ctxs == 2 and width % (owners * 16) == 0
    halved = ctxs == 2 and w_query.shape[0] % 32 == 0
    pk = Packing(shards if direct else 4, 2, width, ff)
    got = run_step(
        (shards, ctxs, halved), pk, direct, piece_start.T, piece_len.T, inputs, first_memory, memory_grad,
        out_grad, weights, gains,
    )
    if direct:
        out = run_store(pk, owners, got[:4], got[4], got[5])
        return out[:13] + (out[13].T, out[14].T) + tuple(v.reshape(-1) for v in out[15:])
    every = ("shard", "ctx", "tp")
    out = list(got[:4])
    for i, g in enumerate(full_gradients(pk, got[4])):
        if i in (3, 4, 5):
            out.append(lax.psum_scatter(g, every, scatter_dimension=0, tiled=True))
            continue
        sum_dim = 1 if i >= 9 else 0
        cut = lax.psum_scatter(g, "tp", scatter_dimension=1 - sum_dim, tiled=True)
        out.append(lax.psum_scatter(cut, ("shard", "ctx"), scatter_dimension=sum_dim, tiled=True))
    for i in range(4):
        out.append(lax.psum_scatter(got[5][i], every, scatter_dimension=0, tiled=True))
    return tuple(out)


def solution(mesh):
    cut = P(("shard", "tp"), None)
    head, rows, turned = P(("shard", "ctx"), "tp"), P(("shard", "ctx", "tp"), None), P("tp", ("shard", "ctx"))
    vector = P(("shard", "ctx", "tp"))
    over_rows, over_ctx = P("shard", ("ctx", "tp"), None), P("shard", "ctx", None)
    return jax.shard_map(
        local,
        mesh=mesh,
        in_specs=(over_ctx, P("shard", None, None), P("shard", "ctx"), P("shard", "ctx"))
        + (cut,) * 11 + (P(),) * 4 + (over_rows, over_ctx),
        out_specs=(over_rows, over_ctx, over_rows, over_ctx)
        + (head,) * 3 + (rows,) * 3 + (head,) * 3 + (turned,) * 2 + (vector,) * 4,
        check_vma=False,
    )
```

```python
from functools import partial

import jax
import jax.numpy as jnp
from jax import lax
from jax.experimental import pallas as pl
from jax.experimental.pallas import tpu as pltpu
from jax.sharding import PartitionSpec as P

F32 = jnp.float32
BF = jnp.bfloat16
MESH = pl.DeviceIdType.MESH
HEAD = 64
EPS = 1e-05
NEG = -1e30
VMEM_LIMIT = 67000000

WQ, WK, WV, WO, WUP, WDOWN, UQ, UK, UV, UO, UGATE = 0, 1, 2, 3, 4, 8, 12, 13, 14, 15, 16
TILES = 17


def dot(a, b):
    return lax.dot_general(a, b, (((1,), (0,)), ((), ())), preferred_element_type=F32)


def dot_nt(a, b):
    return lax.dot_general(a, b, (((1,), (1,)), ((), ())), preferred_element_type=F32)


def dot_tn(a, b):
    return lax.dot_general(a, b, (((0,), (0,)), ((), ())), preferred_element_type=F32)


def rows_at(i, size):
    return pl.ds(pl.multiple_of(i * size, size), size)


def loop(count, unroll=1):
    def run(body):
        def step(i, carry):
            body(i)
            return carry

        lax.fori_loop(0, count, step, 0, unroll=unroll)

    return run


BLOCK = 64
UNROLL = 4


def blocks(total, body, carry=None):
    def step(n, carry):
        for k in range(UNROLL):
            i = n * UNROLL + k
            carry = body(rows_at(i, BLOCK), i, carry)
        return carry

    return lax.fori_loop(0, total // (BLOCK * UNROLL), step, carry)


def fold(values):
    return jnp.sum(values.reshape(values.shape[0] // 8, 8, values.shape[1]), axis=0)


def normed(v):
    mean = jnp.mean(v, axis=-1, keepdims=True)
    centered = v - mean
    inv = lax.rsqrt(jnp.mean(centered * centered, axis=-1, keepdims=True) + EPS)
    return centered * inv, inv


def norm_pull(e, gain, hat, inv):
    h = e * gain
    m0 = jnp.mean(h, axis=-1, keepdims=True)
    m1 = jnp.mean(h * hat, axis=-1, keepdims=True)
    return inv * (h - m0 - hat * m1)


def lane_block(width, block):
    return lax.broadcasted_iota(jnp.int32, (1, width), 1) // block


class Weights:
    def __init__(self, ref):
        self.ref = ref
        self.blocks, _, self.rows, self.width = ref.shape

    def cols(self, tile, start, size):
        got = self.ref[:, tile, :, pl.ds(start, size)]
        return got.reshape(self.blocks * self.rows, size)

    def row_part(self, tile, part, parts):
        count = self.blocks // parts
        got = self.ref[pl.ds(part * count, count), tile]
        return got.reshape(count * self.rows, self.width)

    def down_cols(self, chunk, chunks, start, size):
        count = self.blocks // chunks
        got = self.ref[pl.ds(chunk * count, count), WDOWN : WDOWN + 4, :, pl.ds(start, size)]
        return got.reshape(count * 4 * self.rows, size)

    def down_rows(self, part, parts):
        count = self.blocks // parts
        got = self.ref[pl.ds(part * count, count), WDOWN : WDOWN + 4]
        return got.reshape(count * 4 * self.rows, self.width)


def unit_scratch(tokens, slots, width, ff):
    r = tokens + slots
    heads = width // HEAD
    quads = width // 256
    v = pltpu.VMEM
    return dict(
        mem=v((slots, width), F32),
        xh=v((r, width), F32),
        xr=v((r, 1), F32),
        enc=v((r, width), BF),
        q=v((tokens, width), BF),
        k=v((r, width), BF),
        v=v((r, width), BF),
        kt=v((width, r), BF),
        vt=v((width, r), BF),
        pt=v((heads, r, tokens), BF),
        ptop=v((heads, 1, tokens), F32),
        psum=v((heads, 1, tokens), F32),
        pinv=v((heads, 1, tokens), F32),
        top=v((2, 1, 256), F32),
        mixt=v((width, tokens), BF),
        af=v((r, width), F32),
        ah=v((tokens, width), F32),
        ar=v((tokens, 1), F32),
        fin=v((tokens, width), BF),
        act=v((ff // 512, tokens, 512), BF),
        dg=v((ff // 512, tokens, 512), BF),
        yh=v((tokens, width), F32),
        yr=v((tokens, 1), F32),
        wri=v((r, width), BF),
        sq=v((slots, width), BF),
        sk=v((r, width), BF),
        sv=v((r, width), BF),
        spt=v((quads, r, 256), BF),
        wrt=v((slots, width), BF),
        gate=v((slots, width), F32),
        f1=v((slots, width), F32),
        f2=v((slots, width), F32),
        gm=v((slots, width), F32),
        gup=v((slots, width), BF),
        ggl=v((slots, width), BF),
        dsq=v((slots, width), BF),
        dsk=v((r, width), BF),
        dsv=v((r, width), BF),
        e=v((r, width), F32),
        gy=v((tokens, width), F32),
        gyb=v((tokens, width), BF),
        bwm=v((slots, width), F32),
        gpre=v((ff // 512, tokens, 512), BF),
        gab=v((tokens, width), BF),
        gmx=v((tokens, width), BF),
        dst=v((2, r, tokens), BF),
        dqt=v((width, tokens), BF),
        dq=v((tokens, width), BF),
        dk=v((r, width), BF),
        dv=v((r, width), BF),
    )


class Unit:
    def __init__(self, refs, w, x, gains, small):
        self.__dict__.update(refs)
        self.w = w
        self.x = x
        self.gains = gains
        self.small = small
        self.tokens, self.width = x.shape
        self.slots = self.mem.shape[0]
        self.r = self.tokens + self.slots
        self.ff = self.act.shape[0] * 512

    def gain(self, i):
        return self.gains[i][...]

    def make_bias(self, first, length):
        t = self.tokens

        @loop(t // 64)
        def _(i):
            key = lax.broadcasted_iota(jnp.int32, (64, t), 0) + i * 64
            query = lax.broadcasted_iota(jnp.int32, (64, t), 1)
            last = first + length
            inside = (key >= first) & (key < last) & (query >= first) & (query < last)
            seen = (key <= query) | inside
            self.e[rows_at(i, 64), :] = jnp.where(seen, 0.0, NEG).astype(F32)

    def norm_in(self, rows, values):
        hat, inv = normed(values)
        self.xh[rows, :] = hat
        self.xr[rows, :] = inv
        self.enc[rows, :] = (hat * self.gain(0)).astype(BF)

    def tokens_in(self):
        def body(rows, i, carry):
            self.norm_in(rows, self.x[rows, :].astype(F32))

        blocks(self.tokens, body)

    def project_tokens(self):
        t = self.tokens

        @loop(self.width // 256)
        def _(n):
            cols = rows_at(n, 256)
            enc = self.enc[0:t, :]
            got = dot(enc, self.w.cols(WQ, n * 256, 256)).astype(BF)
            self.q[:, cols] = got * BF(HEAD**-0.5)
            self.k[0:t, cols] = dot(enc, self.w.cols(WK, n * 256, 256)).astype(BF)
            self.v[0:t, cols] = dot(enc, self.w.cols(WV, n * 256, 256)).astype(BF)

        self.vt[:, 0:t] = self.v[0:t, :].T

    def memory_in(self):
        t, r = self.tokens, self.r
        self.norm_in(slice(t, r), self.mem[...])
        enc = self.enc[t:r, :]
        self.k[t:r, :] = dot(enc, self.w.cols(WK, 0, self.width)).astype(BF)
        self.v[t:r, :] = dot(enc, self.w.cols(WV, 0, self.width)).astype(BF)
        self.vt[:, t:r] = self.v[t:r, :].T

    def held(self, j):
        return self.af.at[:, j % 2 * 256 : j % 2 * 256 + 256]

    def attend(self, first, count):
        t = self.tokens
        span = 256

        @loop(count)
        def _(i):
            p = i + first
            cols = rows_at(p, 128)
            half = lane_block(128, HEAD)
            steps = [(hh, n) for hh in range(2) for n in range(t // span)]

            def score(j):
                hh, n = steps[j]
                qc = slice(n * span, n * span + span)
                q = self.q[qc, cols]
                s = dot_nt(self.k[0:t, cols], jnp.where(half == hh, q, jnp.zeros_like(q)))
                part = s[n * span : t] + self.e[n * span : t, qc]
                top = jnp.max(part, axis=0, keepdims=True)
                self.held(j)[n * span : t, :] = part
                if n > 0:
                    self.held(j)[0 : n * span, :] = s[0 : n * span]
                    top = jnp.maximum(top, jnp.max(s[0 : n * span], axis=0, keepdims=True))
                self.ptop[2 * p + hh, :, qc] = top

            def soften(j):
                hh, n = steps[j]
                qc = slice(n * span, n * span + span)
                e = jnp.exp(self.held(j)[0:t, :] - self.ptop[2 * p + hh, :, qc])
                self.psum[2 * p + hh, :, qc] = jnp.sum(e, axis=0, keepdims=True)
                self.pt[2 * p + hh, 0:t, qc] = e.astype(BF)

            def mix(j):
                hh, n = steps[j]
                qc = slice(n * span, n * span + span)
                feats = pl.ds(pl.multiple_of(p * 128 + hh * HEAD, HEAD), HEAD)
                self.yh[feats, qc] = dot(self.vt[feats, 0:t], self.pt[2 * p + hh, 0:t, qc])

            score(0)
            for j in range(len(steps)):
                if j + 1 < len(steps):
                    score(j + 1)
                soften(j)
                mix(j)

    def attend_memory(self):
        t, r = self.tokens, self.r

        @loop(self.width // 128)
        def _(p):
            cols = rows_at(p, 128)
            half = lane_block(128, HEAD)
            for hh in range(2):
                h = 2 * p + hh
                feats = pl.ds(pl.multiple_of(p * 128 + hh * HEAD, HEAD), HEAD)
                q = self.q[:, cols]
                s = dot_nt(self.k[t:r, cols], jnp.where(half == hh, q, jnp.zeros_like(q)))
                top = jnp.maximum(self.ptop[h], jnp.max(s, axis=0, keepdims=True))
                fade = jnp.exp(self.ptop[h] - top)
                e = jnp.exp(s - top)
                inv = 1.0 / (fade * self.psum[h] + jnp.sum(e, axis=0, keepdims=True))
                self.pinv[h] = inv
                low = e.astype(BF)
                self.pt[h, t:r, :] = low
                got = self.yh[feats, :] * fade + dot(self.vt[feats, t:r], low)
                self.mixt[feats, :] = (got * inv).astype(BF)
                for m in range(t // 64):
                    rows = slice(m * 64, m * 64 + 64)
                    self.pt[h, rows, :] = (self.pt[h, rows, :].astype(F32) * fade).astype(BF)

    def after_attention(self):
        t = self.tokens
        self.gmx[...] = self.mixt[...].T

        @loop(self.width // 256)
        def _(n):
            cols = rows_at(n, 256)
            got = dot(self.gmx[...], self.w.cols(WO, n * 256, 256))
            self.af[0:t, cols] = self.x[:, cols].astype(F32) + got

        def body(rows, i, carry):
            hat, inv = normed(self.af[rows, :])
            self.ah[rows, :] = hat
            self.ar[rows, :] = inv
            self.fin[rows, :] = (hat * self.gain(1)).astype(BF)

        blocks(t, body)

    def feed_forward_up(self, first, count):
        t = self.tokens
        c = 0.7978845608028654

        @loop(count)
        def _(i):
            j = i + first

            def project(n):
                part = slice(n * 256, n * 256 + 256)
                self.gy[:, part] = dot(self.fin[...], self.w.cols(WUP + j, n * 256, 256))

            def activate(n):
                part = slice(n * 256, n * 256 + 256)
                for m in range(t // 64):
                    rows = slice(m * 64, m * 64 + 64)
                    pre = self.gy[rows, part]
                    sq = pre * pre
                    th = jnp.tanh(pre * (c + (c * 0.044715) * sq))
                    half = 0.5 + 0.5 * th
                    self.act[j, rows, part] = (pre * half).astype(BF)
                    slope = half + (0.5 * pre) * (1.0 - th * th) * (c + (3 * c * 0.044715) * sq)
                    self.dg[j, rows, part] = slope.astype(BF)

            project(0)
            project(1)
            activate(0)
            activate(1)

    def feed_forward_down(self):
        t = self.tokens

        @loop(self.width // 256)
        def _(n):
            cols = rows_at(n, 256)
            total = self.af[0:t, cols]
            for j in range(self.ff // 512):
                total = total + dot(
                    self.act[j], self.w.down_cols(j, self.ff // 512, n * 256, 256)
                )
            self.af[0:t, cols] = total

        def body(rows, i, carry):
            hat, inv = normed(self.af[rows, :])
            self.yh[rows, :] = hat
            self.yr[rows, :] = inv
            self.wri[rows, :] = (hat * self.gain(2)).astype(BF)

        blocks(t, body)

        self.wri[t : self.r, :] = (self.xh[t : self.r, :] * self.gain(2)).astype(BF)

    def spread_heads(self, rows, g):
        part = rows[:, g * 256 : g * 256 + 256]
        block = lane_block(256, HEAD)
        return jnp.concatenate(
            [jnp.where(block == h, part, jnp.zeros_like(part)) for h in range(4)], axis=0
        )

    def gather_heads(self, stacked):
        block = lane_block(256, HEAD)
        s = self.slots
        total = jnp.where(block == 0, stacked[0:s], 0.0)
        for h in range(1, 4):
            total = total + jnp.where(block == h, stacked[h * s : h * s + s], 0.0)
        return total

    def write_memory(self):
        t, r = self.tokens, self.r

        @loop(self.width // 256)
        def _(n):
            cols = rows_at(n, 256)
            wri = self.wri[...]
            self.sk[:, cols] = dot(wri, self.w.cols(UK, n * 256, 256)).astype(BF)
            self.sv[:, cols] = dot(wri, self.w.cols(UV, n * 256, 256)).astype(BF)

        wm = self.wri[t:r, :]
        sq = dot(wm, self.w.cols(UQ, 0, self.width)).astype(BF)
        self.sq[...] = sq * BF(HEAD**-0.5)
        for g in range(self.width // 256):
            cols = slice(g * 256, g * 256 + 256)
            s = dot_nt(self.sk[:, cols], self.spread_heads(self.sq[...], g))
            e = jnp.exp(s - jnp.max(s, axis=0, keepdims=True))
            probs = (e * (1.0 / jnp.sum(e, axis=0, keepdims=True))).astype(BF)
            self.spt[g] = probs
            self.wrt[:, cols] = self.gather_heads(dot_tn(probs, self.sv[:, cols])).astype(BF)
        th = jnp.tanh(dot(self.wrt[...], self.w.cols(UO, 0, self.width)))
        pre = dot(wm, self.w.cols(UGATE, 0, self.width))
        gate = jax.nn.sigmoid(pre + self.gain(3))
        mem = self.mem[...]
        self.gate[...] = gate
        self.f1[...] = (mem - th) * gate * (1.0 - gate)
        self.f2[...] = (1.0 - gate) * (1.0 - th * th)
        return gate * mem + (1.0 - gate) * th

    def backward_early(self):
        self.kt[...] = self.k[...].T

    def write_back(self):
        gm = self.gm[...]
        ggp = gm * self.f1[...]
        gup = (gm * self.f2[...]).astype(BF)
        ggl = ggp.astype(BF)
        self.gup[...] = gup
        self.ggl[...] = ggl
        self.small[3:4, :] = jnp.sum(ggp, axis=0, keepdims=True)
        gwr = dot_nt(gup, self.w.row_part(UO, 0, 1)).astype(BF)
        quads = range(self.width // 256)
        cols = [slice(g * 256, g * 256 + 256) for g in quads]
        grads = [self.spread_heads(gwr, g) for g in quads]
        for g in quads:
            self.af[:, cols[g]] = dot_nt(self.sv[:, cols[g]], grads[g])
        for g in quads:
            self.dsv[:, cols[g]] = dot(self.spt[g], grads[g]).astype(BF)
        for g in quads:
            pf = self.spt[g].astype(F32)
            dp = self.af[:, cols[g]]
            self.dst[0, :, cols[g]] = (pf * (dp - jnp.sum(pf * dp, axis=0, keepdims=True))).astype(BF)
        for g in quads:
            dq = self.gather_heads(dot_tn(self.dst[0, :, cols[g]], self.sk[:, cols[g]])) * HEAD**-0.5
            self.dsq[:, cols[g]] = dq.astype(BF)
            self.dsk[:, cols[g]] = dot(self.dst[0, :, cols[g]], self.spread_heads(self.sq[...], g)).astype(BF)

    def write_enter(self, out_grad):
        t, r = self.tokens, self.r

        @loop(2)
        def _(n):
            cols = rows_at(n, self.width // 2)
            self.e[:, cols] = dot_nt(self.dsk[...], self.w.row_part(UK, n, 2)) + dot_nt(
                self.dsv[...], self.w.row_part(UV, n, 2)
            )

        em = self.e[t:r, :] + dot_nt(self.dsq[...], self.w.row_part(UQ, 0, 1))
        em = em + dot_nt(self.ggl[...], self.w.row_part(UGATE, 0, 1))
        hat = self.xh[t:r, :]
        self.bwm[...] = norm_pull(em, self.gain(2), hat, self.xr[t:r, :])

        def body(rows, i, carry):
            e = self.e[rows, :]
            hat = self.yh[rows, :]
            grad = out_grad(i) + norm_pull(e, self.gain(2), hat, self.yr[rows, :])
            self.gy[rows, :] = grad
            self.gyb[rows, :] = grad.astype(BF)
            return carry + fold(e * hat)

        total = blocks(t, body, fold(em * hat))
        self.small[2:3, :] = jnp.sum(total, axis=0, keepdims=True)

    def feed_forward_back(self):
        chunks = self.ff // 512

        @loop(chunks)
        def _(j):
            for n in range(2):
                cols = slice(n * 256, n * 256 + 256)
                got = dot_nt(self.gyb[...], self.w.down_rows(2 * j + n, 2 * chunks))
                self.gpre[j, :, cols] = (got * self.dg[j, :, cols].astype(F32)).astype(BF)

    def feed_forward_enter(self):
        t = self.tokens
        chunks = self.ff // 512

        @loop(2)
        def _(n):
            cols = rows_at(n, self.width // 2)
            total = dot_nt(self.gpre[0], self.w.row_part(WUP, n, 2))
            for j in range(1, chunks):
                total = total + dot_nt(self.gpre[j], self.w.row_part(WUP + j, n, 2))
            self.e[0:t, cols] = total

        def body(rows, i, carry):
            e = self.e[rows, :]
            hat = self.ah[rows, :]
            grad = self.gy[rows, :] + norm_pull(e, self.gain(1), hat, self.ar[rows, :])
            self.gy[rows, :] = grad
            self.gab[rows, :] = grad.astype(BF)
            return carry + fold(e * hat)

        total = blocks(t, body, jnp.zeros((8, self.width), F32))
        self.small[1:2, :] = jnp.sum(total, axis=0, keepdims=True)

    def project_back(self):
        heads = self.pinv.shape[0]
        inv = jnp.concatenate([self.pinv[h] for h in range(heads)], axis=0).T
        for n in range(2):
            cols = slice(n * 256, n * 256 + 256)
            block = lane_block(256, HEAD)
            scale = inv[:, 4 * n : 4 * n + 1]
            for h in range(1, 4):
                scale = jnp.where(block >= h, inv[:, 4 * n + h : 4 * n + h + 1], scale)
            self.gmx[:, cols] = (dot_nt(self.gab[...], self.w.row_part(WO, n, 2)) * scale).astype(BF)

    def attend_back(self, first, count):
        t, r = self.tokens, self.r
        span = 256

        @loop(count)
        def _(i):
            p = i + first
            cols = rows_at(p, 128)
            half = lane_block(128, HEAD)
            steps = [(hh, n) for hh in range(2) for n in range(t // span)]

            def score(j):
                hh, n = steps[j]
                qc = slice(n * span, n * span + span)
                g = self.gmx[qc, cols]
                dp = dot_nt(self.v[:, cols], jnp.where(half == hh, g, jnp.zeros_like(g)))
                self.held(j)[...] = dp
                total = jnp.sum(self.pt[2 * p + hh, :, qc].astype(F32) * dp, axis=0, keepdims=True)
                self.top[j % 2] = total * self.pinv[2 * p + hh, :, qc]

            def soften(j):
                hh, n = steps[j]
                qc = slice(n * span, n * span + span)
                e = self.pt[2 * p + hh, :, qc].astype(F32)
                self.dst[hh, :, qc] = (e * (self.held(j)[...] - self.top[j % 2])).astype(BF)

            def queries(j):
                hh, n = steps[j]
                qc = slice(n * span, n * span + span)
                feats = pl.ds(pl.multiple_of(p * 128 + hh * HEAD, HEAD), HEAD)
                got = dot(self.kt[feats, :], self.dst[hh, :, qc])
                self.dqt[feats, qc] = (got * HEAD**-0.5).astype(BF)

            def keys(hh):
                dv = dot(self.pt[2 * p + hh], self.gmx[:, cols]).astype(BF)
                dk = dot(self.dst[hh], self.q[:, cols]).astype(BF)
                if hh == 1:
                    dv = jnp.where(half == 0, self.dv[:, cols], dv)
                    dk = jnp.where(half == 0, self.dk[:, cols], dk)
                self.dv[:, cols] = dv
                self.dk[:, cols] = dk

            score(0)
            for j in range(len(steps)):
                if j + 1 < len(steps):
                    score(j + 1)
                soften(j)
                queries(j)
                if steps[j][1] == t // span - 1:
                    keys(steps[j][0])

    def queries_back(self):
        self.dq[...] = self.dqt[...].T

    def enter_back(self):
        t = self.tokens

        @loop(2)
        def _(n):
            cols = rows_at(n, self.width // 2)
            self.e[:, cols] = dot_nt(self.dk[...], self.w.row_part(WK, n, 2)) + dot_nt(
                self.dv[...], self.w.row_part(WV, n, 2)
            )
            self.e[0:t, cols] += dot_nt(self.dq[...], self.w.row_part(WQ, n, 2))

    def norm_enter(self, input_grad):
        t, r = self.tokens, self.r
        e = self.e[t:r, :]
        hat = self.xh[t:r, :]
        first = fold(e * hat)
        mem_grad = self.gm[...] * self.gate[...] + self.bwm[...]
        mem_grad = mem_grad + norm_pull(e, self.gain(0), hat, self.xr[t:r, :])

        def body(rows, i, carry):
            e = self.e[rows, :]
            hat = self.xh[rows, :]
            grad = self.gy[rows, :] + norm_pull(e, self.gain(0), hat, self.xr[rows, :])
            input_grad[rows, :] = grad.astype(BF)
            return carry + fold(e * hat)

        total = blocks(t, body, first)
        self.small[0:1, :] = jnp.sum(total, axis=0, keepdims=True)

        return mem_grad


class Packing:
    def __init__(self, shards, ctxs, width, ff):
        self.shards, self.ctxs, self.width, self.ff = shards, ctxs, width, ff
        self.head_rows = h = width // (shards * ctxs)
        self.row_rows = width // (shards * ctxs * 4)
        self.down_rows = ff // (shards * ctxs * 4)
        at = 0
        self.heads = {}
        bounds = [at]
        for name in ("uq", "uk", "uv", "uo", "ugate"):
            self.heads[name] = at
            at += h
        bounds.append(at)
        self.at_down = at
        at += self.down_rows * (width // 128)
        bounds.append(at)
        self.at_up = at
        at += self.row_rows * (ff // 128)
        bounds.append(at)
        self.at_wo = at
        at += self.row_rows * (width // 128)
        for name in ("wq", "wk", "wv"):
            self.heads[name] = at
            at += h
        self.rows = at
        bounds.append(at)
        chunks = []
        for lo, hi in zip(bounds[:-1], bounds[1:]):
            middle = lo + (hi - lo) // 2 // 16 * 16
            chunks += [(lo, middle), (middle, hi)]
        self.chunks = tuple(chunks)

    @property
    def shape(self):
        return (self.shards, self.ctxs, 2, 2, self.rows, 128)


def weight_grads(u, g, pk, names):
    width = u.width
    tile = 256

    def store_head(at, m, got):
        h = pk.head_rows
        per = tile // h
        for i in range(per):
            s = m * (per // pk.ctxs) + i // pk.ctxs
            for t in range(4):
                g[s, i % pk.ctxs, t // 2, t % 2, at : at + h, :] = got[
                    i * h : i * h + h, t * 128 : t * 128 + 128
                ]

    def store_rows(at, h, m, got, chunk0):
        per = tile // h
        for i in range(per):
            if per % (pk.ctxs * 4) == 0:
                s, c = m * (per // (pk.ctxs * 4)) + i // (pk.ctxs * 4), (i // 4) % pk.ctxs
            else:
                owner = m * (per // 4) + i // 4
                s, c = lax.div(owner, pk.ctxs), lax.rem(owner, pk.ctxs)
            for j in range(got.shape[1] // 128):
                lo = at + (chunk0 + j) * h
                g[s, c, (i // 2) % 2, i % 2, lo : lo + h, :] = got[
                    i * h : i * h + h, j * 128 : j * 128 + 128
                ]

    def heads(left, items):
        @loop(width // tile)
        def _(m):
            lt = left[:, rows_at(m, tile)].T
            for name, lo, hi, right in items:
                store_head(pk.heads[name], m, dot(lt[:, lo:hi], right[...]).astype(BF))

    t, r = u.tokens, u.r
    if "down" in names:
        for j in range(u.ff // 512):

            @loop(512 // tile)
            def _(m, j=j):
                lt = u.act[j, :, rows_at(m, tile)].T
                got = dot(lt, u.gyb[...]).astype(BF)
                store_rows(pk.at_down, pk.down_rows, m + j * (512 // tile), got, 0)

    if "up" in names:

        @loop(width // tile)
        def _(m):
            lt = u.fin[:, rows_at(m, tile)].T
            for j in range(u.ff // 512):
                store_rows(pk.at_up, pk.row_rows, m, dot(lt, u.gpre[j]).astype(BF), 4 * j)

    if "wo" in names:

        @loop(width // tile)
        def _(m):
            got = dot(u.mixt[rows_at(m, tile), :], u.gab[...]).astype(BF)
            store_rows(pk.at_wo, pk.row_rows, m, got, 0)

    if "write" in names:
        heads(u.wri, (("uq", t, r, u.dsq), ("uk", 0, r, u.dsk), ("uv", 0, r, u.dsv)))
        heads(u.gup, (("uo", 0, r - t, u.wrt),))
        heads(u.ggl, (("ugate", 0, r - t, u.wri.at[t:r]),))
    if "enter" in names:
        heads(u.enc, (("wq", 0, t, u.dq), ("wk", 0, r, u.dk), ("wv", 0, r, u.dv)))


GROUPS = ((0, 3), (3, 8), (8, 12), (12, 17))


def greet(peers):
    barrier = pltpu.get_barrier_semaphore()
    count = 0
    for cond, device in peers:

        @pl.when(cond)
        def _(device=device):
            pl.semaphore_signal(barrier, inc=1, device_id=device, device_id_type=MESH)

        count = count + jnp.where(cond, 1, 0)
    pl.semaphore_wait(barrier, count)


class Gather:
    UP, DOWN, ACROSS, BESIDE, FAR, PAIR, PAIR_ACROSS, PAIR_BESIDE, PAIR_FAR = range(9)
    LINKS = {ACROSS: 0, BESIDE: 1, FAR: 2, PAIR: 3, PAIR_ACROSS: 3, PAIR_BESIDE: 3, PAIR_FAR: 3}

    def __init__(self, shards, halved, w, send, line_send, recv, pair_recv):
        self.n, self.halved, self.w = shards, halved, w
        self.send, self.line_send, self.recv, self.pair_recv = send, line_send, recv, pair_recv
        self.s, self.c, self.t = (lax.axis_index(a) for a in ("shard", "ctx", "tp"))
        odd = lax.rem(self.t, 2)
        self.pair_tp = self.t + 1 - 2 * odd
        self.across_tp = lax.rem(self.t + 2, 4)
        self.pair = {"tp": self.pair_tp}
        self.across = {"tp": self.across_tp}
        self.beside = {"ctx": self.c + 1 - 2 * lax.rem(self.c, 2)}

    def copy(self, kind, source, tp, g, device, half=None):
        lo, hi = GROUPS[g]
        block = self.w.at[source * 4 + tp, lo:hi]
        if half is not None:
            size = self.w.shape[2] // 2
            block = self.w.at[source * 4 + tp, lo:hi, pl.ds(pl.multiple_of(half * size, size), size)]
        return self.between(block, kind, source, g, device)

    def between(self, block, kind, source, g, device):
        if kind in (self.UP, self.DOWN):
            send = self.line_send.at[kind, source]
        else:
            send = self.send.at[self.LINKS[kind]]
        to_pair = kind in (self.PAIR, self.PAIR_ACROSS, self.PAIR_BESIDE, self.PAIR_FAR)
        recv = self.pair_recv.at[g] if to_pair else self.recv.at[kind, source, g]
        return pltpu.make_async_remote_copy(
            src_ref=block, dst_ref=block, send_sem=send, recv_sem=recv, device_id=device, device_id_type=MESH,
        )

    @property
    def mine(self):
        return self.c if self.halved else None

    @property
    def others(self):
        return 1 - self.c

    def up(self, source, g, far):
        return self.copy(self.UP, source, self.t, g, {"shard": self.s + 1}, self.mine if far else None)

    def down(self, source, g, far):
        return self.copy(self.DOWN, source, self.t, g, {"shard": self.s - 1}, self.mine if far else None)

    def to_across(self, source, g, tp=None):
        return self.copy(self.ACROSS, source, self.t if tp is None else tp, g, self.across, self.mine)

    def to_pair(self, source, g, far, tp=None):
        return self.copy(self.PAIR, source, self.t if tp is None else tp, g, self.pair, self.mine if far else None)

    def far(self, d):
        return self.halved and d == self.n - 1

    def start_own(self, g):
        s, n = self.s, self.n
        if n > 1:

            @pl.when(s < n - 1)
            def _():
                self.up(s, g, self.far(1)).start()

            @pl.when(s > 0)
            def _():
                self.down(s, g, self.far(1)).start()

        self.to_across(s, g).start()
        self.to_pair(s, g, False).start()

    def came(self, source, g, d):
        self.to_across(source, g).start()
        self.to_pair(source, g, self.far(d)).start()
        if self.far(d):
            self.copy(self.FAR, source, self.t, g, self.beside, self.c).start()

    def line_step(self, d, g):
        s, n = self.s, self.n

        @pl.when(s - d >= 0)
        def _():
            self.up(s - d, g, self.far(d)).wait_recv()

            @pl.when(s < n - 1)
            def _():
                self.up(s - d, g, self.far(d + 1)).start()

            self.came(s - d, g, d)

        @pl.when(s + d <= n - 1)
        def _():
            self.down(s + d, g, self.far(d)).wait_recv()

            @pl.when(s > 0)
            def _():
                self.down(s + d, g, self.far(d + 1)).start()

            self.came(s + d, g, d)

    def sources(self, d):
        s, n = self.s, self.n
        both = ((s - d, s - d >= 0), (s + d, s + d <= n - 1))
        return both[:1] if d == 0 else both

    def across_step(self, d, g):
        for source, cond in self.sources(d):

            @pl.when(cond)
            def _(source=source):
                tp = self.across_tp
                self.to_across(source, g, tp).wait_recv()
                self.copy(self.PAIR_ACROSS, source, tp, g, self.pair, self.mine).start()
                if self.halved:
                    self.copy(self.BESIDE, source, tp, g, self.beside, self.c).start()

    def beside_step(self, d, g):
        if not self.halved:
            return
        for source, cond in self.sources(d):

            @pl.when(cond)
            def _(source=source):
                tp = self.across_tp
                self.copy(self.BESIDE, source, tp, g, self.beside, self.others).wait_recv()
                self.copy(self.PAIR_BESIDE, source, tp, g, self.pair, self.others).start()

    def far_step(self, g):
        if not self.halved:
            return
        for source, cond in self.sources(self.n - 1):

            @pl.when(cond)
            def _(source=source):
                self.copy(self.FAR, source, self.t, g, self.beside, self.others).wait_recv()
                self.copy(self.PAIR_FAR, source, self.t, g, self.pair, self.others).start()

    def finish(self, g):
        lo, hi = GROUPS[g]
        self.between(self.w.at[0 : 2 * self.n, lo:hi], self.PAIR, 0, g, self.pair).wait_recv()

    def drain(self):
        s, n = self.s, self.n
        parts = n // 2 if self.halved else n
        half = self.w.at[0, :, 0 : self.w.shape[2] // 2]
        self.between(self.w.at[0 : 2 * n], self.PAIR, 0, 0, self.pair).wait_send()
        self.between(self.w.at[0:parts], self.ACROSS, 0, 0, self.across).wait_send()
        if self.halved:
            self.between(self.w.at[0:parts], self.BESIDE, 0, 0, self.beside).wait_send()

            @pl.when(jnp.logical_or(s == 0, s == n - 1))
            def _():
                self.between(half, self.FAR, 0, 0, self.beside).wait_send()

        for d in range(n - 1):
            block = half if self.far(d + 1) else self.w.at[0]

            @pl.when(jnp.logical_and(s - d >= 0, s < n - 1))
            def _(d=d, block=block):
                self.between(block, self.UP, s - d, 0, {"shard": s + 1}).wait_send()

            @pl.when(jnp.logical_and(s + d <= n - 1, s > 0))
            def _(d=d, block=block):
                self.between(block, self.DOWN, s + d, 0, {"shard": s - 1}).wait_send()

    def events(self, time, ready, between):
        n = self.n
        groups = range(len(GROUPS))
        for g in groups:
            if time == max(g - 1, 0):
                ready(g)
                self.start_own(g)
        for g in groups:
            d = time - g
            if not 1 <= d <= n + 1:
                continue
            if d <= n - 1:
                self.line_step(d, g)
            if d <= n:
                self.across_step(d - 1, g)
            if d >= 2:
                self.beside_step(d - 2, g)
            if d == n + 1:
                self.far_step(g)
                self.finish(g)
            between(time - n - 1 if g >= time - n - 1 else -1)

    @property
    def last(self):
        return (len(GROUPS) - 1) + self.n + 1


def line_peers(n):
    s = lax.axis_index("shard")
    return [(s >= 0, {"shard": lax.rem(s + d, n)}) for d in range(1, n)]


def tp_peers():
    t = lax.axis_index("tp")
    return [(t >= 0, {"tp": lax.rem(t + d, 4)}) for d in (1, 2, 3)]


def own_tiles(weights, w, own, sems):
    names = [WQ, WK, WV, WO, WUP, WDOWN, UQ, UK, UV, UO, UGATE]
    rows = w.shape[2]
    out = []
    for name, ref in zip(names, weights):
        parts = {WUP: 4, WDOWN: 4}.get(name, 1)
        for j in range(parts):
            src = ref
            if name == WUP:
                src = ref.at[:, j * 512 : j * 512 + 512]
            if name == WDOWN:
                src = ref.at[j * rows : j * rows + rows]
            out.append(pltpu.make_async_copy(src, w.at[own, name + j], sems.at[name + j]))
    return out


class Reduce:
    ORDER = (0, 2, 0, 1, 0, 1, 0, 1)

    def __init__(self, shards, chunks, g, r1, r2, r3, z, zfirst, send, recv):
        self.n = shards
        self.sizes = [hi - lo for lo, hi in chunks]
        self.rows = [pl.ds(lo, hi - lo) for lo, hi in chunks]
        self.g, self.r1, self.r2, self.r3, self.z = g, r1, r2, r3, z
        self.zz, self.zx, self.zy, self.zsend, self.zrecv = zfirst
        self.send, self.recv = send, recv
        self.s, self.c, self.t = (lax.axis_index(a) for a in ("shard", "ctx", "tp"))
        self.core = lax.rem(self.t, 2)
        self.x = lax.div(self.t, 2)
        self.pair = {"tp": self.t + 1 - 2 * self.core}
        self.across = {"tp": lax.rem(self.t + 2, 4)}
        self.beside = {"ctx": 1 - self.c}

    def early(self, k, step):
        rows = self.rows[k]
        if step < self.n - 1:
            to = lax.rem(self.s + step + 1, self.n)
            src, dst, device = self.r1.at[to, :, :, rows], self.zz.at[step], {"shard": to}
        elif step == self.n - 1:
            src, dst, device = self.r1.at[self.s, :, 1 - self.x, rows], self.zx, self.across
        else:
            src, dst, device = self.zx.at[1 - self.c], self.zy, self.beside
        return pltpu.make_async_remote_copy(
            src_ref=src, dst_ref=dst, send_sem=self.zsend.at[step], recv_sem=self.zrecv.at[step],
            device_id=device, device_id_type=MESH,
        )

    def copy(self, src, dst, k, kind, device):
        return pltpu.make_async_remote_copy(
            src_ref=src, dst_ref=dst, send_sem=self.send.at[kind], recv_sem=self.recv.at[k, kind],
            device_id=device, device_id_type=MESH,
        )

    def one(self, k):
        rows = self.rows[k]
        return self.copy(self.g.at[:, :, :, 1 - self.core, rows], self.r1.at[:, :, :, rows], k, 0, self.pair)

    def two(self, k):
        rows = self.rows[k]
        if self.ORDER[k] == 0:
            src, device = self.r1.at[:, :, 1 - self.x, rows], self.across
        else:
            src, device = self.r1.at[:, 1 - self.c, :, rows], self.beside
        return self.copy(src, self.r2.at[:, :, rows], k, 1, device)

    def three(self, k):
        rows = self.rows[k]
        if self.ORDER[k] == 0:
            src, device = self.r2.at[:, 1 - self.c, rows], self.beside
        else:
            src, device = self.r2.at[:, 1 - self.x, rows], self.across
        return self.copy(src, self.r3.at[:, rows], k, 2, device)

    def along(self, k, d):
        to = lax.rem(self.s + d, self.n)
        rows = self.rows[k]
        return self.copy(self.r3.at[to, rows], self.z.at[d - 1, rows], k, 2 + d, {"shard": to})

    def start(self, k):
        self.one(k).start()

    def to_second(self, k):
        self.one(k).wait_recv()
        rows = self.rows[k]
        for j in range(2):
            for x in range(2):
                self.r1[:, j, x, rows] += self.g[:, j, x, self.core, rows]
        if self.ORDER[k] == 2:
            for step in range(self.n - 1):
                self.early(k, step).start()
            return
        self.two(k).start()

    def to_third(self, k):
        rows = self.rows[k]
        if self.ORDER[k] == 2:
            for step in range(self.n - 1):
                self.early(k, step).wait_recv()
            for j in range(2):
                for x in range(2):
                    total = self.r1[self.s, j, x, rows].astype(F32)
                    for step in range(self.n - 1):
                        total = total + self.zz[step, j, x].astype(F32)
                    self.r1[self.s, j, x, rows] = total.astype(BF)
            self.early(k, self.n - 1).start()
            return
        self.two(k).wait_recv()
        for j in range(2):
            own = self.r1[:, j, self.x, rows] if self.ORDER[k] == 0 else self.r1[:, self.c, j, rows]
            self.r2[:, j, rows] += own
        self.three(k).start()

    def to_last(self, k):
        rows = self.rows[k]
        if self.ORDER[k] == 2:
            self.early(k, self.n - 1).wait_recv()
            for j in range(2):
                self.zx[j] += self.r1[self.s, j, self.x, rows]
            self.early(k, self.n).start()
            return
        self.three(k).wait_recv()
        own = self.c if self.ORDER[k] == 0 else self.x
        self.r3[:, rows] += self.r2[:, own, rows]
        for d in range(1, self.n):
            self.along(k, d).start()

    def arrive(self, k, out):
        rows = self.rows[k]
        if self.ORDER[k] == 2:
            self.early(k, self.n).wait_recv()
            out[rows, :] = (self.zx[self.c].astype(F32) + self.zy[...].astype(F32)).astype(out.dtype)
            return
        for d in range(1, self.n):
            self.along(k, d).wait_recv()
        total = self.r3[self.s, rows].astype(F32)
        for d in range(1, self.n):
            total = total + self.z[d - 1, rows].astype(F32)
        out[rows, :] = total.astype(out.dtype)

    def drain(self):
        first = self.ORDER.index(2)
        rest = sum(self.sizes) - self.sizes[first]
        whole = [(self.r1, 0), (self.r1.at[:, :, 0, 0:rest], 1), (self.r1.at[:, 0, 0, 0:rest], 2)]
        whole += [(self.r3.at[0, 0:rest], 2 + d) for d in range(1, self.n)]
        for ref, kind in whole:
            self.copy(ref, ref, 0, kind, self.pair).wait_send()
        for step in range(self.n + 1):
            self.early(first, step).wait_send()


class SmallSum:
    def __init__(self, shards, own, got, send, recv):
        self.n, self.own, self.got, self.send, self.recv = shards, own, got, send, recv
        self.s, self.c, self.t = (lax.axis_index(a) for a in ("shard", "ctx", "tp"))

    def copy(self, i):
        near = [{"tp": self.t + 1 - 2 * lax.rem(self.t, 2)}, {"tp": lax.rem(self.t + 2, 4)}, {"ctx": 1 - self.c}]
        device = near[i] if i < 3 else {"shard": lax.rem(self.s + i - 2, self.n)}
        return pltpu.make_async_remote_copy(
            src_ref=self.own.at[min(i, 3)], dst_ref=self.got.at[i], send_sem=self.send.at[i],
            recv_sem=self.recv.at[i], device_id=device, device_id_type=MESH,
        )

    def start(self, value):
        self.own[0] = value
        self.copy(0).start()

    def step(self, i):
        self.copy(i).wait_recv()
        self.own[i + 1] = self.own[i] + self.got[i]
        if i < 2:
            self.copy(i + 1).start()
        else:
            for d in range(1, self.n):
                self.copy(2 + d).start()

    def arrive(self, out):
        total = self.own[3]
        for d in range(1, self.n):
            self.copy(2 + d).wait_recv()
            total = total + self.got[2 + d]
        out[...] = total

    def drain(self):
        for i in range(2 + self.n):
            self.copy(i).wait_send()


class Spread:
    def __init__(self, src, dst, send, recv):
        self.src, self.dst, self.send, self.recv = src, dst, send, recv
        self.t = lax.axis_index("tp")

    def copy(self, d):
        to = lax.rem(self.t + d, 4)
        share = self.dst.shape[1]
        src = self.src.at[pl.ds(pl.multiple_of(to * share, share), share)]
        dst = self.dst.at[self.t]
        if d == 0:
            return pltpu.make_async_copy(src, dst, self.send.at[d])
        return pltpu.make_async_remote_copy(
            src_ref=src, dst_ref=dst, send_sem=self.send.at[d], recv_sem=self.recv.at[d],
            device_id={"tp": to}, device_id_type=MESH,
        )

    def start(self):
        for d in (2, 3, 1, 0):
            self.copy(d).start()

    def finish(self):
        for d in (1, 2, 3):
            self.copy(d).wait_recv()
            self.copy(d).wait_send()
        self.copy(0).wait()


class Share:
    def __init__(self, held, send, recv):
        self.held, self.send, self.recv = held, send, recv
        self.t = lax.axis_index("tp")
        self.pair_tp = self.t + 1 - 2 * lax.rem(self.t, 2)
        self.across_tp = lax.rem(self.t + 2, 4)

    def copy(self, i, tp, to):
        return pltpu.make_async_remote_copy(
            src_ref=self.held.at[tp], dst_ref=self.held.at[tp], send_sem=self.send.at[i],
            recv_sem=self.recv.at[i], device_id={"tp": to}, device_id_type=MESH,
        )

    def start(self):
        self.copy(0, self.t, self.across_tp).start()
        self.copy(1, self.t, self.pair_tp).start()

    def relay(self):
        self.copy(0, self.across_tp, self.across_tp).wait_recv()
        self.copy(2, self.across_tp, self.pair_tp).start()

    def finish(self):
        self.copy(1, self.pair_tp, self.pair_tp).wait_recv()
        self.copy(2, lax.rem(self.pair_tp + 2, 4), self.pair_tp).wait_recv()
        self.copy(0, self.t, self.across_tp).wait_send()
        self.copy(1, self.t, self.pair_tp).wait_send()
        self.copy(2, self.across_tp, self.pair_tp).wait_send()


class Comm:
    pass


def step_scratch(shards, pk, direct, tokens, slots, width):
    v, dma = pltpu.VMEM, pltpu.SemaphoreType.DMA
    n = shards
    out = dict(
        w=v((n * 4, TILES, width // (n * 4), width), BF),
        x=v((tokens, width), BF),
        m0=v((slots, width), F32),
        og=v((4, tokens // 4, width), BF),
        y=v((tokens, width), BF),
        xg=v((tokens, width), BF),
        mems=v((4, slots, width), BF),
        migs=v((4, slots, width), BF),
        small=v((8, width), F32),
        m_send=v((slots, width), BF),
        m_recv=v((slots, width), BF),
        g_send=v((slots, width), BF),
        g_recv=v((slots, width), BF),
        chain=dma((4,)),
        loads=dma((3,)),
        local=dma((TILES,)),
        w_send=dma((4,)),
        w_line_send=dma((2, n)),
        w_recv=dma((5, n, len(GROUPS))),
        w_pair_recv=dma((len(GROUPS),)),
        og_send=dma((4,)),
        og_recv=dma((4,)),
        y_send=dma((4,)),
        y_recv=dma((4,)),
        xg_send=dma((4,)),
        xg_recv=dma((4,)),
        mem_send=dma((3,)),
        mem_recv=dma((3,)),
        mig_send=dma((3,)),
        mig_recv=dma((3,)),
    )
    if direct:
        c = len(pk.chunks)
        lo, hi = pk.chunks[Reduce.ORDER.index(2)]
        early = hi - lo
        out.update(
            g=v(pk.shape, BF),
            r1=v((n, 2, 2, pk.rows, 128), BF),
            r2=v((n, 2, pk.rows, 128), BF),
            r3=v((n, pk.rows, 128), BF),
            z=v((n - 1, pk.rows, 128), BF),
            zz=v((n - 1, 2, 2, early, 128), BF),
            zx=v((2, early, 128), BF),
            zy=v((early, 128), BF),
            zsend=dma((n + 1,)),
            zrecv=dma((n + 1,)),
            own=v((4, 8, width), F32),
            got=v((2 + n, 8, width), F32),
            r_send=dma((2 + n,)),
            r_recv=dma((c, 2 + n)),
            s_send=dma((2 + n,)),
            s_recv=dma((2 + n,)),
        )
    return out


def step_kernel(dims, pk, direct, names, unit_names, *refs):
    shards, ctxs, halved = dims
    first, length, inputs, first_memory, memory_grad, out_grad = refs[:6]
    weights, gains, outs = refs[6:17], refs[17:21], refs[21:27]
    scratch = refs[27:]
    b = Comm()
    b.__dict__.update(zip(names, scratch))
    unit_refs = dict(zip(unit_names, scratch[len(names) :]))
    if not direct:
        b.g = outs[4]
    s, c, t = (lax.axis_index(a) for a in ("shard", "ctx", "tp"))
    u = Unit(unit_refs, Weights(b.w), b.x, gains, b.small)

    loads = [
        pltpu.make_async_copy(inputs.at[t], b.x, b.loads.at[0]),
        pltpu.make_async_copy(first_memory.at[t], b.m0, b.loads.at[1]),
        pltpu.make_async_copy(memory_grad.at[t], u.gm, b.loads.at[2]),
    ]
    copies = own_tiles(weights, b.w, s * 4 + t, b.local)
    for copy in copies + loads:
        copy.start()
    mine = pltpu.make_async_copy(out_grad.at[t], b.og.at[t], b.og_send.at[0])
    mine.start()
    peers = line_peers(shards) + tp_peers()
    if ctxs > 1:
        peers += [(c > 0, {"ctx": c - 1}), (c < ctxs - 1, {"ctx": c + 1})]
    greet(peers)
    gather = Gather(shards, halved, b.w, b.w_send, b.w_line_send, b.w_recv, b.w_pair_recv)

    def ready(g):
        for copy in copies[GROUPS[g][0] : GROUPS[g][1]]:
            copy.wait()

    lead, follow = pl.when(c == 0), pl.when(c > 0)
    pairs = u.width // 128
    chunks = u.ff // 512

    def on_lead(*calls):
        def run():
            @lead
            def _():
                for call in calls:
                    call()

        return run

    def take_memory():
        u.mem[...] = b.m0[...]
        u.memory_in()
        u.attend_memory()

    def project_and_attend():
        u.project_tokens()
        u.attend(0, 1)

    work = [(0, project_and_attend)]
    work += [(0, partial(u.attend, p, 1)) for p in range(1, pairs)]
    work += [
        (0, on_lead(take_memory)),
        (1, on_lead(u.after_attention)),
        (1, on_lead(partial(u.feed_forward_up, 0, chunks // 2))),
        (1, on_lead(partial(u.feed_forward_up, chunks // 2, chunks - chunks // 2))),
        (2, on_lead(u.feed_forward_down)),
    ]

    def between(complete):
        if work and work[0][0] <= complete:
            work.pop(0)[1]()

    def chain_copy(i, to):
        src, dst = ((b.m_send, b.m_recv), (b.g_send, b.g_recv))[i]
        return pltpu.make_async_remote_copy(
            src_ref=src, dst_ref=dst, send_sem=b.chain.at[2 * i], recv_sem=b.chain.at[2 * i + 1],
            device_id={"ctx": to}, device_id_type=MESH,
        )

    def og_copy(d):
        to = lax.rem(t + d, 4)
        return pltpu.make_async_remote_copy(
            src_ref=out_grad.at[to], dst_ref=b.og.at[t], send_sem=b.og_send.at[d],
            recv_sem=b.og_recv.at[d], device_id={"tp": to}, device_id_type=MESH,
        )

    spread_y = Spread(b.y, outs[0], b.y_send, b.y_recv)
    spread_xg = Spread(b.xg, outs[2], b.xg_send, b.xg_recv)
    share_mem = Share(b.mems, b.mem_send, b.mem_recv)
    share_mig = Share(b.migs, b.mig_send, b.mig_recv)
    gather.events(0, ready, between)
    for copy in loads:
        copy.wait()
    u.make_bias(first[0, t], length[0, t])
    gather.events(1, ready, between)
    u.tokens_in()
    for time in range(2, gather.last + 1):
        gather.events(time, ready, between)
    while work:
        work.pop(0)[1]()
    for d in (1, 2, 3):
        og_copy(d).start()

    if ctxs > 1:

        @follow
        def _():
            gather.drain()
            chain_copy(0, c - 1).wait_recv()
            u.mem[...] = b.m_recv[...].astype(F32)
            u.memory_in()
            u.attend_memory()
            u.after_attention()
            u.feed_forward_up(0, chunks)
            u.feed_forward_down()

    after = u.write_memory()
    b.m_send[...] = after.astype(BF)
    if ctxs > 1:

        @pl.when(c < ctxs - 1)
        def _():
            chain_copy(0, c + 1).start()

    b.mems[t] = after.astype(BF)
    b.y[...] = u.af[0 : u.tokens, :].astype(BF)
    share_mem.start()
    spread_y.start()
    u.backward_early()
    mine.wait()
    for d in (1, 2, 3):
        og_copy(d).wait_recv()
    share_mem.relay()

    @lead
    def _():
        gather.drain()

    if ctxs > 1:

        @pl.when(c < ctxs - 1)
        def _():
            chain_copy(1, c + 1).wait_recv()
            u.gm[...] += b.g_recv[...].astype(F32)

    def out_grad_rows(i):
        per = b.og.shape[1] // BLOCK
        return b.og[lax.div(i, per), pl.ds(lax.rem(i, per) * BLOCK, BLOCK), :].astype(F32)

    def grads(*which):
        weight_grads(u, b.g, pk, which)

    red = None
    if direct:
        early = (b.zz, b.zx, b.zy, b.zsend, b.zrecv)
        red = Reduce(shards, pk.chunks, b.g, b.r1, b.r2, b.r3, b.z, early, b.r_send, b.r_recv)
    sums = SmallSum(shards, b.own, b.got, b.s_send, b.s_recv) if direct else None
    WRITE, DOWN, UP, ENTER = (0, 1), (2, 3), (4, 5), (6, 7)

    def reduce(*todo):
        for what, chunks in todo if direct else ():
            for k in chunks:
                getattr(red, what)(k, *((outs[4],) if what == "arrive" else ()))

    u.write_back()

    @lead
    def _():
        grads("write")
        reduce(("start", WRITE))

    u.write_enter(out_grad_rows)

    @lead
    def _():
        grads("down")
        reduce(("start", DOWN), ("to_second", WRITE))

    u.feed_forward_back()

    @lead
    def _():
        grads("up")
        reduce(("start", UP), ("to_second", DOWN))

    u.feed_forward_enter()

    @lead
    def _():
        grads("wo")
        reduce(("to_second", UP))

    u.project_back()
    u.attend_back(0, pairs // 2)

    @lead
    def _():
        reduce(("to_third", WRITE))

    u.attend_back(pairs // 2, pairs - pairs // 2)
    u.queries_back()

    @lead
    def _():
        grads("enter")
        reduce(("start", ENTER), ("to_third", DOWN))

    u.enter_back()

    @lead
    def _():
        reduce(("to_second", ENTER), ("to_third", UP), ("to_last", WRITE))

    back = u.norm_enter(b.xg)
    b.migs[t] = back.astype(BF)

    if ctxs > 1:

        @follow
        def _():
            b.g_send[...] = back.astype(BF)
            chain_copy(1, c - 1).start()
            grads("write")
            reduce(("start", WRITE))
            grads("down")
            reduce(("start", DOWN))
            grads("up")
            reduce(("start", UP), ("to_second", WRITE))
            grads("wo", "enter")
            reduce(("start", ENTER), ("to_second", DOWN), ("to_second", UP), ("to_second", ENTER))

    share_mig.start()
    if direct:
        sums.start(b.small[...])

    def sum_step(i):
        if direct:
            sums.step(i)

    @lead
    def _():
        sum_step(0)
        reduce(("to_third", ENTER))
        spread_xg.start()
        reduce(("to_last", DOWN), ("to_last", UP))
        sum_step(1)

    if ctxs > 1:

        @follow
        def _():
            sum_step(0)
            spread_xg.start()
            reduce(("to_third", (0, 2, 4, 6)), ("to_third", (1, 3, 5)))
            sum_step(1)
            reduce(("to_last", WRITE), ("to_last", DOWN), ("to_third", (7,)), ("to_last", UP))

    share_mig.relay()
    reduce(("to_last", ENTER))
    sum_step(2)

    for spread in (spread_y, share_mem):
        spread.finish()
    reduce(*(("arrive", pair) for pair in (WRITE, DOWN, UP)))
    for spread in (share_mig, spread_xg):
        spread.finish()
    kept = [
        pltpu.make_async_copy(b.mems, outs[1], b.loads.at[0]),
        pltpu.make_async_copy(b.migs, outs[3], b.loads.at[1]),
    ]
    for copy in kept:
        copy.start()
    for d in (1, 2, 3):
        og_copy(d).wait_send()
    if ctxs > 1:

        @pl.when(c < ctxs - 1)
        def _():
            chain_copy(0, c + 1).wait_send()

        @pl.when(c > 0)
        def _():
            chain_copy(1, c - 1).wait_send()

    if direct:
        sums.arrive(outs[5])
        reduce(("arrive", ENTER))
        sums.drain()
        red.drain()
    else:
        outs[5][...] = b.small[...]
    for copy in kept:
        copy.wait()


def run_step(dims, pk, direct, first, length, inputs, first_memory, memory_grad, out_grad, weights, gains):
    _, tokens, width = inputs.shape
    slots = first_memory.shape[1]
    vm = pl.BlockSpec(memory_space=pltpu.VMEM)
    sm = pl.BlockSpec(memory_space=pltpu.SMEM)
    hbm = pl.BlockSpec(memory_space=pl.ANY)
    scratch = step_scratch(dims[0], pk, direct, tokens, slots, width)
    unit = unit_scratch(tokens, slots, width, pk.ff)
    shape = jax.ShapeDtypeStruct
    return pl.pallas_call(
        partial(step_kernel, dims, pk, direct, tuple(scratch), tuple(unit)),
        out_shape=(
            shape((4, tokens // 4, width), BF), shape((4, slots, width), BF),
            shape((4, tokens // 4, width), BF), shape((4, slots, width), BF),
            shape((pk.rows, 128) if direct else pk.shape, BF), shape((8, width), F32),
        ),
        in_specs=[sm, sm] + [hbm] * 15 + [vm] * 4,
        out_specs=(hbm, hbm, hbm, hbm, vm, vm),
        scratch_shapes=list(scratch.values()) + list(unit.values()),
        compiler_params=pltpu.CompilerParams(
            vmem_limit_bytes=VMEM_LIMIT, collective_id=1, has_side_effects=True
        ),
        name="step",
    )(first, length, inputs, first_memory, memory_grad, out_grad, *weights, *gains)


def store_kernel(pk, owners, *refs):
    rows_in, total, small = refs[:4], refs[4], refs[5]
    rows_out, (wq, wk, wv, wo, up, down, uq, uk, uv, uo, ugate), vectors = refs[6:10], refs[10:21], refs[21:]
    for src, dst in zip(rows_in, rows_out):
        dst[...] = src[...].astype(dst.dtype)

    def part(at, size):
        return total[at : at + size, :].astype(F32)

    h = pk.head_rows
    for name, ref in dict(wq=wq, wk=wk, wv=wv, uq=uq, uk=uk, uv=uv).items():
        ref[...] = part(pk.heads[name], h)
    for name, ref in dict(uo=uo, ugate=ugate).items():
        ref[...] = part(pk.heads[name], h)
    for at, r, ref in ((pk.at_wo, pk.row_rows, wo), (pk.at_up, pk.row_rows, up), (pk.at_down, pk.down_rows, down)):
        for j in range(ref.shape[1] // 128):
            ref[:, j * 128 : j * 128 + 128] = part(at + j * r, r)
    share = small.shape[1] // owners
    owner = lax.axis_index("shard")
    for axis in ("ctx", "tp"):
        owner = owner * lax.axis_size(axis) + lax.axis_index(axis)
    turned = pltpu.roll(small[...], small.shape[1] - owner * share, 1)
    for i, ref in enumerate(vectors):
        ref[...] = turned[i : i + 1, 0:share]


def run_store(pk, owners, rows, total, small):
    vm = pl.BlockSpec(memory_space=pltpu.VMEM)
    shape = jax.ShapeDtypeStruct
    width = small.shape[1]
    h = pk.head_rows
    head = shape((h, 128), F32)
    outs = tuple(shape(r.shape, d) for r, d in zip(rows, (BF, F32, BF, F32))) + (
        head, head, head, shape((pk.row_rows, width), F32), shape((pk.row_rows, pk.ff), F32),
        shape((pk.down_rows, width), F32), head, head, head, head, head,
    ) + (shape((1, width // owners), F32),) * 4
    return pl.pallas_call(
        partial(store_kernel, pk, owners),
        out_shape=outs,
        in_specs=[vm] * 6,
        out_specs=(vm,) * len(outs),
        compiler_params=pltpu.CompilerParams(vmem_limit_bytes=VMEM_LIMIT),
        name="store",
    )(*rows, total, small)


def full_gradients(pk, grads):
    groups, owners = pk.shards * pk.ctxs, pk.shards * pk.ctxs * 4
    by_head = grads.reshape(groups, 4, pk.rows, 128)
    by_owner = grads.reshape(owners, pk.rows, 128)

    def head(name):
        at = pk.heads[name]
        got = by_head[:, :, at : at + pk.head_rows]
        return got.transpose(0, 2, 1, 3).reshape(pk.width, pk.width).astype(F32)

    def rows(at, h, n):
        got = by_owner[:, at : at + h * n].reshape(owners, n, h, 128)
        return got.transpose(0, 2, 1, 3).reshape(owners * h, n * 128).astype(F32)

    return (
        head("wq"), head("wk"), head("wv"),
        rows(pk.at_wo, pk.row_rows, pk.width // 128),
        rows(pk.at_up, pk.row_rows, pk.ff // 128),
        rows(pk.at_down, pk.down_rows, pk.width // 128),
        head("uq"), head("uk"), head("uv"), head("uo").T, head("ugate").T,
    )


def local(
    inputs, first_memory, piece_start, piece_len,
    w_query, w_key, w_value, w_out, w_up, w_down, u_query, u_key, u_value, u_out, u_gate,
    gain_attn, gain_ffn, gain_write, gate_bias, out_grad, memory_grad,
):
    shards, ctxs, tps = (lax.axis_size(a) for a in ("shard", "ctx", "tp"))
    seqs, tokens, width = inputs.shape
    ff = w_up.shape[1]
    assert seqs == tps == 4 and tokens == width == 512 and ff == 2048
    weights = (w_query, w_key, w_value, w_out, w_up, w_down, u_query, u_key, u_value, u_out, u_gate)
    gains = [v.reshape(1, -1) for v in (gain_attn, gain_ffn, gain_write, gate_bias)]
    owners = shards * ctxs * tps
    direct = ctxs == 2 and width % (owners * 16) == 0
    halved = ctxs == 2 and w_query.shape[0] % 32 == 0
    pk = Packing(shards if direct else 4, 2, width, ff)
    got = run_step(
        (shards, ctxs, halved), pk, direct, piece_start.T, piece_len.T, inputs, first_memory, memory_grad,
        out_grad, weights, gains,
    )
    if direct:
        out = run_store(pk, owners, got[:4], got[4], got[5])
        return out[:13] + (out[13].T, out[14].T) + tuple(v.reshape(-1) for v in out[15:])
    every = ("shard", "ctx", "tp")
    out = [got[0], got[1].astype(F32), got[2], got[3].astype(F32)]
    for i, g in enumerate(full_gradients(pk, got[4])):
        if i in (3, 4, 5):
            out.append(lax.psum_scatter(g, every, scatter_dimension=0, tiled=True))
            continue
        sum_dim = 1 if i >= 9 else 0
        cut = lax.psum_scatter(g, "tp", scatter_dimension=1 - sum_dim, tiled=True)
        out.append(lax.psum_scatter(cut, ("shard", "ctx"), scatter_dimension=sum_dim, tiled=True))
    for i in range(4):
        out.append(lax.psum_scatter(got[5][i], every, scatter_dimension=0, tiled=True))
    return tuple(out)


def solution(mesh):
    cut = P(("shard", "tp"), None)
    head, rows, turned = P(("shard", "ctx"), "tp"), P(("shard", "ctx", "tp"), None), P("tp", ("shard", "ctx"))
    vector = P(("shard", "ctx", "tp"))
    over_rows, over_ctx = P("shard", ("ctx", "tp"), None), P("shard", "ctx", None)
    return jax.shard_map(
        local,
        mesh=mesh,
        in_specs=(over_ctx, P("shard", None, None), P("shard", "ctx"), P("shard", "ctx"))
        + (cut,) * 11 + (P(),) * 4 + (over_rows, over_ctx),
        out_specs=(over_rows, over_ctx, over_rows, over_ctx)
        + (head,) * 3 + (rows,) * 3 + (head,) * 3 + (turned,) * 2 + (vector,) * 4,
        check_vma=False,
    )
```

```python
from functools import partial

import jax
import jax.numpy as jnp
from jax import lax
from jax.experimental import pallas as pl
from jax.experimental.pallas import tpu as pltpu
from jax.sharding import PartitionSpec as P

F32 = jnp.float32
BF = jnp.bfloat16
MESH = pl.DeviceIdType.MESH
HEAD = 64
EPS = 1e-05
NEG = -1e30
VMEM_LIMIT = 67000000

WQ, WK, WV, WO, WUP, WDOWN, UQ, UK, UV, UO, UGATE = 0, 1, 2, 3, 4, 8, 12, 13, 14, 15, 16
TILES = 17


def dot(a, b):
    return lax.dot_general(a, b, (((1,), (0,)), ((), ())), preferred_element_type=F32)


def dot_nt(a, b):
    return lax.dot_general(a, b, (((1,), (1,)), ((), ())), preferred_element_type=F32)


def dot_tn(a, b):
    return lax.dot_general(a, b, (((0,), (0,)), ((), ())), preferred_element_type=F32)


def rows_at(i, size):
    return pl.ds(pl.multiple_of(i * size, size), size)


def loop(count, unroll=1):
    def run(body):
        def step(i, carry):
            body(i)
            return carry

        lax.fori_loop(0, count, step, 0, unroll=unroll)

    return run


BLOCK = 64
UNROLL = 4


def blocks(total, body, carry=None):
    def step(n, carry):
        for k in range(UNROLL):
            i = n * UNROLL + k
            carry = body(rows_at(i, BLOCK), i, carry)
        return carry

    return lax.fori_loop(0, total // (BLOCK * UNROLL), step, carry)


def fold(values):
    return jnp.sum(values.reshape(values.shape[0] // 8, 8, values.shape[1]), axis=0)


def normed(v):
    mean = jnp.mean(v, axis=-1, keepdims=True)
    centered = v - mean
    inv = lax.rsqrt(jnp.mean(centered * centered, axis=-1, keepdims=True) + EPS)
    return centered * inv, inv


def norm_pull(e, gain, hat, inv):
    h = e * gain
    m0 = jnp.mean(h, axis=-1, keepdims=True)
    m1 = jnp.mean(h * hat, axis=-1, keepdims=True)
    return inv * (h - m0 - hat * m1)


def lane_block(width, block):
    return lax.broadcasted_iota(jnp.int32, (1, width), 1) // block


class Weights:
    def __init__(self, ref):
        self.ref = ref
        self.blocks, _, self.rows, self.width = ref.shape

    def cols(self, tile, start, size):
        got = self.ref[:, tile, :, pl.ds(start, size)]
        return got.reshape(self.blocks * self.rows, size)

    def row_part(self, tile, part, parts):
        count = self.blocks // parts
        got = self.ref[pl.ds(part * count, count), tile]
        return got.reshape(count * self.rows, self.width)

    def down_cols(self, chunk, chunks, start, size):
        count = self.blocks // chunks
        got = self.ref[pl.ds(chunk * count, count), WDOWN : WDOWN + 4, :, pl.ds(start, size)]
        return got.reshape(count * 4 * self.rows, size)

    def down_rows(self, part, parts):
        count = self.blocks // parts
        got = self.ref[pl.ds(part * count, count), WDOWN : WDOWN + 4]
        return got.reshape(count * 4 * self.rows, self.width)


def unit_scratch(tokens, slots, width, ff):
    r = tokens + slots
    heads = width // HEAD
    quads = width // 256
    v = pltpu.VMEM
    return dict(
        mem=v((slots, width), F32),
        xh=v((r, width), F32),
        xr=v((r, 1), F32),
        enc=v((r, width), BF),
        q=v((tokens, width), BF),
        k=v((r, width), BF),
        v=v((r, width), BF),
        kt=v((width, r), BF),
        vt=v((width, r), BF),
        pt=v((heads, r, tokens), BF),
        ptop=v((heads, 1, tokens), F32),
        psum=v((heads, 1, tokens), F32),
        pinv=v((heads, 1, tokens), F32),
        top=v((2, 1, 256), F32),
        mixt=v((width, tokens), BF),
        af=v((r, width), F32),
        ah=v((tokens, width), F32),
        ar=v((tokens, 1), F32),
        fin=v((tokens, width), BF),
        act=v((ff // 512, tokens, 512), BF),
        dg=v((ff // 512, tokens, 512), BF),
        yh=v((tokens, width), F32),
        yr=v((tokens, 1), F32),
        wri=v((r, width), BF),
        sq=v((slots, width), BF),
        sk=v((r, width), BF),
        sv=v((r, width), BF),
        spt=v((quads, r, 256), BF),
        wrt=v((slots, width), BF),
        gate=v((slots, width), F32),
        f1=v((slots, width), F32),
        f2=v((slots, width), F32),
        gm=v((slots, width), F32),
        gup=v((slots, width), BF),
        ggl=v((slots, width), BF),
        dsq=v((slots, width), BF),
        dsk=v((r, width), BF),
        dsv=v((r, width), BF),
        e=v((r, width), F32),
        gy=v((tokens, width), F32),
        gyb=v((tokens, width), BF),
        bwm=v((slots, width), F32),
        folded=v((8, width), F32),
        gpre=v((ff // 512, tokens, 512), BF),
        gab=v((tokens, width), BF),
        gmx=v((tokens, width), BF),
        dst=v((2, r, tokens), BF),
        dqt=v((width, tokens), BF),
        dq=v((tokens, width), BF),
        dk=v((r, width), BF),
        dv=v((r, width), BF),
    )


class Unit:
    def __init__(self, refs, w, x, gains, small):
        self.__dict__.update(refs)
        self.w = w
        self.x = x
        self.gains = gains
        self.small = small
        self.tokens, self.width = x.shape
        self.slots = self.mem.shape[0]
        self.r = self.tokens + self.slots
        self.ff = self.act.shape[0] * 512

    def gain(self, i):
        return self.gains[i][...]

    def make_bias(self, first, length):
        t = self.tokens

        @loop(t // 64)
        def _(i):
            key = lax.broadcasted_iota(jnp.int32, (64, t), 0) + i * 64
            query = lax.broadcasted_iota(jnp.int32, (64, t), 1)
            last = first + length
            inside = (key >= first) & (key < last) & (query >= first) & (query < last)
            seen = (key <= query) | inside
            self.e[rows_at(i, 64), :] = jnp.where(seen, 0.0, NEG).astype(F32)

    def norm_in(self, rows, values):
        hat, inv = normed(values)
        self.xh[rows, :] = hat
        self.xr[rows, :] = inv
        self.enc[rows, :] = (hat * self.gain(0)).astype(BF)

    def tokens_in(self):
        def body(rows, i, carry):
            self.norm_in(rows, self.x[rows, :].astype(F32))

        blocks(self.tokens, body)

    def project_tokens(self):
        t = self.tokens

        @loop(self.width // 256)
        def _(n):
            cols = rows_at(n, 256)
            enc = self.enc[0:t, :]
            got = dot(enc, self.w.cols(WQ, n * 256, 256)).astype(BF)
            self.q[:, cols] = got * BF(HEAD**-0.5)
            self.k[0:t, cols] = dot(enc, self.w.cols(WK, n * 256, 256)).astype(BF)
            self.v[0:t, cols] = dot(enc, self.w.cols(WV, n * 256, 256)).astype(BF)

        self.vt[:, 0:t] = self.v[0:t, :].T

    def memory_in(self):
        t, r = self.tokens, self.r
        self.norm_in(slice(t, r), self.mem[...])
        enc = self.enc[t:r, :]
        self.k[t:r, :] = dot(enc, self.w.cols(WK, 0, self.width)).astype(BF)
        self.v[t:r, :] = dot(enc, self.w.cols(WV, 0, self.width)).astype(BF)
        self.vt[:, t:r] = self.v[t:r, :].T

    def held(self, j):
        return self.af.at[:, j % 2 * 256 : j % 2 * 256 + 256]

    def attend(self, first, count):
        t = self.tokens
        span = 256

        @loop(count)
        def _(i):
            p = i + first
            cols = rows_at(p, 128)
            half = lane_block(128, HEAD)
            steps = [(hh, n) for hh in range(2) for n in range(t // span)]

            def score(j):
                hh, n = steps[j]
                qc = slice(n * span, n * span + span)
                q = self.q[qc, cols]
                s = dot_nt(self.k[0:t, cols], jnp.where(half == hh, q, jnp.zeros_like(q)))
                part = s[n * span : t] + self.e[n * span : t, qc]
                top = jnp.max(part, axis=0, keepdims=True)
                self.held(j)[n * span : t, :] = part
                if n > 0:
                    self.held(j)[0 : n * span, :] = s[0 : n * span]
                    top = jnp.maximum(top, jnp.max(s[0 : n * span], axis=0, keepdims=True))
                self.ptop[2 * p + hh, :, qc] = top

            def soften(j):
                hh, n = steps[j]
                qc = slice(n * span, n * span + span)
                e = jnp.exp(self.held(j)[0:t, :] - self.ptop[2 * p + hh, :, qc])
                self.psum[2 * p + hh, :, qc] = jnp.sum(e, axis=0, keepdims=True)
                self.pt[2 * p + hh, 0:t, qc] = e.astype(BF)

            def mix(j):
                hh, n = steps[j]
                qc = slice(n * span, n * span + span)
                feats = pl.ds(pl.multiple_of(p * 128 + hh * HEAD, HEAD), HEAD)
                self.yh[feats, qc] = dot(self.vt[feats, 0:t], self.pt[2 * p + hh, 0:t, qc])

            score(0)
            for j in range(len(steps)):
                if j + 1 < len(steps):
                    score(j + 1)
                soften(j)
                mix(j)

    def attend_memory(self):
        t, r = self.tokens, self.r

        @loop(self.width // 128)
        def _(p):
            cols = rows_at(p, 128)
            half = lane_block(128, HEAD)
            for hh in range(2):
                h = 2 * p + hh
                feats = pl.ds(pl.multiple_of(p * 128 + hh * HEAD, HEAD), HEAD)
                q = self.q[:, cols]
                s = dot_nt(self.k[t:r, cols], jnp.where(half == hh, q, jnp.zeros_like(q)))
                top = jnp.maximum(self.ptop[h], jnp.max(s, axis=0, keepdims=True))
                fade = jnp.exp(self.ptop[h] - top)
                e = jnp.exp(s - top)
                inv = 1.0 / (fade * self.psum[h] + jnp.sum(e, axis=0, keepdims=True))
                self.pinv[h] = inv
                low = e.astype(BF)
                self.pt[h, t:r, :] = low
                got = self.yh[feats, :] * fade + dot(self.vt[feats, t:r], low)
                self.mixt[feats, :] = (got * inv).astype(BF)
                for m in range(t // 64):
                    rows = slice(m * 64, m * 64 + 64)
                    self.pt[h, rows, :] = (self.pt[h, rows, :].astype(F32) * fade).astype(BF)

    def after_attention(self):
        t = self.tokens
        self.gmx[...] = self.mixt[...].T

        @loop(self.width // 256)
        def _(n):
            cols = rows_at(n, 256)
            got = dot(self.gmx[...], self.w.cols(WO, n * 256, 256))
            self.af[0:t, cols] = self.x[:, cols].astype(F32) + got

        def body(rows, i, carry):
            hat, inv = normed(self.af[rows, :])
            self.ah[rows, :] = hat
            self.ar[rows, :] = inv
            self.fin[rows, :] = (hat * self.gain(1)).astype(BF)

        blocks(t, body)

    def feed_forward_up(self, first, count):
        t = self.tokens
        c = 0.7978845608028654

        @loop(count)
        def _(i):
            j = i + first

            def project(n):
                part = slice(n * 256, n * 256 + 256)
                self.gy[:, part] = dot(self.fin[...], self.w.cols(WUP + j, n * 256, 256))

            def activate(n):
                part = slice(n * 256, n * 256 + 256)
                for m in range(t // 64):
                    rows = slice(m * 64, m * 64 + 64)
                    pre = self.gy[rows, part]
                    sq = pre * pre
                    th = jnp.tanh(pre * (c + (c * 0.044715) * sq))
                    half = 0.5 + 0.5 * th
                    self.act[j, rows, part] = (pre * half).astype(BF)
                    slope = half + (0.5 * pre) * (1.0 - th * th) * (c + (3 * c * 0.044715) * sq)
                    self.dg[j, rows, part] = slope.astype(BF)

            project(0)
            project(1)
            activate(0)
            activate(1)

    def feed_forward_down(self):
        t = self.tokens

        @loop(self.width // 256)
        def _(n):
            cols = rows_at(n, 256)
            total = self.af[0:t, cols]
            for j in range(self.ff // 512):
                total = total + dot(
                    self.act[j], self.w.down_cols(j, self.ff // 512, n * 256, 256)
                )
            self.af[0:t, cols] = total

        def body(rows, i, carry):
            hat, inv = normed(self.af[rows, :])
            self.yh[rows, :] = hat
            self.yr[rows, :] = inv
            self.wri[rows, :] = (hat * self.gain(2)).astype(BF)

        blocks(t, body)

        self.wri[t : self.r, :] = (self.xh[t : self.r, :] * self.gain(2)).astype(BF)

    def spread_heads(self, rows, g):
        part = rows[:, g * 256 : g * 256 + 256]
        block = lane_block(256, HEAD)
        return jnp.concatenate(
            [jnp.where(block == h, part, jnp.zeros_like(part)) for h in range(4)], axis=0
        )

    def gather_heads(self, stacked):
        block = lane_block(256, HEAD)
        s = self.slots
        total = jnp.where(block == 0, stacked[0:s], 0.0)
        for h in range(1, 4):
            total = total + jnp.where(block == h, stacked[h * s : h * s + s], 0.0)
        return total

    def write_memory(self):
        t, r = self.tokens, self.r

        @loop(self.width // 256)
        def _(n):
            cols = rows_at(n, 256)
            wri = self.wri[...]
            self.sk[:, cols] = dot(wri, self.w.cols(UK, n * 256, 256)).astype(BF)
            self.sv[:, cols] = dot(wri, self.w.cols(UV, n * 256, 256)).astype(BF)

        wm = self.wri[t:r, :]
        sq = dot(wm, self.w.cols(UQ, 0, self.width)).astype(BF)
        self.sq[...] = sq * BF(HEAD**-0.5)
        for g in range(self.width // 256):
            cols = slice(g * 256, g * 256 + 256)
            s = dot_nt(self.sk[:, cols], self.spread_heads(self.sq[...], g))
            e = jnp.exp(s - jnp.max(s, axis=0, keepdims=True))
            probs = (e * (1.0 / jnp.sum(e, axis=0, keepdims=True))).astype(BF)
            self.spt[g] = probs
            self.wrt[:, cols] = self.gather_heads(dot_tn(probs, self.sv[:, cols])).astype(BF)
        th = jnp.tanh(dot(self.wrt[...], self.w.cols(UO, 0, self.width)))
        pre = dot(wm, self.w.cols(UGATE, 0, self.width))
        gate = jax.nn.sigmoid(pre + self.gain(3))
        mem = self.mem[...]
        self.gate[...] = gate
        self.f1[...] = (mem - th) * gate * (1.0 - gate)
        self.f2[...] = (1.0 - gate) * (1.0 - th * th)
        return gate * mem + (1.0 - gate) * th

    def backward_early(self):
        self.kt[...] = self.k[...].T

    def write_back(self):
        gm = self.gm[...]
        ggp = gm * self.f1[...]
        gup = (gm * self.f2[...]).astype(BF)
        ggl = ggp.astype(BF)
        self.gup[...] = gup
        self.ggl[...] = ggl
        self.small[3:4, :] = jnp.sum(ggp, axis=0, keepdims=True)
        gwr = dot_nt(gup, self.w.row_part(UO, 0, 1)).astype(BF)
        quads = range(self.width // 256)
        cols = [slice(g * 256, g * 256 + 256) for g in quads]
        grads = [self.spread_heads(gwr, g) for g in quads]
        for g in quads:
            self.af[:, cols[g]] = dot_nt(self.sv[:, cols[g]], grads[g])
        for g in quads:
            self.dsv[:, cols[g]] = dot(self.spt[g], grads[g]).astype(BF)
        for g in quads:
            pf = self.spt[g].astype(F32)
            dp = self.af[:, cols[g]]
            self.dst[0, :, cols[g]] = (pf * (dp - jnp.sum(pf * dp, axis=0, keepdims=True))).astype(BF)
        for g in quads:
            dq = self.gather_heads(dot_tn(self.dst[0, :, cols[g]], self.sk[:, cols[g]])) * HEAD**-0.5
            self.dsq[:, cols[g]] = dq.astype(BF)
            self.dsk[:, cols[g]] = dot(self.dst[0, :, cols[g]], self.spread_heads(self.sq[...], g)).astype(BF)

    def write_enter(self, out_grad):
        t, r = self.tokens, self.r

        @loop(2)
        def _(n):
            cols = rows_at(n, self.width // 2)
            self.e[:, cols] = dot_nt(self.dsk[...], self.w.row_part(UK, n, 2)) + dot_nt(
                self.dsv[...], self.w.row_part(UV, n, 2)
            )

        em = self.e[t:r, :] + dot_nt(self.dsq[...], self.w.row_part(UQ, 0, 1))
        em = em + dot_nt(self.ggl[...], self.w.row_part(UGATE, 0, 1))
        hat = self.xh[t:r, :]
        self.bwm[...] = norm_pull(em, self.gain(2), hat, self.xr[t:r, :])

        def body(rows, i, carry):
            e = self.e[rows, :]
            hat = self.yh[rows, :]
            grad = out_grad(i) + norm_pull(e, self.gain(2), hat, self.yr[rows, :])
            self.gy[rows, :] = grad
            self.gyb[rows, :] = grad.astype(BF)
            return carry + fold(e * hat)

        total = blocks(t, body, fold(em * hat))
        self.small[2:3, :] = jnp.sum(total, axis=0, keepdims=True)

    def feed_forward_back(self):
        chunks = self.ff // 512

        @loop(chunks)
        def _(j):
            for n in range(2):
                cols = slice(n * 256, n * 256 + 256)
                got = dot_nt(self.gyb[...], self.w.down_rows(2 * j + n, 2 * chunks))
                self.gpre[j, :, cols] = (got * self.dg[j, :, cols].astype(F32)).astype(BF)

    def feed_forward_enter(self):
        t = self.tokens
        chunks = self.ff // 512

        @loop(2)
        def _(n):
            cols = rows_at(n, self.width // 2)
            total = dot_nt(self.gpre[0], self.w.row_part(WUP, n, 2))
            for j in range(1, chunks):
                total = total + dot_nt(self.gpre[j], self.w.row_part(WUP + j, n, 2))
            self.e[0:t, cols] = total

        def body(rows, i, carry):
            e = self.e[rows, :]
            hat = self.ah[rows, :]
            grad = self.gy[rows, :] + norm_pull(e, self.gain(1), hat, self.ar[rows, :])
            self.gy[rows, :] = grad
            self.gab[rows, :] = grad.astype(BF)
            return carry + fold(e * hat)

        total = blocks(t, body, jnp.zeros((8, self.width), F32))
        self.small[1:2, :] = jnp.sum(total, axis=0, keepdims=True)

    def project_back(self):
        heads = self.pinv.shape[0]
        inv = jnp.concatenate([self.pinv[h] for h in range(heads)], axis=0).T
        for n in range(2):
            cols = slice(n * 256, n * 256 + 256)
            block = lane_block(256, HEAD)
            scale = inv[:, 4 * n : 4 * n + 1]
            for h in range(1, 4):
                scale = jnp.where(block >= h, inv[:, 4 * n + h : 4 * n + h + 1], scale)
            self.gmx[:, cols] = (dot_nt(self.gab[...], self.w.row_part(WO, n, 2)) * scale).astype(BF)

    def attend_back(self, first, count):
        t, r = self.tokens, self.r
        span = 256

        @loop(count)
        def _(i):
            p = i + first
            cols = rows_at(p, 128)
            half = lane_block(128, HEAD)
            steps = [(hh, n) for hh in range(2) for n in range(t // span)]

            def score(j):
                hh, n = steps[j]
                qc = slice(n * span, n * span + span)
                g = self.gmx[qc, cols]
                dp = dot_nt(self.v[:, cols], jnp.where(half == hh, g, jnp.zeros_like(g)))
                self.held(j)[...] = dp
                total = jnp.sum(self.pt[2 * p + hh, :, qc].astype(F32) * dp, axis=0, keepdims=True)
                self.top[j % 2] = total * self.pinv[2 * p + hh, :, qc]

            def soften(j):
                hh, n = steps[j]
                qc = slice(n * span, n * span + span)
                e = self.pt[2 * p + hh, :, qc].astype(F32)
                self.dst[hh, :, qc] = (e * (self.held(j)[...] - self.top[j % 2])).astype(BF)

            def queries(j):
                hh, n = steps[j]
                qc = slice(n * span, n * span + span)
                feats = pl.ds(pl.multiple_of(p * 128 + hh * HEAD, HEAD), HEAD)
                got = dot(self.kt[feats, :], self.dst[hh, :, qc])
                self.dqt[feats, qc] = (got * HEAD**-0.5).astype(BF)

            def keys(hh):
                dv = dot(self.pt[2 * p + hh], self.gmx[:, cols]).astype(BF)
                dk = dot(self.dst[hh], self.q[:, cols]).astype(BF)
                if hh == 1:
                    dv = jnp.where(half == 0, self.dv[:, cols], dv)
                    dk = jnp.where(half == 0, self.dk[:, cols], dk)
                self.dv[:, cols] = dv
                self.dk[:, cols] = dk

            score(0)
            for j in range(len(steps)):
                if j + 1 < len(steps):
                    score(j + 1)
                soften(j)
                if j == len(steps) - 2:
                    keys(0)
                queries(j)
            keys(1)

    def queries_back(self):
        self.dq[...] = self.dqt[...].T

    def enter_memory(self):
        t, r = self.tokens, self.r
        e = dot_nt(self.dk[t:r, :], self.w.row_part(WK, 0, 1)) + dot_nt(
            self.dv[t:r, :], self.w.row_part(WV, 0, 1)
        )
        hat = self.xh[t:r, :]
        self.folded[...] = fold(e * hat)
        back = self.gm[...] * self.gate[...] + self.bwm[...]
        return back + norm_pull(e, self.gain(0), hat, self.xr[t:r, :])

    def enter_back(self):
        t = self.tokens

        @loop(2)
        def _(n):
            cols = rows_at(n, self.width // 2)
            self.e[0:t, cols] = (
                dot_nt(self.dk[0:t, :], self.w.row_part(WK, n, 2))
                + dot_nt(self.dv[0:t, :], self.w.row_part(WV, n, 2))
                + dot_nt(self.dq[...], self.w.row_part(WQ, n, 2))
            )

    def norm_enter(self, input_grad):
        t = self.tokens

        def body(rows, i, carry):
            e = self.e[rows, :]
            hat = self.xh[rows, :]
            grad = self.gy[rows, :] + norm_pull(e, self.gain(0), hat, self.xr[rows, :])
            input_grad[rows, :] = grad.astype(BF)
            return carry + fold(e * hat)

        total = blocks(t, body, self.folded[...])
        self.small[0:1, :] = jnp.sum(total, axis=0, keepdims=True)


class Packing:
    def __init__(self, shards, ctxs, width, ff):
        self.shards, self.ctxs, self.width, self.ff = shards, ctxs, width, ff
        self.head_rows = h = width // (shards * ctxs)
        self.row_rows = width // (shards * ctxs * 4)
        self.down_rows = ff // (shards * ctxs * 4)
        at = 0
        self.heads = {}
        bounds = [at]
        for name in ("uq", "uk", "uv", "uo", "ugate"):
            self.heads[name] = at
            at += h
        bounds.append(at)
        self.at_down = at
        at += self.down_rows * (width // 128)
        bounds.append(at)
        self.at_up = at
        at += self.row_rows * (ff // 128)
        bounds.append(at)
        self.at_wo = at
        at += self.row_rows * (width // 128)
        for name in ("wq", "wk", "wv"):
            self.heads[name] = at
            at += h
        self.rows = at
        bounds.append(at)
        chunks = []
        for lo, hi in zip(bounds[:-1], bounds[1:]):
            middle = lo + (hi - lo) // 2 // 16 * 16
            chunks += [(lo, middle), (middle, hi)]
        self.chunks = tuple(chunks)

    @property
    def shape(self):
        return (self.shards, self.ctxs, 2, 2, self.rows, 128)


def weight_grads(u, g, pk, names):
    width = u.width
    tile = 256

    def store_head(at, m, got):
        h = pk.head_rows
        per = tile // h
        for i in range(per):
            s = m * (per // pk.ctxs) + i // pk.ctxs
            for t in range(4):
                g[s, i % pk.ctxs, t // 2, t % 2, at : at + h, :] = got[
                    i * h : i * h + h, t * 128 : t * 128 + 128
                ]

    def store_rows(at, h, m, got, chunk0):
        per = tile // h
        for i in range(per):
            if per % (pk.ctxs * 4) == 0:
                s, c = m * (per // (pk.ctxs * 4)) + i // (pk.ctxs * 4), (i // 4) % pk.ctxs
            else:
                owner = m * (per // 4) + i // 4
                s, c = lax.div(owner, pk.ctxs), lax.rem(owner, pk.ctxs)
            for j in range(got.shape[1] // 128):
                lo = at + (chunk0 + j) * h
                g[s, c, (i // 2) % 2, i % 2, lo : lo + h, :] = got[
                    i * h : i * h + h, j * 128 : j * 128 + 128
                ]

    def heads(left, items):
        @loop(width // tile)
        def _(m):
            lt = left[:, rows_at(m, tile)].T
            for name, lo, hi, right in items:
                store_head(pk.heads[name], m, dot(lt[:, lo:hi], right[...]).astype(BF))

    t, r = u.tokens, u.r
    if "down" in names:
        for j in range(u.ff // 512):

            @loop(512 // tile)
            def _(m, j=j):
                lt = u.act[j, :, rows_at(m, tile)].T
                got = dot(lt, u.gyb[...]).astype(BF)
                store_rows(pk.at_down, pk.down_rows, m + j * (512 // tile), got, 0)

    if "up" in names:

        @loop(width // tile)
        def _(m):
            lt = u.fin[:, rows_at(m, tile)].T
            for j in range(u.ff // 512):
                store_rows(pk.at_up, pk.row_rows, m, dot(lt, u.gpre[j]).astype(BF), 4 * j)

    if "wo" in names:

        @loop(width // tile)
        def _(m):
            got = dot(u.mixt[rows_at(m, tile), :], u.gab[...]).astype(BF)
            store_rows(pk.at_wo, pk.row_rows, m, got, 0)

    if "write" in names:
        heads(u.wri, (("uq", t, r, u.dsq), ("uk", 0, r, u.dsk), ("uv", 0, r, u.dsv)))
        heads(u.gup, (("uo", 0, r - t, u.wrt),))
        heads(u.ggl, (("ugate", 0, r - t, u.wri.at[t:r]),))
    if "enter" in names:
        heads(u.enc, (("wq", 0, t, u.dq), ("wk", 0, r, u.dk), ("wv", 0, r, u.dv)))


GROUPS = ((0, 3), (3, 8), (8, 12), (12, 17))


def greet(peers):
    barrier = pltpu.get_barrier_semaphore()
    count = 0
    for cond, device in peers:

        @pl.when(cond)
        def _(device=device):
            pl.semaphore_signal(barrier, inc=1, device_id=device, device_id_type=MESH)

        count = count + jnp.where(cond, 1, 0)
    pl.semaphore_wait(barrier, count)


class Gather:
    UP, DOWN, ACROSS, BESIDE, FAR, PAIR, PAIR_ACROSS, PAIR_BESIDE, PAIR_FAR = range(9)
    LINKS = {ACROSS: 0, BESIDE: 1, FAR: 2, PAIR: 3, PAIR_ACROSS: 3, PAIR_BESIDE: 3, PAIR_FAR: 3}

    def __init__(self, shards, halved, w, send, line_send, recv, pair_recv):
        self.n, self.halved, self.w = shards, halved, w
        self.send, self.line_send, self.recv, self.pair_recv = send, line_send, recv, pair_recv
        self.s, self.c, self.t = (lax.axis_index(a) for a in ("shard", "ctx", "tp"))
        odd = lax.rem(self.t, 2)
        self.pair_tp = self.t + 1 - 2 * odd
        self.across_tp = lax.rem(self.t + 2, 4)
        self.pair = {"tp": self.pair_tp}
        self.across = {"tp": self.across_tp}
        self.beside = {"ctx": self.c + 1 - 2 * lax.rem(self.c, 2)}

    def copy(self, kind, source, tp, g, device, half=None):
        lo, hi = GROUPS[g]
        block = self.w.at[source * 4 + tp, lo:hi]
        if half is not None:
            size = self.w.shape[2] // 2
            block = self.w.at[source * 4 + tp, lo:hi, pl.ds(pl.multiple_of(half * size, size), size)]
        return self.between(block, kind, source, g, device)

    def between(self, block, kind, source, g, device):
        if kind in (self.UP, self.DOWN):
            send = self.line_send.at[kind, source]
        else:
            send = self.send.at[self.LINKS[kind]]
        to_pair = kind in (self.PAIR, self.PAIR_ACROSS, self.PAIR_BESIDE, self.PAIR_FAR)
        recv = self.pair_recv.at[g] if to_pair else self.recv.at[kind, source, g]
        return pltpu.make_async_remote_copy(
            src_ref=block, dst_ref=block, send_sem=send, recv_sem=recv, device_id=device, device_id_type=MESH,
        )

    @property
    def mine(self):
        return self.c if self.halved else None

    @property
    def others(self):
        return 1 - self.c

    def up(self, source, g, far):
        return self.copy(self.UP, source, self.t, g, {"shard": self.s + 1}, self.mine if far else None)

    def down(self, source, g, far):
        return self.copy(self.DOWN, source, self.t, g, {"shard": self.s - 1}, self.mine if far else None)

    def to_across(self, source, g, tp=None):
        return self.copy(self.ACROSS, source, self.t if tp is None else tp, g, self.across, self.mine)

    def to_pair(self, source, g, far, tp=None):
        return self.copy(self.PAIR, source, self.t if tp is None else tp, g, self.pair, self.mine if far else None)

    def far(self, d):
        return self.halved and d == self.n - 1

    def start_own(self, g):
        s, n = self.s, self.n
        if n > 1:

            @pl.when(s < n - 1)
            def _():
                self.up(s, g, self.far(1)).start()

            @pl.when(s > 0)
            def _():
                self.down(s, g, self.far(1)).start()

        self.to_across(s, g).start()
        self.to_pair(s, g, False).start()

    def came(self, source, g, d):
        self.to_across(source, g).start()
        self.to_pair(source, g, self.far(d)).start()
        if self.far(d):
            self.copy(self.FAR, source, self.t, g, self.beside, self.c).start()

    def line_step(self, d, g):
        s, n = self.s, self.n

        @pl.when(s - d >= 0)
        def _():
            self.up(s - d, g, self.far(d)).wait_recv()

            @pl.when(s < n - 1)
            def _():
                self.up(s - d, g, self.far(d + 1)).start()

            self.came(s - d, g, d)

        @pl.when(s + d <= n - 1)
        def _():
            self.down(s + d, g, self.far(d)).wait_recv()

            @pl.when(s > 0)
            def _():
                self.down(s + d, g, self.far(d + 1)).start()

            self.came(s + d, g, d)

    def sources(self, d):
        s, n = self.s, self.n
        both = ((s - d, s - d >= 0), (s + d, s + d <= n - 1))
        return both[:1] if d == 0 else both

    def across_step(self, d, g):
        for source, cond in self.sources(d):

            @pl.when(cond)
            def _(source=source):
                tp = self.across_tp
                self.to_across(source, g, tp).wait_recv()
                self.copy(self.PAIR_ACROSS, source, tp, g, self.pair, self.mine).start()
                if self.halved:
                    self.copy(self.BESIDE, source, tp, g, self.beside, self.c).start()

    def beside_step(self, d, g):
        if not self.halved:
            return
        for source, cond in self.sources(d):

            @pl.when(cond)
            def _(source=source):
                tp = self.across_tp
                self.copy(self.BESIDE, source, tp, g, self.beside, self.others).wait_recv()
                self.copy(self.PAIR_BESIDE, source, tp, g, self.pair, self.others).start()

    def far_step(self, g):
        if not self.halved:
            return
        for source, cond in self.sources(self.n - 1):

            @pl.when(cond)
            def _(source=source):
                self.copy(self.FAR, source, self.t, g, self.beside, self.others).wait_recv()
                self.copy(self.PAIR_FAR, source, self.t, g, self.pair, self.others).start()

    def finish(self, g):
        lo, hi = GROUPS[g]
        self.between(self.w.at[0 : 2 * self.n, lo:hi], self.PAIR, 0, g, self.pair).wait_recv()

    def drain(self):
        s, n = self.s, self.n
        parts = n // 2 if self.halved else n
        half = self.w.at[0, :, 0 : self.w.shape[2] // 2]
        self.between(self.w.at[0 : 2 * n], self.PAIR, 0, 0, self.pair).wait_send()
        self.between(self.w.at[0:parts], self.ACROSS, 0, 0, self.across).wait_send()
        if self.halved:
            self.between(self.w.at[0:parts], self.BESIDE, 0, 0, self.beside).wait_send()

            @pl.when(jnp.logical_or(s == 0, s == n - 1))
            def _():
                self.between(half, self.FAR, 0, 0, self.beside).wait_send()

        for d in range(n - 1):
            block = half if self.far(d + 1) else self.w.at[0]

            @pl.when(jnp.logical_and(s - d >= 0, s < n - 1))
            def _(d=d, block=block):
                self.between(block, self.UP, s - d, 0, {"shard": s + 1}).wait_send()

            @pl.when(jnp.logical_and(s + d <= n - 1, s > 0))
            def _(d=d, block=block):
                self.between(block, self.DOWN, s + d, 0, {"shard": s - 1}).wait_send()

    def events(self, time, ready, between):
        n = self.n
        groups = range(len(GROUPS))
        for g in groups:
            if time == max(g - 1, 0):
                ready(g)
                self.start_own(g)
        for g in groups:
            d = time - g
            if not 1 <= d <= n + 1:
                continue
            if d <= n - 1:
                self.line_step(d, g)
            if d <= n:
                self.across_step(d - 1, g)
            if d >= 2:
                self.beside_step(d - 2, g)
            if d == n + 1:
                self.far_step(g)
                self.finish(g)
            between(time - n - 1 if g >= time - n - 1 else -1)

    @property
    def last(self):
        return (len(GROUPS) - 1) + self.n + 1


def line_peers(n):
    s = lax.axis_index("shard")
    return [(s >= 0, {"shard": lax.rem(s + d, n)}) for d in range(1, n)]


def tp_peers():
    t = lax.axis_index("tp")
    return [(t >= 0, {"tp": lax.rem(t + d, 4)}) for d in (1, 2, 3)]


def own_tiles(weights, w, own, sems):
    names = [WQ, WK, WV, WO, WUP, WDOWN, UQ, UK, UV, UO, UGATE]
    rows = w.shape[2]
    out = []
    for name, ref in zip(names, weights):
        parts = {WUP: 4, WDOWN: 4}.get(name, 1)
        for j in range(parts):
            src = ref
            if name == WUP:
                src = ref.at[:, j * 512 : j * 512 + 512]
            if name == WDOWN:
                src = ref.at[j * rows : j * rows + rows]
            out.append(pltpu.make_async_copy(src, w.at[own, name + j], sems.at[name + j]))
    return out


class Reduce:
    ORDER = (0, 2, 0, 1, 0, 1, 0, 1)

    def __init__(self, shards, chunks, g, r1, r2, r3, z, zfirst, send, recv):
        self.n = shards
        self.sizes = [hi - lo for lo, hi in chunks]
        self.rows = [pl.ds(lo, hi - lo) for lo, hi in chunks]
        self.g, self.r1, self.r2, self.r3, self.z = g, r1, r2, r3, z
        self.zz, self.zx, self.zy, self.zsend, self.zrecv = zfirst
        self.send, self.recv = send, recv
        self.s, self.c, self.t = (lax.axis_index(a) for a in ("shard", "ctx", "tp"))
        self.core = lax.rem(self.t, 2)
        self.x = lax.div(self.t, 2)
        self.pair = {"tp": self.t + 1 - 2 * self.core}
        self.across = {"tp": lax.rem(self.t + 2, 4)}
        self.beside = {"ctx": 1 - self.c}

    def early(self, k, step):
        rows = self.rows[k]
        if step < self.n - 1:
            to = lax.rem(self.s + step + 1, self.n)
            src, dst, device = self.r1.at[to, :, :, rows], self.zz.at[step], {"shard": to}
        elif step == self.n - 1:
            src, dst, device = self.r1.at[self.s, :, 1 - self.x, rows], self.zx, self.across
        else:
            src, dst, device = self.zx.at[1 - self.c], self.zy, self.beside
        return pltpu.make_async_remote_copy(
            src_ref=src, dst_ref=dst, send_sem=self.zsend.at[step], recv_sem=self.zrecv.at[step],
            device_id=device, device_id_type=MESH,
        )

    def copy(self, src, dst, k, kind, device):
        return pltpu.make_async_remote_copy(
            src_ref=src, dst_ref=dst, send_sem=self.send.at[kind], recv_sem=self.recv.at[k, kind],
            device_id=device, device_id_type=MESH,
        )

    def one(self, k):
        rows = self.rows[k]
        return self.copy(self.g.at[:, :, :, 1 - self.core, rows], self.r1.at[:, :, :, rows], k, 0, self.pair)

    def two(self, k):
        rows = self.rows[k]
        if self.ORDER[k] == 0:
            src, device = self.r1.at[:, :, 1 - self.x, rows], self.across
        else:
            src, device = self.r1.at[:, 1 - self.c, :, rows], self.beside
        return self.copy(src, self.r2.at[:, :, rows], k, 1, device)

    def three(self, k):
        rows = self.rows[k]
        if self.ORDER[k] == 0:
            src, device = self.r2.at[:, 1 - self.c, rows], self.beside
        else:
            src, device = self.r2.at[:, 1 - self.x, rows], self.across
        return self.copy(src, self.r3.at[:, rows], k, 2, device)

    def along(self, k, d):
        to = lax.rem(self.s + d, self.n)
        rows = self.rows[k]
        return self.copy(self.r3.at[to, rows], self.z.at[d - 1, rows], k, 2 + d, {"shard": to})

    def start(self, k):
        self.one(k).start()

    def to_second(self, k):
        self.one(k).wait_recv()
        rows = self.rows[k]
        for j in range(2):
            for x in range(2):
                self.r1[:, j, x, rows] += self.g[:, j, x, self.core, rows]
        if self.ORDER[k] == 2:
            for step in range(self.n - 1):
                self.early(k, step).start()
            return
        self.two(k).start()

    def to_third(self, k):
        rows = self.rows[k]
        if self.ORDER[k] == 2:
            for step in range(self.n - 1):
                self.early(k, step).wait_recv()
            for j in range(2):
                for x in range(2):
                    total = self.r1[self.s, j, x, rows].astype(F32)
                    for step in range(self.n - 1):
                        total = total + self.zz[step, j, x].astype(F32)
                    self.r1[self.s, j, x, rows] = total.astype(BF)
            self.early(k, self.n - 1).start()
            return
        self.two(k).wait_recv()
        for j in range(2):
            own = self.r1[:, j, self.x, rows] if self.ORDER[k] == 0 else self.r1[:, self.c, j, rows]
            self.r2[:, j, rows] += own
        self.three(k).start()

    def to_last(self, k):
        rows = self.rows[k]
        if self.ORDER[k] == 2:
            self.early(k, self.n - 1).wait_recv()
            for j in range(2):
                self.zx[j] += self.r1[self.s, j, self.x, rows]
            self.early(k, self.n).start()
            return
        self.three(k).wait_recv()
        own = self.c if self.ORDER[k] == 0 else self.x
        self.r3[:, rows] += self.r2[:, own, rows]
        for d in range(1, self.n):
            self.along(k, d).start()

    def arrive(self, k, out):
        rows = self.rows[k]
        if self.ORDER[k] == 2:
            self.early(k, self.n).wait_recv()
            out[rows, :] = (self.zx[self.c].astype(F32) + self.zy[...].astype(F32)).astype(out.dtype)
            return
        for d in range(1, self.n):
            self.along(k, d).wait_recv()
        total = self.r3[self.s, rows].astype(F32)
        for d in range(1, self.n):
            total = total + self.z[d - 1, rows].astype(F32)
        out[rows, :] = total.astype(out.dtype)

    def drain(self):
        first = self.ORDER.index(2)
        rest = sum(self.sizes) - self.sizes[first]
        whole = [(self.r1, 0), (self.r1.at[:, :, 0, 0:rest], 1), (self.r1.at[:, 0, 0, 0:rest], 2)]
        whole += [(self.r3.at[0, 0:rest], 2 + d) for d in range(1, self.n)]
        for ref, kind in whole:
            self.copy(ref, ref, 0, kind, self.pair).wait_send()
        for step in range(self.n + 1):
            self.early(first, step).wait_send()


class SmallSum:
    def __init__(self, shards, own, got, send, recv):
        self.n, self.own, self.got, self.send, self.recv = shards, own, got, send, recv
        self.s, self.c, self.t = (lax.axis_index(a) for a in ("shard", "ctx", "tp"))

    def copy(self, i):
        near = [{"tp": self.t + 1 - 2 * lax.rem(self.t, 2)}, {"tp": lax.rem(self.t + 2, 4)}, {"ctx": 1 - self.c}]
        device = near[i] if i < 3 else {"shard": lax.rem(self.s + i - 2, self.n)}
        return pltpu.make_async_remote_copy(
            src_ref=self.own.at[min(i, 3)], dst_ref=self.got.at[i], send_sem=self.send.at[i],
            recv_sem=self.recv.at[i], device_id=device, device_id_type=MESH,
        )

    def start(self, value):
        self.own[0] = value
        self.copy(0).start()

    def step(self, i):
        self.copy(i).wait_recv()
        self.own[i + 1] = self.own[i] + self.got[i]
        if i < 2:
            self.copy(i + 1).start()
        else:
            for d in range(1, self.n):
                self.copy(2 + d).start()

    def arrive(self, out):
        total = self.own[3]
        for d in range(1, self.n):
            self.copy(2 + d).wait_recv()
            total = total + self.got[2 + d]
        out[...] = total

    def drain(self):
        for i in range(2 + self.n):
            self.copy(i).wait_send()


class Spread:
    def __init__(self, src, dst, send, recv):
        self.src, self.dst, self.send, self.recv = src, dst, send, recv
        self.t = lax.axis_index("tp")

    def copy(self, d):
        to = lax.rem(self.t + d, 4)
        share = self.dst.shape[1]
        src = self.src.at[pl.ds(pl.multiple_of(to * share, share), share)]
        dst = self.dst.at[self.t]
        if d == 0:
            return pltpu.make_async_copy(src, dst, self.send.at[d])
        return pltpu.make_async_remote_copy(
            src_ref=src, dst_ref=dst, send_sem=self.send.at[d], recv_sem=self.recv.at[d],
            device_id={"tp": to}, device_id_type=MESH,
        )

    def start(self):
        for d in (2, 3, 1, 0):
            self.copy(d).start()

    def finish(self):
        for d in (1, 2, 3):
            self.copy(d).wait_recv()
            self.copy(d).wait_send()
        self.copy(0).wait()


class Share:
    def __init__(self, held, send, recv):
        self.held, self.send, self.recv = held, send, recv
        self.t = lax.axis_index("tp")
        self.pair_tp = self.t + 1 - 2 * lax.rem(self.t, 2)
        self.across_tp = lax.rem(self.t + 2, 4)

    def copy(self, i, tp, to):
        return pltpu.make_async_remote_copy(
            src_ref=self.held.at[tp], dst_ref=self.held.at[tp], send_sem=self.send.at[i],
            recv_sem=self.recv.at[i], device_id={"tp": to}, device_id_type=MESH,
        )

    def start(self):
        self.copy(0, self.t, self.across_tp).start()
        self.copy(1, self.t, self.pair_tp).start()

    def relay(self):
        self.copy(0, self.across_tp, self.across_tp).wait_recv()
        self.copy(2, self.across_tp, self.pair_tp).start()

    def finish(self):
        self.copy(1, self.pair_tp, self.pair_tp).wait_recv()
        self.copy(2, lax.rem(self.pair_tp + 2, 4), self.pair_tp).wait_recv()
        self.copy(0, self.t, self.across_tp).wait_send()
        self.copy(1, self.t, self.pair_tp).wait_send()
        self.copy(2, self.across_tp, self.pair_tp).wait_send()


class Comm:
    pass


def step_scratch(shards, pk, direct, tokens, slots, width):
    v, dma = pltpu.VMEM, pltpu.SemaphoreType.DMA
    n = shards
    out = dict(
        w=v((n * 4, TILES, width // (n * 4), width), BF),
        x=v((tokens, width), BF),
        m0=v((slots, width), F32),
        og=v((4, tokens // 4, width), BF),
        y=v((tokens, width), BF),
        xg=v((tokens, width), BF),
        mems=v((4, slots, width), BF),
        migs=v((4, slots, width), BF),
        small=v((8, width), F32),
        m_send=v((slots, width), BF),
        m_recv=v((slots, width), BF),
        g_send=v((slots, width), BF),
        g_recv=v((slots, width), BF),
        chain=dma((4,)),
        loads=dma((3,)),
        local=dma((TILES,)),
        w_send=dma((4,)),
        w_line_send=dma((2, n)),
        w_recv=dma((5, n, len(GROUPS))),
        w_pair_recv=dma((len(GROUPS),)),
        og_send=dma((4,)),
        og_recv=dma((4,)),
        y_send=dma((4,)),
        y_recv=dma((4,)),
        xg_send=dma((4,)),
        xg_recv=dma((4,)),
        mem_send=dma((3,)),
        mem_recv=dma((3,)),
        mig_send=dma((3,)),
        mig_recv=dma((3,)),
    )
    if direct:
        c = len(pk.chunks)
        lo, hi = pk.chunks[Reduce.ORDER.index(2)]
        early = hi - lo
        out.update(
            g=v(pk.shape, BF),
            r1=v((n, 2, 2, pk.rows, 128), BF),
            r2=v((n, 2, pk.rows, 128), BF),
            r3=v((n, pk.rows, 128), BF),
            z=v((n - 1, pk.rows, 128), BF),
            zz=v((n - 1, 2, 2, early, 128), BF),
            zx=v((2, early, 128), BF),
            zy=v((early, 128), BF),
            zsend=dma((n + 1,)),
            zrecv=dma((n + 1,)),
            own=v((4, 8, width), F32),
            got=v((2 + n, 8, width), F32),
            r_send=dma((2 + n,)),
            r_recv=dma((c, 2 + n)),
            s_send=dma((2 + n,)),
            s_recv=dma((2 + n,)),
        )
    return out


def step_kernel(dims, pk, direct, names, unit_names, *refs):
    shards, ctxs, halved = dims
    first, length, inputs, first_memory, memory_grad, out_grad = refs[:6]
    weights, gains, outs = refs[6:17], refs[17:21], refs[21:27]
    scratch = refs[27:]
    b = Comm()
    b.__dict__.update(zip(names, scratch))
    unit_refs = dict(zip(unit_names, scratch[len(names) :]))
    if not direct:
        b.g = outs[4]
    s, c, t = (lax.axis_index(a) for a in ("shard", "ctx", "tp"))
    u = Unit(unit_refs, Weights(b.w), b.x, gains, b.small)

    loads = [
        pltpu.make_async_copy(inputs.at[t], b.x, b.loads.at[0]),
        pltpu.make_async_copy(first_memory.at[t], b.m0, b.loads.at[1]),
        pltpu.make_async_copy(memory_grad.at[t], u.gm, b.loads.at[2]),
    ]
    copies = own_tiles(weights, b.w, s * 4 + t, b.local)
    for copy in copies + loads:
        copy.start()
    mine = pltpu.make_async_copy(out_grad.at[t], b.og.at[t], b.og_send.at[0])
    mine.start()
    peers = line_peers(shards) + tp_peers()
    if ctxs > 1:
        peers += [(c > 0, {"ctx": c - 1}), (c < ctxs - 1, {"ctx": c + 1})]
    greet(peers)
    gather = Gather(shards, halved, b.w, b.w_send, b.w_line_send, b.w_recv, b.w_pair_recv)

    def ready(g):
        for copy in copies[GROUPS[g][0] : GROUPS[g][1]]:
            copy.wait()

    lead, follow = pl.when(c == 0), pl.when(c > 0)
    pairs = u.width // 128
    chunks = u.ff // 512

    def on_lead(*calls):
        def run():
            @lead
            def _():
                for call in calls:
                    call()

        return run

    def take_memory():
        u.mem[...] = b.m0[...]
        u.memory_in()
        u.attend_memory()

    def project_and_attend():
        u.project_tokens()
        u.attend(0, 1)

    work = [(0, project_and_attend)]
    work += [(0, partial(u.attend, p, 1)) for p in range(1, pairs)]
    work += [
        (0, on_lead(take_memory)),
        (1, on_lead(u.after_attention)),
        (1, on_lead(partial(u.feed_forward_up, 0, chunks // 2))),
        (1, on_lead(partial(u.feed_forward_up, chunks // 2, chunks - chunks // 2))),
        (2, on_lead(u.feed_forward_down)),
    ]

    def between(complete):
        if work and work[0][0] <= complete:
            work.pop(0)[1]()

    def chain_copy(i, to):
        src, dst = ((b.m_send, b.m_recv), (b.g_send, b.g_recv))[i]
        return pltpu.make_async_remote_copy(
            src_ref=src, dst_ref=dst, send_sem=b.chain.at[2 * i], recv_sem=b.chain.at[2 * i + 1],
            device_id={"ctx": to}, device_id_type=MESH,
        )

    def og_copy(d):
        to = lax.rem(t + d, 4)
        return pltpu.make_async_remote_copy(
            src_ref=out_grad.at[to], dst_ref=b.og.at[t], send_sem=b.og_send.at[d],
            recv_sem=b.og_recv.at[d], device_id={"tp": to}, device_id_type=MESH,
        )

    spread_y = Spread(b.y, outs[0], b.y_send, b.y_recv)
    spread_xg = Spread(b.xg, outs[2], b.xg_send, b.xg_recv)
    share_mem = Share(b.mems, b.mem_send, b.mem_recv)
    share_mig = Share(b.migs, b.mig_send, b.mig_recv)
    gather.events(0, ready, between)
    for copy in loads:
        copy.wait()
    u.make_bias(first[0, t], length[0, t])
    gather.events(1, ready, between)
    u.tokens_in()
    for time in range(2, gather.last + 1):
        gather.events(time, ready, between)
    while work:
        work.pop(0)[1]()
    for d in (1, 2, 3):
        og_copy(d).start()

    if ctxs > 1:

        @follow
        def _():
            gather.drain()
            chain_copy(0, c - 1).wait_recv()
            u.mem[...] = b.m_recv[...].astype(F32)
            u.memory_in()
            u.attend_memory()
            u.after_attention()
            u.feed_forward_up(0, chunks)
            u.feed_forward_down()

    after = u.write_memory()
    b.m_send[...] = after.astype(BF)
    if ctxs > 1:

        @pl.when(c < ctxs - 1)
        def _():
            chain_copy(0, c + 1).start()

    b.mems[t] = after.astype(BF)
    b.y[...] = u.af[0 : u.tokens, :].astype(BF)
    share_mem.start()
    spread_y.start()
    u.backward_early()
    mine.wait()
    for d in (1, 2, 3):
        og_copy(d).wait_recv()
    share_mem.relay()

    @lead
    def _():
        gather.drain()

    if ctxs > 1:

        @pl.when(c < ctxs - 1)
        def _():
            chain_copy(1, c + 1).wait_recv()
            u.gm[...] += b.g_recv[...].astype(F32)

    def out_grad_rows(i):
        per = b.og.shape[1] // BLOCK
        return b.og[lax.div(i, per), pl.ds(lax.rem(i, per) * BLOCK, BLOCK), :].astype(F32)

    def grads(*which):
        weight_grads(u, b.g, pk, which)

    red = None
    if direct:
        early = (b.zz, b.zx, b.zy, b.zsend, b.zrecv)
        red = Reduce(shards, pk.chunks, b.g, b.r1, b.r2, b.r3, b.z, early, b.r_send, b.r_recv)
    sums = SmallSum(shards, b.own, b.got, b.s_send, b.s_recv) if direct else None
    WRITE, DOWN, UP, ENTER = (0, 1), (2, 3), (4, 5), (6, 7)

    def reduce(*todo):
        for what, chunks in todo if direct else ():
            for k in chunks:
                getattr(red, what)(k, *((outs[4],) if what == "arrive" else ()))

    u.write_back()

    @lead
    def _():
        grads("write")
        reduce(("start", WRITE))

    u.write_enter(out_grad_rows)

    @lead
    def _():
        grads("down")
        reduce(("start", DOWN), ("to_second", WRITE))

    u.feed_forward_back()

    @lead
    def _():
        grads("up")
        reduce(("start", UP), ("to_second", DOWN))

    u.feed_forward_enter()

    @lead
    def _():
        grads("wo")
        reduce(("to_second", UP))

    u.project_back()
    u.attend_back(0, pairs // 2)

    @lead
    def _():
        reduce(("to_third", WRITE))

    u.attend_back(pairs // 2, pairs - pairs // 2)
    back = u.enter_memory()
    b.migs[t] = back.astype(BF)
    if ctxs > 1:

        @follow
        def _():
            b.g_send[...] = back.astype(BF)
            chain_copy(1, c - 1).start()

    u.queries_back()

    @lead
    def _():
        grads("enter")
        reduce(("start", ENTER), ("to_third", DOWN))

    u.enter_back()

    @lead
    def _():
        reduce(("to_second", ENTER), ("to_third", UP), ("to_last", WRITE))

    u.norm_enter(b.xg)

    if ctxs > 1:

        @follow
        def _():
            grads("write")
            reduce(("start", WRITE))
            grads("down")
            reduce(("start", DOWN))
            grads("up")
            reduce(("start", UP), ("to_second", WRITE))
            grads("wo", "enter")
            reduce(("start", ENTER), ("to_second", DOWN), ("to_second", UP), ("to_second", ENTER))

    share_mig.start()
    if direct:
        sums.start(b.small[...])

    def sum_step(i):
        if direct:
            sums.step(i)

    @lead
    def _():
        sum_step(0)
        reduce(("to_third", ENTER))
        spread_xg.start()
        reduce(("to_last", DOWN), ("to_last", UP))
        sum_step(1)

    if ctxs > 1:

        @follow
        def _():
            sum_step(0)
            spread_xg.start()
            reduce(("to_third", (0, 2, 4, 6)), ("to_third", (1, 3, 5)))
            sum_step(1)
            reduce(("to_last", WRITE), ("to_last", DOWN), ("to_third", (7,)), ("to_last", UP))

    share_mig.relay()
    reduce(("to_last", ENTER))
    sum_step(2)

    for spread in (spread_y, share_mem):
        spread.finish()
    reduce(*(("arrive", pair) for pair in (WRITE, DOWN, UP)))
    for spread in (share_mig, spread_xg):
        spread.finish()
    kept = [
        pltpu.make_async_copy(b.mems, outs[1], b.loads.at[0]),
        pltpu.make_async_copy(b.migs, outs[3], b.loads.at[1]),
    ]
    for copy in kept:
        copy.start()
    for d in (1, 2, 3):
        og_copy(d).wait_send()
    if ctxs > 1:

        @pl.when(c < ctxs - 1)
        def _():
            chain_copy(0, c + 1).wait_send()

        @pl.when(c > 0)
        def _():
            chain_copy(1, c - 1).wait_send()

    if direct:
        sums.arrive(outs[5])
        reduce(("arrive", ENTER))
        sums.drain()
        red.drain()
    else:
        outs[5][...] = b.small[...]
    for copy in kept:
        copy.wait()


def run_step(dims, pk, direct, first, length, inputs, first_memory, memory_grad, out_grad, weights, gains):
    _, tokens, width = inputs.shape
    slots = first_memory.shape[1]
    vm = pl.BlockSpec(memory_space=pltpu.VMEM)
    sm = pl.BlockSpec(memory_space=pltpu.SMEM)
    hbm = pl.BlockSpec(memory_space=pl.ANY)
    scratch = step_scratch(dims[0], pk, direct, tokens, slots, width)
    unit = unit_scratch(tokens, slots, width, pk.ff)
    shape = jax.ShapeDtypeStruct
    return pl.pallas_call(
        partial(step_kernel, dims, pk, direct, tuple(scratch), tuple(unit)),
        out_shape=(
            shape((4, tokens // 4, width), BF), shape((4, slots, width), BF),
            shape((4, tokens // 4, width), BF), shape((4, slots, width), BF),
            shape((pk.rows, 128) if direct else pk.shape, BF), shape((8, width), F32),
        ),
        in_specs=[sm, sm] + [hbm] * 15 + [vm] * 4,
        out_specs=(hbm, hbm, hbm, hbm, vm, vm),
        scratch_shapes=list(scratch.values()) + list(unit.values()),
        compiler_params=pltpu.CompilerParams(
            vmem_limit_bytes=VMEM_LIMIT, collective_id=1, has_side_effects=True
        ),
        name="step",
    )(first, length, inputs, first_memory, memory_grad, out_grad, *weights, *gains)


def store_kernel(pk, owners, *refs):
    rows_in, total, small = refs[:4], refs[4], refs[5]
    rows_out, (wq, wk, wv, wo, up, down, uq, uk, uv, uo, ugate), vectors = refs[6:10], refs[10:21], refs[21:]
    for src, dst in zip(rows_in, rows_out):
        dst[...] = src[...].astype(dst.dtype)

    def part(at, size):
        return total[at : at + size, :].astype(F32)

    h = pk.head_rows
    for name, ref in dict(wq=wq, wk=wk, wv=wv, uq=uq, uk=uk, uv=uv).items():
        ref[...] = part(pk.heads[name], h)
    for name, ref in dict(uo=uo, ugate=ugate).items():
        ref[...] = part(pk.heads[name], h)
    for at, r, ref in ((pk.at_wo, pk.row_rows, wo), (pk.at_up, pk.row_rows, up), (pk.at_down, pk.down_rows, down)):
        for j in range(ref.shape[1] // 128):
            ref[:, j * 128 : j * 128 + 128] = part(at + j * r, r)
    share = small.shape[1] // owners
    owner = lax.axis_index("shard")
    for axis in ("ctx", "tp"):
        owner = owner * lax.axis_size(axis) + lax.axis_index(axis)
    turned = pltpu.roll(small[...], small.shape[1] - owner * share, 1)
    for i, ref in enumerate(vectors):
        ref[...] = turned[i : i + 1, 0:share]


def run_store(pk, owners, rows, total, small):
    vm = pl.BlockSpec(memory_space=pltpu.VMEM)
    shape = jax.ShapeDtypeStruct
    width = small.shape[1]
    h = pk.head_rows
    head = shape((h, 128), F32)
    outs = tuple(shape(r.shape, d) for r, d in zip(rows, (BF, F32, BF, F32))) + (
        head, head, head, shape((pk.row_rows, width), F32), shape((pk.row_rows, pk.ff), F32),
        shape((pk.down_rows, width), F32), head, head, head, head, head,
    ) + (shape((1, width // owners), F32),) * 4
    return pl.pallas_call(
        partial(store_kernel, pk, owners),
        out_shape=outs,
        in_specs=[vm] * 6,
        out_specs=(vm,) * len(outs),
        compiler_params=pltpu.CompilerParams(vmem_limit_bytes=VMEM_LIMIT),
        name="store",
    )(*rows, total, small)


def full_gradients(pk, grads):
    groups, owners = pk.shards * pk.ctxs, pk.shards * pk.ctxs * 4
    by_head = grads.reshape(groups, 4, pk.rows, 128)
    by_owner = grads.reshape(owners, pk.rows, 128)

    def head(name):
        at = pk.heads[name]
        got = by_head[:, :, at : at + pk.head_rows]
        return got.transpose(0, 2, 1, 3).reshape(pk.width, pk.width).astype(F32)

    def rows(at, h, n):
        got = by_owner[:, at : at + h * n].reshape(owners, n, h, 128)
        return got.transpose(0, 2, 1, 3).reshape(owners * h, n * 128).astype(F32)

    return (
        head("wq"), head("wk"), head("wv"),
        rows(pk.at_wo, pk.row_rows, pk.width // 128),
        rows(pk.at_up, pk.row_rows, pk.ff // 128),
        rows(pk.at_down, pk.down_rows, pk.width // 128),
        head("uq"), head("uk"), head("uv"), head("uo").T, head("ugate").T,
    )


def local(
    inputs, first_memory, piece_start, piece_len,
    w_query, w_key, w_value, w_out, w_up, w_down, u_query, u_key, u_value, u_out, u_gate,
    gain_attn, gain_ffn, gain_write, gate_bias, out_grad, memory_grad,
):
    shards, ctxs, tps = (lax.axis_size(a) for a in ("shard", "ctx", "tp"))
    seqs, tokens, width = inputs.shape
    ff = w_up.shape[1]
    assert seqs == tps == 4 and tokens == width == 512 and ff == 2048
    weights = (w_query, w_key, w_value, w_out, w_up, w_down, u_query, u_key, u_value, u_out, u_gate)
    gains = [v.reshape(1, -1) for v in (gain_attn, gain_ffn, gain_write, gate_bias)]
    owners = shards * ctxs * tps
    direct = ctxs == 2 and width % (owners * 16) == 0
    halved = ctxs == 2 and w_query.shape[0] % 32 == 0
    pk = Packing(shards if direct else 4, 2, width, ff)
    got = run_step(
        (shards, ctxs, halved), pk, direct, piece_start.T, piece_len.T, inputs, first_memory, memory_grad,
        out_grad, weights, gains,
    )
    if direct:
        out = run_store(pk, owners, got[:4], got[4], got[5])
        return out[:13] + (out[13].T, out[14].T) + tuple(v.reshape(-1) for v in out[15:])
    every = ("shard", "ctx", "tp")
    out = [got[0], got[1].astype(F32), got[2], got[3].astype(F32)]
    for i, g in enumerate(full_gradients(pk, got[4])):
        if i in (3, 4, 5):
            out.append(lax.psum_scatter(g, every, scatter_dimension=0, tiled=True))
            continue
        sum_dim = 1 if i >= 9 else 0
        cut = lax.psum_scatter(g, "tp", scatter_dimension=1 - sum_dim, tiled=True)
        out.append(lax.psum_scatter(cut, ("shard", "ctx"), scatter_dimension=sum_dim, tiled=True))
    for i in range(4):
        out.append(lax.psum_scatter(got[5][i], every, scatter_dimension=0, tiled=True))
    return tuple(out)


def solution(mesh):
    cut = P(("shard", "tp"), None)
    head, rows, turned = P(("shard", "ctx"), "tp"), P(("shard", "ctx", "tp"), None), P("tp", ("shard", "ctx"))
    vector = P(("shard", "ctx", "tp"))
    over_rows, over_ctx = P("shard", ("ctx", "tp"), None), P("shard", "ctx", None)
    return jax.shard_map(
        local,
        mesh=mesh,
        in_specs=(over_ctx, P("shard", None, None), P("shard", "ctx"), P("shard", "ctx"))
        + (cut,) * 11 + (P(),) * 4 + (over_rows, over_ctx),
        out_specs=(over_rows, over_ctx, over_rows, over_ctx)
        + (head,) * 3 + (rows,) * 3 + (head,) * 3 + (turned,) * 2 + (vector,) * 4,
        check_vma=False,
    )
```
